32 devices in a mesh: seq: 8 (over z, core), span: 4 (over y, x).
Axes of the slice: x: 2, y: 2, z: 4, core: 2. Of those that a mesh axis runs over, the one named last changes fastest.
Arguments:
- q_prefill: bfloat16 [4, 1024, 64, 192], P('span', 'seq'), may hold values from -3000 to 3000
- kv_latent: bfloat16 [4, 1024, 512], P('span', 'seq'), may hold values from -200 to 200
- key_rope: bfloat16 [4, 1024, 64], P('span', 'seq'), may hold values from -6 to 6
- segment_ids: int32 [4, 1024], replicated, may hold values from 0 to 15, never falling along the last dimension, each value on 1 to 512 neighbouring positions
- assignment: int32 [64], replicated, may hold values from 0 to 63, each once
- absorb_key: bfloat16 [64, 128, 512], replicated, may hold values from -0.5 to 0.5
- absorb_value: bfloat16 [64, 512, 128], replicated, may hold values from -0.25 to 0.25
- q_decode: bfloat16 [2, 64, 64, 192], P(None, 'span'), may hold values from -3000 to 3000
- new_latent: bfloat16 [2, 64, 512], P(None, 'span'), may hold values from -6 to 6
- new_rope: bfloat16 [2, 64, 64], P(None, 'span'), may hold values from -6 to 6
Outputs:
- prefill_out: bfloat16 [4, 1024, 8192], P('span', 'seq')
- decode_out: bfloat16 [2, 64, 8192], P(None, 'span')
The draws below stay inside these ranges and needn't reach their ends.
Inputs may be any that keep to these rules, and one draw needn't show every extreme that they name: `segment_ids`: within a span the numbers never fall; each of the 16 numbers appears, on 1 to 512 positions. `assignment`: each sequence number appears once; entry c * 16 + d is the sequence of prompt d of span c, and sequence g is decoded at span index g // 16, slot g % 16.
All inputs are finite; a program needn't handle non-finite values.
Results may differ from the reference program's by a relative error of at most 0.014.
Values may be sent and summed in bfloat16 or wider, within the bound.
No kernel may reach another device: no remote copies, remote signals or barrier semaphores. Data moves between devices by JAX's collectives and lax.ppermute only.
A program may use at most 192 MiB of HBM per device.

```python
import math
import jax
import jax.numpy as jnp
import numpy as np
from jax import lax

H = 64
NOPE = 128
ROPE = 64
LAT = 512
VHEAD = 128
DOCS = 16
STEPS = 2
LEN = 1024
SPANS = 4
SEQS = 64
MOST = 512


def prefill_align(key):
    base = jax.random.fold_in(key, 7001)
    first = jax.random.fold_in(base, 0)
    rope = jnp.clip(jax.random.normal(first, (SPANS, LEN, ROPE), jnp.float32), -6.0, 6.0)
    return rope


def decode_align(key):
    base = jax.random.fold_in(key, 7003)
    first = jax.random.fold_in(base, 0)
    rope = jnp.clip(jax.random.normal(first, (STEPS, SEQS, ROPE), jnp.float32), -6.0, 6.0)
    return rope


def draw_key_rope(key, part):
    rope = prefill_align(key)
    return rope.astype(jnp.bfloat16)


def draw_q_prefill(key, part):
    base = jax.random.fold_in(key, 7002)
    query = jnp.clip(jax.random.normal(base, (SPANS, LEN, H, NOPE + ROPE), jnp.float32), -6.0, 6.0)
    return query.astype(jnp.bfloat16)


def draw_new_rope(key, part):
    rope = decode_align(key)
    return rope.astype(jnp.bfloat16)


def draw_q_decode(key, part):
    base = jax.random.fold_in(key, 7004)
    query = jnp.clip(jax.random.normal(base, (STEPS, SEQS, H, NOPE + ROPE), jnp.float32), -6.0, 6.0)
    return query.astype(jnp.bfloat16)


def draw_kv_latent(key, part):
    base = jax.random.fold_in(key, 7005)
    first = jax.random.fold_in(base, 0)
    values = jnp.clip(jax.random.normal(first, (SPANS, LEN, LAT), jnp.float32), -6.0, 6.0)
    return values.astype(jnp.bfloat16)


def block_scale(own_key, dims, cuts, least, top_value):
    factor_of, own = 1.0, jax.random.fold_in(own_key, 6)
    for axis_at, parts in cuts:
        steps = jnp.exp(jax.random.uniform(jax.random.fold_in(own, axis_at), (parts,), jnp.float32, least / len(cuts), top_value / len(cuts)))
        factor_of = factor_of * jnp.repeat(steps, dims[axis_at] // parts).reshape([-1 if axis == axis_at else 1 for axis in range(len(dims))])
    return factor_of


def length_profile(number_of, total, limit, slope):
    weights = [(1 << 20) // math.isqrt(rank ** slope) + 1 for rank in range(2, number_of + 1)]
    spare, given = total - limit - (number_of - 1), [1] * (number_of - 1)
    while spare > 0:
        candidates = [i for i in range(number_of - 1) if given[i] < limit]
        mass, remaining = sum([weights[i] for i in candidates]), spare
        for i in candidates:
            more = min(limit - given[i], max(1, remaining * weights[i] // mass), spare)
            given[i] = given[i] + more
            spare = spare - more
    return np.array([limit] + given)


def ragged(stream_key, count, total, reach, skew):
    if count == 2:
        one = jax.random.randint(stream_key, (), max(1, total - reach), min(reach, total - 1) + 1)
        return jnp.stack([one, total - one])
    tallies = jnp.asarray(length_profile(count, total, reach, skew), jnp.int32)
    couples = (count - 1) // 2
    giver, taker = tallies[1:1 + 2 * couples:2], tallies[2:2 + 2 * couples:2]
    slack = jnp.minimum(giver - 1, reach - taker)
    shifted = jax.random.randint(jax.random.fold_in(stream_key, 1), (couples,), 0, 1 << 20) % (slack + 1)
    tallies = tallies.at[1:1 + 2 * couples:2].set(giver - shifted).at[2:2 + 2 * couples:2].set(taker + shifted)
    return tallies[jax.random.permutation(jax.random.fold_in(stream_key, 2), count)]


def bell_draw(rng, shape, deviation, limit, cuts=(), kind=jnp.bfloat16):
    values = jax.random.normal(rng, shape, jnp.float32) * deviation
    if len(cuts) > 0:
        values = block_scale(rng, shape, cuts, -0.22, 0.18) * values
    return jnp.clip(values, min=-limit, max=limit).astype(kind)


def setup_inputs(seed: int = 0) -> dict:
    arg_keys = jax.random.split(jax.random.key(seed), 11)
    return {
        "q_prefill": draw_q_prefill(jax.random.fold_in(arg_keys[10], 71), 0),
        "kv_latent": draw_kv_latent(jax.random.fold_in(arg_keys[10], 71), 0),
        "key_rope": draw_key_rope(jax.random.fold_in(arg_keys[10], 71), 0),
        "segment_ids": jax.vmap(lambda own: jnp.searchsorted(jnp.cumsum(ragged(own, DOCS, LEN, MOST, 2)), jnp.arange(LEN), side="right"))(jax.random.split(arg_keys[3], SPANS)).reshape((SPANS, LEN)).astype(jnp.int32),
        "assignment": jax.random.permutation(arg_keys[4], SEQS).astype(jnp.int32),
        "absorb_key": bell_draw(arg_keys[5], (H, NOPE, LAT), NOPE ** -0.5, 0.5),
        "absorb_value": bell_draw(arg_keys[6], (H, LAT, VHEAD), LAT ** -0.5, 0.25),
        "q_decode": draw_q_decode(jax.random.fold_in(arg_keys[10], 71), 0),
        "new_latent": bell_draw(arg_keys[8], (STEPS, SEQS, LAT), 1.0, 6.0, ((1, 4),)),
        "new_rope": draw_new_rope(jax.random.fold_in(arg_keys[10], 71), 0),
    }


def make_cache(latent, rope):
    values = latent.astype(jnp.float32)
    normed = values * lax.rsqrt(lax.optimization_barrier(jnp.mean(values * values, axis=-1, keepdims=True)) + 1e-06)
    return jnp.concatenate([normed, rope.astype(jnp.float32)], axis=-1).astype(jnp.bfloat16)

def absorb(query, absorb_key):
    latent = jnp.einsum('...hd,hdc->...hc', query[..., :NOPE].astype(jnp.float32), absorb_key.astype(jnp.float32))
    return jnp.concatenate([latent.astype(jnp.bfloat16), query[..., NOPE:]], axis=-1)

def project(latent_out, absorb_value):
    result = jnp.einsum('...hc,hcv->...hv', latent_out.astype(jnp.float32), absorb_value.astype(jnp.float32))
    return result.astype(jnp.bfloat16)

def reference(q_prefill, kv_latent, key_rope, segment_ids, assignment, absorb_key, absorb_value, q_decode, new_latent, new_rope):
    scale = (NOPE + ROPE) ** (-0.5)
    block = LEN // 4

    def prefill_span(args):
        query, latent, rope, seg = args
        cache = make_cache(latent, rope)
        queries = absorb(query, absorb_key)
        pieces = []
        for index in range(4):
            start = index * block
            end = start + block
            keys = cache[:end].astype(jnp.float32)
            scores = jnp.einsum('thc,kc->thk', queries[start:end].astype(jnp.float32), keys) * scale
            pos_q = start + jnp.arange(block, dtype=jnp.int32)
            pos_k = jnp.arange(end, dtype=jnp.int32)
            mask = (seg[start:end, None] == seg[None, :end]) & (pos_q[:, None] >= pos_k[None, :])
            scores = jnp.where(mask[:, None, :], scores, -jnp.inf)
            best = lax.optimization_barrier(jnp.max(scores, axis=-1, keepdims=True))
            weights = jnp.exp(scores - best)
            total = lax.optimization_barrier(jnp.sum(weights, axis=-1))
            accum = jnp.einsum('thk,kc->thc', weights.astype(jnp.bfloat16).astype(jnp.float32), keys[:, :LAT])
            latent_out = (accum / total[..., None]).astype(jnp.bfloat16)
            pieces.append(project(latent_out, absorb_value).reshape(block, H * VHEAD))
        return jnp.concatenate(pieces, axis=0)
    prefill_out = lax.map(prefill_span, (q_prefill, kv_latent, key_rope, segment_ids))

    def decode_span(args):
        queries, fresh_latent, fresh_rope, latent, rope, seg = args
        cache = make_cache(latent, rope).astype(jnp.float32)
        fresh = make_cache(fresh_latent, fresh_rope).astype(jnp.float32)
        dq = absorb(queries, absorb_key).astype(jnp.float32)
        old = jnp.einsum('sdhc,kc->sdhk', dq, cache) * scale
        old_mask = (seg[None, :] == jnp.arange(DOCS, dtype=jnp.int32)[:, None])[None, :, None, :]
        new = jnp.einsum('sdhc,udc->sdhu', dq, fresh) * scale
        steps = jnp.arange(STEPS, dtype=jnp.int32)
        new_mask = (steps[None, :] <= steps[:, None])[:, None, None, :]
        old = jnp.where(old_mask, old, -jnp.inf)
        new = jnp.where(new_mask, new, -jnp.inf)
        best = jnp.maximum(lax.optimization_barrier(jnp.max(old, axis=-1)), lax.optimization_barrier(jnp.max(new, axis=-1)))[..., None]
        old_w = jnp.exp(old - best)
        new_w = jnp.exp(new - best)
        total = lax.optimization_barrier(jnp.sum(old_w, axis=-1)) + lax.optimization_barrier(jnp.sum(new_w, axis=-1))
        accum = jnp.einsum('sdhk,kc->sdhc', old_w.astype(jnp.bfloat16).astype(jnp.float32), cache[:, :LAT])
        accum = accum + jnp.einsum('sdhu,udc->sdhc', new_w.astype(jnp.bfloat16).astype(jnp.float32), fresh[..., :LAT])
        heads_out = jnp.einsum('sdhc,hcv->sdhv', accum, absorb_value.astype(jnp.float32), precision=lax.Precision.HIGHEST)
        result = (heads_out / total[..., None]).astype(jnp.bfloat16)
        return result.reshape(STEPS, DOCS, H * VHEAD)
    order = assignment.astype(jnp.int32)
    queries = q_decode[:, order].reshape(STEPS, SPANS, DOCS, H, NOPE + ROPE).transpose(1, 0, 2, 3, 4)
    fresh_latent = new_latent[:, order].reshape(STEPS, SPANS, DOCS, LAT).transpose(1, 0, 2, 3)
    fresh_rope = new_rope[:, order].reshape(STEPS, SPANS, DOCS, ROPE).transpose(1, 0, 2, 3)
    results = lax.map(decode_span, (queries, fresh_latent, fresh_rope, kv_latent, key_rope, segment_ids))
    results = results.transpose(1, 0, 2, 3).reshape(STEPS, SEQS, H * VHEAD)
    decode_out = jnp.zeros((STEPS, SEQS, H * VHEAD), jnp.bfloat16).at[:, order].set(results)
    return (prefill_out, decode_out)
```

```python
import functools
import math

import jax
import jax.numpy as jnp
from jax import lax
from jax.experimental import pallas as pl
from jax.experimental.pallas import tpu as pltpu
from jax.sharding import PartitionSpec as P

NOPE = 128
ROPE = 64
LAT = 512
VHEAD = 128
WIDTH = LAT + ROPE

NEG = -1e30
EPS = 1e-06
SCALE2 = (NOPE + ROPE) ** (-0.5) * math.log2(math.e)
TOK = 16
PARTS = 2
VMEM_LIMIT = 60 << 20

NT = (((1,), (1,)), ((), ()))


def cache_rows(latent, rope):
    values = latent.astype(jnp.float32)
    normed = values * lax.rsqrt(jnp.mean(values * values, axis=-1, keepdims=True) + EPS)
    return jnp.concatenate([normed, rope.astype(jnp.float32)], axis=-1).astype(jnp.bfloat16)


def absorb_kernel(q_ref, ak_ref, o_ref, *, group, tokens):
    q = jnp.swapaxes(q_ref[...], 0, 1)
    for h in range(group):
        lat = jnp.dot(q[h, :, :NOPE], ak_ref[h], preferred_element_type=jnp.float32)
        row = pl.ds(h * TOK, TOK)
        o_ref[:, row, :LAT] = lat.astype(jnp.bfloat16).reshape(tokens // TOK, TOK, LAT)
        o_ref[:, row, LAT:] = q[h, :, NOPE:].reshape(tokens // TOK, TOK, ROPE)


def absorb_prefill(q, absorb_key, group=16):
    tokens, heads, size = q.shape
    return pl.pallas_call(
        functools.partial(absorb_kernel, group=group, tokens=tokens),
        grid=(heads // group,),
        in_specs=[
            pl.BlockSpec((tokens, group, size), lambda i: (0, i, 0)),
            pl.BlockSpec((group, NOPE, LAT), lambda i: (i, 0, 0)),
        ],
        out_specs=pl.BlockSpec((tokens // TOK, group * TOK, WIDTH), lambda i: (0, i, 0)),
        out_shape=jax.ShapeDtypeStruct((tokens // TOK, heads * TOK, WIDTH), jnp.bfloat16),
        cost_estimate=pl.CostEstimate(
            flops=2 * tokens * heads * NOPE * LAT,
            bytes_accessed=2 * heads * (tokens * (size + WIDTH) + NOPE * LAT),
            transcendentals=0,
        ),
        compiler_params=pltpu.CompilerParams(vmem_limit_bytes=VMEM_LIMIT),
        name="absorb_prefill",
    )(q, absorb_key)


def gather_copies(pieces, kbuf, sems, seq_idx, count):
    rows = pieces[0].shape[0]
    half = len(pieces) // 2
    copies = []
    for i, piece in enumerate(pieces):
        origin = seq_idx if i < half else seq_idx + 1 - 2 * lax.rem(seq_idx, 2)
        source = lax.rem(origin - 2 * (i % half) + count, count)
        start = pl.multiple_of(source * rows, TOK)
        copies.append(pltpu.make_async_copy(piece, kbuf.at[pl.ds(start, rows)], sems.at[i]))
    return copies


def prefill_kernel(
    info_ref, start_ref, qa_ref, *refs, count, fast, slow, heads, chunk, aliased
):
    pieces = refs[:count]
    refs = refs[count + (1 if aliased else 0) :]
    av_hbm, o_ref, kbuf, olat, av, ksem, vsem = refs
    tb = pl.program_id(0)
    last = pl.num_programs(0) - 1
    tokens = olat.shape[1]
    length = kbuf.shape[0]
    part = info_ref[1]
    av_copy = pltpu.make_async_copy(av_hbm.at[pl.ds(part * heads, heads)], av, vsem)

    @pl.when(tb == 0)
    def _():
        copies = gather_copies(pieces, kbuf, ksem, info_ref[0], count)
        for copy in copies:
            copy.start()
        av_copy.start()
        for copy in copies:
            copy.wait()

    base = info_ref[0] * tokens + tb * TOK
    first = info_ref[2 + tb]

    def attend(window, begin):
        begin = pl.multiple_of(begin, TOK)
        pos_q = base + lax.broadcasted_iota(jnp.int32, (TOK, window), 0)
        pos_k = begin + lax.broadcasted_iota(jnp.int32, (TOK, window), 1)
        keep = (pos_k >= start_ref[...]) & (pos_k <= pos_q)
        bias = jnp.where(keep, 0.0, NEG)[None]
        for c in range(0, heads * TOK, chunk):
            q = qa_ref[0, pl.ds(c, chunk), :]
            keys = kbuf[pl.ds(begin, window), :]
            s = lax.dot_general(q, keys, NT, preferred_element_type=jnp.float32)
            s = (s.reshape(chunk // TOK, TOK, window) + bias).reshape(chunk, window)
            m = jnp.max(s, axis=1, keepdims=True)
            p = jnp.exp2((s - m) * SCALE2)
            den = jnp.sum(p, axis=1, keepdims=True)
            o = jnp.dot(
                p.astype(jnp.bfloat16),
                kbuf[pl.ds(begin, window), :LAT],
                preferred_element_type=jnp.float32,
            )
            o = (o * (1.0 / den)).astype(jnp.bfloat16)
            olat[pl.ds(c // TOK, chunk // TOK), pl.ds(pl.multiple_of(tb * TOK, TOK), TOK), :] = (
                o.reshape(chunk // TOK, TOK, LAT)
            )

    fast_begin = jnp.clip(base + TOK - fast, 0, length - fast)
    slow_begin = jnp.clip(base + TOK - slow, 0, length - slow)

    @pl.when(first >= fast_begin)
    def _():
        attend(fast, fast_begin)

    @pl.when(first < fast_begin)
    def _():
        attend(slow, slow_begin)

    @pl.when(tb == last)
    def _():
        av_copy.wait()
        for h in range(heads):
            r = jnp.dot(olat[h], av[h], preferred_element_type=jnp.float32)
            o_ref[:, h * VHEAD : (h + 1) * VHEAD] = r.astype(jnp.bfloat16)


def attend_prefill(info, starts, qa, pieces, absorb_value, part, parts, most, out=None):
    blocks, rows, _ = qa.shape
    tokens = blocks * TOK
    heads = rows // TOK // parts
    count = len(pieces)
    length = count * tokens
    fast = min(most, length)
    slow = min(most + 128, length)
    hbm = pl.BlockSpec(memory_space=pl.ANY)
    aliased = out is not None
    args = [info, starts, qa, *pieces, *([out] if aliased else []), absorb_value]
    return pl.pallas_call(
        functools.partial(
            prefill_kernel,
            count=count,
            fast=fast,
            slow=slow,
            heads=heads,
            chunk=256,
            aliased=aliased,
        ),
        grid_spec=pltpu.PrefetchScalarGridSpec(
            num_scalar_prefetch=1,
            grid=(blocks,),
            in_specs=[
                pl.BlockSpec((TOK, 1), lambda i, info: (i, 0)),
                pl.BlockSpec((1, heads * TOK, WIDTH), lambda i, info: (i, part, 0)),
                *([hbm] * count),
                *([hbm] if aliased else []),
                hbm,
            ],
            out_specs=pl.BlockSpec((tokens, heads * VHEAD), lambda i, info: (0, part)),
            scratch_shapes=[
                pltpu.VMEM((length, WIDTH), jnp.bfloat16),
                pltpu.VMEM((heads, tokens, LAT), jnp.bfloat16),
                pltpu.VMEM((heads, LAT, VHEAD), jnp.bfloat16),
                pltpu.SemaphoreType.DMA((count,)),
                pltpu.SemaphoreType.DMA,
            ],
        ),
        out_shape=jax.ShapeDtypeStruct((tokens, parts * heads * VHEAD), jnp.bfloat16),
        input_output_aliases={3 + count: 0} if aliased else {},
        cost_estimate=pl.CostEstimate(
            flops=2 * tokens * heads * (fast * (WIDTH + LAT) + LAT * VHEAD),
            bytes_accessed=2 * heads * (tokens * (WIDTH + VHEAD) + LAT * VHEAD),
            transcendentals=tokens * heads * fast,
        ),
        compiler_params=pltpu.CompilerParams(vmem_limit_bytes=VMEM_LIMIT),
        name=f"attend_prefill_{part}",
    )(*args)


def decode_kernel(info_ref, lim_ref, fid_ref, *refs, count, spans, docs, steps, group):
    pieces = refs[:count]
    queries = refs[count : count + spans]
    fresh_refs = refs[count + spans : count + 2 * spans]
    ak_ref, av_ref, o_ref, kbuf, qbuf, ksem, qsem = refs[count + 2 * spans :]
    seq_idx = info_ref[0]
    span_idx = info_ref[1]
    per = steps * group
    rows = docs * per
    copies = gather_copies(pieces, kbuf, ksem, seq_idx, count)
    for copy in copies:
        copy.start()
    for d in range(docs):
        seq = info_ref[2 + d]
        turn = lax.rem(span_idx - seq // docs + spans, spans)
        for j in range(spans):

            @pl.when(turn == j)
            def _():
                pltpu.make_async_copy(
                    queries[j].at[lax.rem(seq, docs)], qbuf.at[d], qsem.at[d]
                ).start()

    for d in range(docs):
        pltpu.make_async_copy(queries[0].at[0], qbuf.at[d], qsem.at[d]).wait()
    q = qbuf[...].reshape(rows, NOPE + ROPE)
    head = lax.rem(lax.broadcasted_iota(jnp.int32, (rows, NOPE), 0), group)
    nope = q[:, :NOPE]
    zero = jnp.zeros_like(nope)
    wide = jnp.concatenate([jnp.where(head == h, nope, zero) for h in range(group)], axis=1)
    lat = jnp.dot(
        wide, ak_ref[...].reshape(group * NOPE, LAT), preferred_element_type=jnp.float32
    ).astype(jnp.bfloat16)
    qa = jnp.concatenate([lat, q[:, NOPE:]], axis=1)
    fresh = jnp.concatenate([ref[...] for ref in fresh_refs], axis=0)
    for copy in copies:
        copy.wait()
    keys = kbuf[...]
    lim = lim_ref[...]
    old = lax.dot_general(qa, keys, NT, preferred_element_type=jnp.float32)
    pos = lax.broadcasted_iota(jnp.int32, old.shape, 1)
    old = jnp.where((pos >= lim[:, 0:1]) & (pos < lim[:, 1:2]), old, NEG)
    new = lax.dot_general(qa, fresh, NT, preferred_element_type=jnp.float32)
    fid = fid_ref[...]
    new = jnp.where((fid >= lim[:, 2:3]) & (fid <= lim[:, 3:4]), new, NEG)
    m = jnp.maximum(
        jnp.max(old, axis=1, keepdims=True), jnp.max(new, axis=1, keepdims=True)
    )
    old = jnp.exp2((old - m) * SCALE2)
    new = jnp.exp2((new - m) * SCALE2)
    den = jnp.sum(old, axis=1, keepdims=True) + jnp.sum(new, axis=1, keepdims=True)
    o = jnp.dot(old.astype(jnp.bfloat16), keys[:, :LAT], preferred_element_type=jnp.float32)
    o = o + jnp.dot(
        new.astype(jnp.bfloat16), fresh[:, :LAT], preferred_element_type=jnp.float32
    )
    o = o * (1.0 / den)
    high = o.astype(jnp.bfloat16)
    low = (o - high.astype(jnp.float32)).astype(jnp.bfloat16)
    both = jnp.concatenate([high, low], axis=0)
    result = jnp.zeros((rows, VHEAD), jnp.float32)
    for h in range(group):
        r = jnp.dot(both, av_ref[h], preferred_element_type=jnp.float32)
        result = jnp.where(head == h, r[:rows] + r[rows:], result)
    o_ref[...] = result.astype(jnp.bfloat16).reshape(docs, per, VHEAD)


def attend_decode(info, limits, fresh_ids, pieces, queries, fresh, absorb_key, absorb_value):
    docs, per, size = queries[0].shape
    count, spans = len(pieces), len(queries)
    tokens = pieces[0].shape[0]
    heads = absorb_key.shape[0]
    group = heads // count
    steps = per // group
    hbm = pl.BlockSpec(memory_space=pl.ANY)
    rows = docs * per
    length = count * tokens
    return pl.pallas_call(
        functools.partial(
            decode_kernel, count=count, spans=spans, docs=docs, steps=steps, group=group
        ),
        grid_spec=pltpu.PrefetchScalarGridSpec(
            num_scalar_prefetch=1,
            grid=(1,),
            in_specs=[
                pl.BlockSpec(limits.shape, lambda i, info: (0, 0)),
                pl.BlockSpec(fresh_ids.shape, lambda i, info: (0, 0)),
                *([hbm] * (count + spans)),
                *([pl.BlockSpec(fresh[0].shape, lambda i, info: (0, 0))] * spans),
                pl.BlockSpec((group, NOPE, LAT), lambda i, info: (info[0], 0, 0)),
                pl.BlockSpec((group, LAT, VHEAD), lambda i, info: (info[0], 0, 0)),
            ],
            out_specs=pl.BlockSpec((docs, per, VHEAD), lambda i, info: (0, 0, 0)),
            scratch_shapes=[
                pltpu.VMEM((length, WIDTH), jnp.bfloat16),
                pltpu.VMEM((docs, per, size), jnp.bfloat16),
                pltpu.SemaphoreType.DMA((count,)),
                pltpu.SemaphoreType.DMA((docs,)),
            ],
        ),
        out_shape=jax.ShapeDtypeStruct((docs, per, VHEAD), jnp.bfloat16),
        cost_estimate=pl.CostEstimate(
            flops=2 * rows * length * (WIDTH + LAT),
            bytes_accessed=2 * (length * WIDTH + group * LAT * VHEAD * 2),
            transcendentals=rows * length,
        ),
        compiler_params=pltpu.CompilerParams(vmem_limit_bytes=VMEM_LIMIT),
        name="attend_decode",
    )(info, limits, fresh_ids, *pieces, *queries, *fresh, absorb_key, absorb_value)


def select_kernel(info_ref, *refs, spans, docs, steps, group):
    parts, o_ref, wide = refs[:spans], refs[spans], refs[spans + 1]
    for slot in range(docs):
        place = info_ref[slot]
        turn = place // docs
        doc = lax.rem(place, docs)
        value = parts[0][doc]
        for j in range(1, spans):
            value = jnp.where(turn == j, parts[j][doc], value)
        value = value.astype(jnp.float32)
        for t in range(steps):
            for h in range(group):
                row = t * group + h
                wide[t, slot : slot + 1, h * VHEAD : (h + 1) * VHEAD] = value[row : row + 1, :]
    o_ref[...] = wide[...].astype(jnp.bfloat16)


def select_rows(places, parts, steps):
    docs, per, _ = parts[0].shape
    group = per // steps
    spans = len(parts)
    shape = (steps, docs, group * VHEAD)
    return pl.pallas_call(
        functools.partial(select_kernel, spans=spans, docs=docs, steps=steps, group=group),
        grid_spec=pltpu.PrefetchScalarGridSpec(
            num_scalar_prefetch=1,
            grid=(1,),
            in_specs=[pl.BlockSpec(parts[0].shape, lambda i, info: (0, 0, 0))] * spans,
            out_specs=pl.BlockSpec(shape, lambda i, info: (0, 0, 0)),
            scratch_shapes=[pltpu.VMEM(shape, jnp.float32)],
        ),
        out_shape=jax.ShapeDtypeStruct(shape, jnp.bfloat16),
        name="select_rows",
    )(places, *parts)


def assemble_kernel(info_ref, *refs):
    count = len(refs) - 1
    half = count // 2
    seq_idx = info_ref[0]
    size = refs[0].shape[2]
    for i in range(count):
        origin = seq_idx if i < half else seq_idx + 1 - 2 * lax.rem(seq_idx, 2)
        source = lax.rem(origin - 2 * (i % half) + count, count)
        refs[count][:, :, pl.ds(pl.multiple_of(source * size, 128), size)] = refs[i][...]


def assemble(info, parts):
    steps, docs, size = parts[0].shape
    count = len(parts)
    shape = (steps, docs, count * size)
    return pl.pallas_call(
        assemble_kernel,
        grid_spec=pltpu.PrefetchScalarGridSpec(
            num_scalar_prefetch=1,
            grid=(1,),
            in_specs=[pl.BlockSpec(parts[0].shape, lambda i, info: (0, 0, 0))] * count,
            out_specs=pl.BlockSpec(shape, lambda i, info: (0, 0, 0)),
        ),
        out_shape=jax.ShapeDtypeStruct(shape, jnp.bfloat16),
        name="assemble",
    )(info, *parts)


def spread_seq(value, count):
    far = [
        lax.ppermute(value, "seq", [(i, (i + 2 * k) % count) for i in range(count)])
        for k in range(1, count // 2)
    ]
    mine = [value, *far]
    swap = [(i, i ^ 1) for i in range(count)]
    return mine + [lax.ppermute(piece, "seq", swap) for piece in mine]


def spread_span(value, spans):
    return [value] + [
        lax.ppermute(value, "span", [(i, (i + k) % spans) for i in range(spans)])
        for k in range(1, spans)
    ]


def body(
    q_prefill,
    kv_latent,
    key_rope,
    segment_ids,
    assignment,
    absorb_key,
    absorb_value,
    q_decode,
    new_latent,
    new_rope,
):
    tokens, heads, size = q_prefill.shape[1:]
    steps, docs = q_decode.shape[:2]
    length = segment_ids.shape[1]
    count = lax.axis_size("seq")
    spans = lax.axis_size("span")
    seq_idx = lax.axis_index("seq")
    span_idx = lax.axis_index("span")
    group = heads // count
    most = length // 2

    pieces = spread_seq(cache_rows(kv_latent[0], key_rope[0]), count)
    q_slice = lax.dynamic_slice_in_dim(q_decode, seq_idx * group, group, 2)
    q_slice = q_slice.transpose(1, 0, 2, 3).reshape(docs, steps * group, size)
    queries = spread_span(q_slice, spans)
    fresh_own = cache_rows(new_latent, new_rope).reshape(steps * docs, WIDTH)
    fresh = spread_span(fresh_own, spans)

    seg = lax.dynamic_index_in_dim(segment_ids, span_idx, 0, keepdims=False)
    seg_q = lax.dynamic_slice_in_dim(seg, seq_idx * tokens, tokens)
    starts = jnp.sum((seg[None, :] < seg_q[:, None]).astype(jnp.int32), axis=1)
    doc_ids = jnp.arange(docs, dtype=jnp.int32)
    doc_lo = jnp.sum((seg[None, :] < doc_ids[:, None]).astype(jnp.int32), axis=1)
    doc_hi = jnp.sum((seg[None, :] <= doc_ids[:, None]).astype(jnp.int32), axis=1)
    own = lax.dynamic_slice_in_dim(assignment, span_idx * docs, docs)

    qa = absorb_prefill(q_prefill[0], absorb_key)

    local = jnp.arange(steps * docs, dtype=jnp.int32)
    local = (local % docs) * steps + local // docs
    turns = (span_idx - jnp.arange(spans, dtype=jnp.int32)) % spans
    fresh_ids = (turns[:, None] * (docs * steps) + local[None, :]).reshape(1, -1)
    row_doc = jnp.repeat(doc_ids, steps * group)
    row_step = jnp.tile(jnp.repeat(jnp.arange(steps, dtype=jnp.int32), group), docs)
    low_id = jnp.repeat(own, steps * group) * steps
    limits = jnp.stack(
        [
            jnp.repeat(doc_lo, steps * group),
            jnp.repeat(doc_hi, steps * group),
            low_id,
            low_id + row_step,
        ],
        axis=1,
    )
    decode_info = jnp.concatenate([jnp.stack([seq_idx, span_idx]).astype(jnp.int32), own])
    decoded = attend_decode(
        decode_info, limits, fresh_ids, pieces, queries, fresh, absorb_key, absorb_value
    )
    returned = spread_span(decoded, spans)

    first = starts.reshape(tokens // TOK, TOK)[:, 0]

    def info_of(part):
        return jnp.concatenate([jnp.stack([seq_idx, jnp.int32(part)]).astype(jnp.int32), first])

    out = None
    starts = starts.reshape(tokens, 1)
    out = attend_prefill(info_of(0), starts, qa, pieces, absorb_value, 0, PARTS, most)

    wanted = span_idx * docs + doc_ids
    index = jnp.arange(spans * docs, dtype=jnp.int32)
    where = jnp.sum(jnp.where(assignment[None, :] == wanted[:, None], index[None, :], 0), axis=1)
    places = ((span_idx - where // docs) % spans) * docs + where % docs
    chosen = select_rows(places.astype(jnp.int32), returned, steps)
    finals = spread_seq(chosen, count)

    for part in range(1, PARTS):
        out = attend_prefill(
            info_of(part), starts, qa, pieces, absorb_value, part, PARTS, most, out
        )
    decode_out = assemble(jnp.stack([seq_idx]).astype(jnp.int32), finals)
    return (out[None], decode_out)


def solution(mesh):
    in_specs = (
        P("span", "seq", None, None),
        P("span", "seq", None),
        P("span", "seq", None),
        P(),
        P(),
        P(),
        P(),
        P(None, "span", None, None),
        P(None, "span", None),
        P(None, "span", None),
    )
    out_specs = (P("span", "seq", None), P(None, "span", None))
    return jax.shard_map(body, mesh=mesh, in_specs=in_specs, out_specs=out_specs, check_vma=False)
```

```python
import functools
import math

import jax
import jax.numpy as jnp
from jax import lax
from jax.experimental import pallas as pl
from jax.experimental.pallas import tpu as pltpu
from jax.sharding import PartitionSpec as P

NOPE = 128
ROPE = 64
LAT = 512
VHEAD = 128
WIDTH = LAT + ROPE

NEG = -1e30
EPS = 1e-06
SCALE2 = (NOPE + ROPE) ** (-0.5) * math.log2(math.e)
TOK = 16
PARTS = 2
VMEM_LIMIT = 60 << 20

NT = (((1,), (1,)), ((), ()))
ANY = pl.BlockSpec(memory_space=pl.ANY)


def normed(values):
    values = values.astype(jnp.float32)
    mean = jnp.sum(values * values, axis=-1, keepdims=True) * (1.0 / values.shape[-1])
    return (values * lax.rsqrt(mean + EPS)).astype(jnp.bfloat16)


def prepare_kernel(info_ref, lat_ref, rope_ref, q_ref, nl_ref, nr_ref, cache_ref, pack_ref, *, group):
    steps, docs, block, _ = q_ref.shape
    cache_ref[:, :LAT] = normed(lat_ref[...])
    rope = jnp.transpose(rope_ref[...].astype(jnp.float32))
    cache_ref[:, LAT:] = rope.astype(jnp.bfloat16)
    wide = group * NOPE
    for t in range(steps):
        row = pl.ds(t * docs, docs)
        q = jnp.swapaxes(q_ref[t].astype(jnp.float32), 0, 1)
        part = q[:group]
        for k in range(1, block // group):
            chosen = lax.rem(info_ref[0], block // group) == k
            part = jnp.where(chosen, q[k * group : (k + 1) * group], part)
        part = part.astype(jnp.bfloat16)
        pack_ref[row, wide : wide + LAT] = normed(nl_ref[t])
        base = wide + LAT
        for h in range(group):
            pack_ref[row, h * NOPE : (h + 1) * NOPE] = part[h, :, :NOPE]
            pack_ref[row, base + h * ROPE : base + (h + 1) * ROPE] = part[h, :, NOPE:]
        pack_ref[row, base + group * ROPE :] = nr_ref[t]


def prepare(info, latent, rope, q_decode, new_latent, new_rope, group):
    tokens = latent.shape[0]
    steps, docs, heads, size = q_decode.shape
    block = max(group, 8)
    ratio = block // group
    full = lambda x: pl.BlockSpec(x.shape, lambda i, info: (0,) * x.ndim)
    out_shape = (
        jax.ShapeDtypeStruct((tokens, WIDTH), jnp.bfloat16),
        jax.ShapeDtypeStruct((steps * docs, group * size + WIDTH), jnp.bfloat16),
    )
    return pl.pallas_call(
        functools.partial(prepare_kernel, group=group),
        grid_spec=pltpu.PrefetchScalarGridSpec(
            num_scalar_prefetch=1,
            grid=(1,),
            in_specs=[
                full(latent),
                full(rope),
                pl.BlockSpec((steps, docs, block, size), lambda i, info: (0, 0, info[0] // ratio, 0)),
                full(new_latent),
                full(new_rope),
            ],
            out_specs=tuple(full(s) for s in out_shape),
        ),
        out_shape=out_shape,
        name="prepare",
    )(info, latent, rope, q_decode, new_latent, new_rope)


def absorb_kernel(q_ref, ak_ref, o_ref, *, group, tokens):
    for h in range(group):
        q = jnp.transpose(q_ref[h])
        lat = jnp.dot(q[:, :NOPE], ak_ref[h], preferred_element_type=jnp.float32)
        row = pl.ds(h * TOK, TOK)
        o_ref[:, row, :LAT] = lat.astype(jnp.bfloat16).reshape(tokens // TOK, TOK, LAT)
        o_ref[:, row, LAT:] = q[:, NOPE:].reshape(tokens // TOK, TOK, ROPE)


def absorb_prefill(q, absorb_key, group=8):
    heads, size, tokens = q.shape
    return pl.pallas_call(
        functools.partial(absorb_kernel, group=group, tokens=tokens),
        grid=(heads // group,),
        in_specs=[
            pl.BlockSpec((group, size, tokens), lambda i: (i, 0, 0)),
            pl.BlockSpec((group, NOPE, LAT), lambda i: (i, 0, 0)),
        ],
        out_specs=pl.BlockSpec((tokens // TOK, group * TOK, WIDTH), lambda i: (0, i, 0)),
        out_shape=jax.ShapeDtypeStruct((tokens // TOK, heads * TOK, WIDTH), jnp.bfloat16),
        cost_estimate=pl.CostEstimate(
            flops=2 * tokens * heads * NOPE * LAT,
            bytes_accessed=2 * heads * (tokens * (size + WIDTH) + NOPE * LAT),
            transcendentals=0,
        ),
        compiler_params=pltpu.CompilerParams(vmem_limit_bytes=VMEM_LIMIT),
        name="absorb_prefill",
    )(q, absorb_key)


def source_of(i, seq_idx, count):
    half = count // 2
    origin = seq_idx if i < half else seq_idx + 1 - 2 * lax.rem(seq_idx, 2)
    return lax.rem(origin - 2 * (i % half) + count, count)


def gather_copies(pieces, kbuf, sems, seq_idx):
    rows = pieces[0].shape[0]
    copies = []
    for i, piece in enumerate(pieces):
        start = pl.multiple_of(source_of(i, seq_idx, len(pieces)) * rows, TOK)
        copies.append(pltpu.make_async_copy(piece, kbuf.at[pl.ds(start, rows)], sems.at[i]))
    return copies


def prefill_kernel(
    info_ref, segs_ref, seg_ref, qa_ref, *refs, count, part, fast, slow, heads, chunk, aliased
):
    pieces = refs[:count]
    refs = refs[count + (1 if aliased else 0) :]
    av_hbm, o_ref, kbuf, olat, av, ksem, vsem = refs
    tb = pl.program_id(0)
    last = pl.num_programs(0) - 1
    tokens = olat.shape[1]
    length = kbuf.shape[0]
    seq_idx = info_ref[0]
    span_idx = info_ref[1]
    av_copy = pltpu.make_async_copy(av_hbm.at[pl.ds(part * heads, heads)], av, vsem)

    @pl.when(tb == 0)
    def _():
        copies = gather_copies(pieces, kbuf, ksem, seq_idx)
        for copy in copies:
            copy.start()
        av_copy.start()
        for copy in copies:
            copy.wait()

    base = seq_idx * tokens + tb * TOK
    seg = seg_ref[pl.ds(span_idx, 1), :]
    first = jnp.sum((seg < segs_ref[span_idx, base]).astype(jnp.int32))
    row = lax.broadcasted_iota(jnp.int32, (TOK, 1), 0)
    seg_q = jnp.zeros((TOK, 1), jnp.int32)
    for i in range(TOK):
        seg_q = jnp.where(row == i, segs_ref[span_idx, base + i], seg_q)
    start = jnp.sum((seg < seg_q).astype(jnp.int32), axis=1, keepdims=True)

    def attend(window, begin):
        begin = pl.multiple_of(begin, TOK)
        pos_k = begin + lax.broadcasted_iota(jnp.int32, (TOK, window), 1)
        keep = (pos_k >= start) & (pos_k <= base + row)
        bias = jnp.where(keep, 0.0, NEG)[None]
        for c in range(0, heads * TOK, chunk):
            q = qa_ref[0, pl.ds(c, chunk), :]
            keys = kbuf[pl.ds(begin, window), :]
            s = lax.dot_general(q, keys, NT, preferred_element_type=jnp.float32)
            s = (s.reshape(chunk // TOK, TOK, window) + bias).reshape(chunk, window)
            m = jnp.max(s, axis=1, keepdims=True)
            p = jnp.exp2((s - m) * SCALE2)
            den = jnp.sum(p, axis=1, keepdims=True)
            o = jnp.dot(
                p.astype(jnp.bfloat16),
                kbuf[pl.ds(begin, window), :LAT],
                preferred_element_type=jnp.float32,
            )
            o = (o * (1.0 / den)).astype(jnp.bfloat16)
            olat[pl.ds(c // TOK, chunk // TOK), pl.ds(pl.multiple_of(tb * TOK, TOK), TOK), :] = (
                o.reshape(chunk // TOK, TOK, LAT)
            )

    fast_begin = jnp.clip(base + TOK - fast, 0, length - fast)
    slow_begin = jnp.clip(base + TOK - slow, 0, length - slow)

    @pl.when(first >= fast_begin)
    def _():
        attend(fast, fast_begin)

    @pl.when(first < fast_begin)
    def _():
        attend(slow, slow_begin)

    @pl.when(tb == last)
    def _():
        av_copy.wait()
        for h in range(heads):
            r = jnp.dot(olat[h], av[h], preferred_element_type=jnp.float32)
            o_ref[:, h * VHEAD : (h + 1) * VHEAD] = r.astype(jnp.bfloat16)


def attend_prefill(info, segment_ids, qa, pieces, absorb_value, part, parts, most, out=None):
    blocks, rows, _ = qa.shape
    tokens = blocks * TOK
    heads = rows // TOK // parts
    count = len(pieces)
    length = count * tokens
    fast = min(most, length)
    slow = min(most + 128, length)
    aliased = out is not None
    args = [info, segment_ids, segment_ids, qa, *pieces, *([out] if aliased else []), absorb_value]
    return pl.pallas_call(
        functools.partial(
            prefill_kernel,
            count=count,
            part=part,
            fast=fast,
            slow=slow,
            heads=heads,
            chunk=256,
            aliased=aliased,
        ),
        grid_spec=pltpu.PrefetchScalarGridSpec(
            num_scalar_prefetch=2,
            grid=(blocks,),
            in_specs=[
                pl.BlockSpec(segment_ids.shape, lambda i, *_: (0, 0)),
                pl.BlockSpec((1, heads * TOK, WIDTH), lambda i, *_: (i, part, 0)),
                *([ANY] * (count + aliased + 1)),
            ],
            out_specs=pl.BlockSpec((tokens, heads * VHEAD), lambda i, *_: (0, part)),
            scratch_shapes=[
                pltpu.VMEM((length, WIDTH), jnp.bfloat16),
                pltpu.VMEM((heads, tokens, LAT), jnp.bfloat16),
                pltpu.VMEM((heads, LAT, VHEAD), jnp.bfloat16),
                pltpu.SemaphoreType.DMA((count,)),
                pltpu.SemaphoreType.DMA,
            ],
        ),
        out_shape=jax.ShapeDtypeStruct((tokens, parts * heads * VHEAD), jnp.bfloat16),
        input_output_aliases={4 + count: 0} if aliased else {},
        cost_estimate=pl.CostEstimate(
            flops=2 * tokens * heads * (fast * (WIDTH + LAT) + LAT * VHEAD),
            bytes_accessed=2 * heads * (tokens * (WIDTH + VHEAD) + LAT * VHEAD),
            transcendentals=tokens * heads * fast,
        ),
        compiler_params=pltpu.CompilerParams(vmem_limit_bytes=VMEM_LIMIT),
        name=f"attend_prefill_{part}",
    )(*args)


def decode_kernel(info_ref, assign_ref, seg_ref, *refs, count, spans, docs, steps, group):
    pieces = refs[:count]
    packs = refs[count : count + spans]
    ak_ref, av_ref, _, o_ref, kbuf, qa, ksem = refs[count + spans :]
    seq_idx = info_ref[0]
    span_idx = info_ref[1]
    near = steps * docs
    rows = near * group
    copies = gather_copies(pieces, kbuf, ksem, seq_idx)
    for copy in copies:
        copy.start()
    pack = jnp.concatenate([ref[...] for ref in packs], axis=0)
    row = lax.broadcasted_iota(jnp.int32, (near, 1), 0)
    want = jnp.zeros((near, 1), jnp.int32)
    for d in range(docs):
        want = jnp.where(lax.rem(row, docs) == d, assign_ref[span_idx * docs + d], want)
    want = want * steps
    step = row // docs
    lane = lax.broadcasted_iota(jnp.int32, (1, spans * near), 1)
    place = lax.rem(lane, near)
    owner = lax.rem(span_idx - lane // near + spans, spans)
    number = (owner * docs + lax.rem(place, docs)) * steps + place // docs
    pick = jnp.where(number == want + step, 1.0, 0.0).astype(jnp.bfloat16)
    wide = group * NOPE
    nope = jnp.dot(pick, pack[:, :wide], preferred_element_type=jnp.float32).astype(jnp.bfloat16)
    rope = jnp.dot(
        pick, pack[:, wide + LAT : wide + LAT + group * ROPE], preferred_element_type=jnp.float32
    ).astype(jnp.bfloat16)
    fresh = jnp.concatenate(
        [pack[:, wide : wide + LAT], pack[:, wide + LAT + group * ROPE :]], axis=1
    )
    for h in range(group):
        lat = jnp.dot(
            nope[:, h * NOPE : (h + 1) * NOPE], ak_ref[h], preferred_element_type=jnp.float32
        )
        qa[pl.ds(h * near, near), :LAT] = lat.astype(jnp.bfloat16)
        qa[pl.ds(h * near, near), LAT:] = rope[:, h * ROPE : (h + 1) * ROPE]
    for copy in copies:
        copy.wait()
    keys = kbuf[...]
    seg = seg_ref[pl.ds(span_idx, 1), :]
    old_bias = jnp.where(seg == lax.rem(row, docs), 0.0, NEG)[None]
    new_bias = jnp.where((number >= want) & (number <= want + step), 0.0, NEG)[None]
    query = qa[...]
    old = lax.dot_general(query, keys, NT, preferred_element_type=jnp.float32)
    old = (old.reshape(group, near, -1) + old_bias).reshape(rows, -1)
    new = lax.dot_general(query, fresh, NT, preferred_element_type=jnp.float32)
    new = (new.reshape(group, near, -1) + new_bias).reshape(rows, -1)
    m = jnp.maximum(jnp.max(old, axis=1, keepdims=True), jnp.max(new, axis=1, keepdims=True))
    old = jnp.exp2((old - m) * SCALE2)
    new = jnp.exp2((new - m) * SCALE2)
    den = jnp.sum(old, axis=1, keepdims=True) + jnp.sum(new, axis=1, keepdims=True)
    o = jnp.dot(old.astype(jnp.bfloat16), keys[:, :LAT], preferred_element_type=jnp.float32)
    o = o + jnp.dot(new.astype(jnp.bfloat16), fresh[:, :LAT], preferred_element_type=jnp.float32)
    o = o * (1.0 / den)
    high = o.astype(jnp.bfloat16)
    low = (o - high.astype(jnp.float32)).astype(jnp.bfloat16)
    for h in range(group):
        both = jnp.concatenate(
            [high[h * near : (h + 1) * near], low[h * near : (h + 1) * near]], axis=0
        )
        r = jnp.dot(both, av_ref[h], preferred_element_type=jnp.float32)
        o_ref[:, h * VHEAD : (h + 1) * VHEAD] = (r[:near] + r[near:]).astype(jnp.bfloat16)


def attend_decode(info, assignment, segment_ids, pieces, packs, absorb_key, absorb_value, after, steps):
    near, size = packs[0].shape
    docs = near // steps
    count, spans = len(pieces), len(packs)
    tokens = pieces[0].shape[0]
    heads = absorb_key.shape[0]
    group = heads // count
    rows = near * group
    length = count * tokens
    return pl.pallas_call(
        functools.partial(
            decode_kernel, count=count, spans=spans, docs=docs, steps=steps, group=group
        ),
        grid_spec=pltpu.PrefetchScalarGridSpec(
            num_scalar_prefetch=2,
            grid=(1,),
            in_specs=[
                pl.BlockSpec(segment_ids.shape, lambda i, *_: (0, 0)),
                *([ANY] * count),
                *([pl.BlockSpec((near, size), lambda i, *_: (0, 0))] * spans),
                pl.BlockSpec((group, NOPE, LAT), lambda i, info, _: (info[0], 0, 0)),
                pl.BlockSpec((group, LAT, VHEAD), lambda i, info, _: (info[0], 0, 0)),
                ANY,
            ],
            out_specs=pl.BlockSpec((near, group * VHEAD), lambda i, *_: (0, 0)),
            scratch_shapes=[
                pltpu.VMEM((length, WIDTH), jnp.bfloat16),
                pltpu.VMEM((rows, WIDTH), jnp.bfloat16),
                pltpu.SemaphoreType.DMA((count,)),
            ],
        ),
        out_shape=jax.ShapeDtypeStruct((near, group * VHEAD), jnp.bfloat16),
        cost_estimate=pl.CostEstimate(
            flops=2 * rows * length * (WIDTH + LAT),
            bytes_accessed=2 * (length * WIDTH + group * LAT * VHEAD * 2),
            transcendentals=rows * length,
        ),
        compiler_params=pltpu.CompilerParams(vmem_limit_bytes=VMEM_LIMIT),
        name="attend_decode",
    )(info, assignment, segment_ids, *pieces, *packs, absorb_key, absorb_value, after)


def select_kernel(info_ref, assign_ref, *refs, spans, docs, steps):
    parts, o_ref = refs[:spans], refs[-1]
    span_idx = info_ref[1]
    near = steps * docs
    value = jnp.concatenate([ref[...] for ref in parts], axis=0)
    lane = lax.broadcasted_iota(jnp.int32, (1, spans * near), 1)
    number = jnp.zeros((1, spans * near), jnp.int32)
    for j in range(spans):
        source = lax.rem(span_idx - j + spans, spans)
        for d in range(docs):
            here = (lane // near == j) & (lax.rem(lane, docs) == d)
            number = jnp.where(here, assign_ref[source * docs + d], number)
    number = number * steps + lax.rem(lane, near) // docs
    row = lax.broadcasted_iota(jnp.int32, (near, 1), 0)
    want = (span_idx * docs + lax.rem(row, docs)) * steps + row // docs
    pick = jnp.where(number == want, 1.0, 0.0).astype(jnp.bfloat16)
    o_ref[...] = jnp.dot(pick, value, preferred_element_type=jnp.float32).astype(jnp.bfloat16)


def select_rows(info, assignment, parts, after, steps):
    near, size = parts[0].shape
    spans = len(parts)
    return pl.pallas_call(
        functools.partial(select_kernel, spans=spans, docs=near // steps, steps=steps),
        grid_spec=pltpu.PrefetchScalarGridSpec(
            num_scalar_prefetch=2,
            grid=(1,),
            in_specs=[*([pl.BlockSpec((near, size), lambda i, *_: (0, 0))] * spans), ANY],
            out_specs=pl.BlockSpec((near, size), lambda i, *_: (0, 0)),
        ),
        out_shape=jax.ShapeDtypeStruct((near, size), jnp.bfloat16),
        name="select_rows",
    )(info, assignment, *parts, after)


def assemble_kernel(info_ref, *refs):
    parts, o_ref, sems = refs[:-2], refs[-2], refs[-1]
    near, size = parts[0].shape
    copies = []
    for i, part in enumerate(parts):
        start = pl.multiple_of(source_of(i, info_ref[0], len(parts)) * size, 128)
        copies.append(pltpu.make_async_copy(part, o_ref.at[:, pl.ds(start, size)], sems.at[i]))
    for copy in copies:
        copy.start()
    for copy in copies:
        copy.wait()


def assemble(info, parts):
    near, size = parts[0].shape
    shape = (near, len(parts) * size)
    return pl.pallas_call(
        assemble_kernel,
        grid_spec=pltpu.PrefetchScalarGridSpec(
            num_scalar_prefetch=1,
            grid=(1,),
            in_specs=[ANY] * len(parts),
            out_specs=pl.BlockSpec(shape, lambda i, info: (0, 0)),
            scratch_shapes=[pltpu.SemaphoreType.DMA((len(parts),))],
        ),
        out_shape=jax.ShapeDtypeStruct(shape, jnp.bfloat16),
        name="assemble",
    )(info, *parts)


def spread_far(value, count):
    return [value] + [
        lax.ppermute(value, "seq", [(i, (i + 2 * k) % count) for i in range(count)])
        for k in range(1, count // 2)
    ]


def spread_near(pieces, count):
    swap = [(i, i ^ 1) for i in range(count)]
    return pieces + [lax.ppermute(piece, "seq", swap) for piece in pieces]


def spread_span(value, spans):
    return [value] + [
        lax.ppermute(value, "span", [(i, (i + k) % spans) for i in range(spans)])
        for k in range(1, spans)
    ]


def body(
    q_prefill,
    kv_latent,
    key_rope,
    segment_ids,
    assignment,
    absorb_key,
    absorb_value,
    q_decode,
    new_latent,
    new_rope,
):
    steps, docs, heads, _ = q_decode.shape
    count = lax.axis_size("seq")
    spans = lax.axis_size("span")
    group = heads // count
    most = segment_ids.shape[1] // 2
    info = jnp.stack([lax.axis_index("seq"), lax.axis_index("span")]).astype(jnp.int32)

    cache, pack = prepare(
        info, kv_latent[0], key_rope[0].T, q_decode, new_latent, new_rope, group
    )
    pieces = spread_far(cache, count)
    packs = spread_span(pack, spans)
    qa = absorb_prefill(q_prefill[0].transpose(1, 2, 0), absorb_key)
    pieces, qa = lax.optimization_barrier((pieces, qa))
    pieces = spread_near(pieces, count)
    decoded = attend_decode(
        info, assignment, segment_ids, pieces, packs, absorb_key, absorb_value, qa, steps
    )
    returned = spread_span(decoded, spans)
    out = attend_prefill(info, segment_ids, qa, pieces, absorb_value, 0, PARTS, most)
    chosen = select_rows(info, assignment, returned, out, steps)
    finals = spread_near(spread_far(chosen, count), count)
    for part in range(1, PARTS):
        out = attend_prefill(info, segment_ids, qa, pieces, absorb_value, part, PARTS, most, out)
    decode_out = assemble(info, finals)
    return (out[None], decode_out.reshape(steps, docs, heads * VHEAD))


def solution(mesh):
    in_specs = (
        P("span", "seq", None, None),
        P("span", "seq", None),
        P("span", "seq", None),
        P(),
        P(),
        P(),
        P(),
        P(None, "span", None, None),
        P(None, "span", None),
        P(None, "span", None),
    )
    out_specs = (P("span", "seq", None), P(None, "span", None))
    return jax.shard_map(body, mesh=mesh, in_specs=in_specs, out_specs=out_specs, check_vma=False)
```

```python
import functools
import math

import jax
import jax.numpy as jnp
from jax import lax
from jax.experimental import pallas as pl
from jax.experimental.pallas import tpu as pltpu
from jax.sharding import PartitionSpec as P

NOPE = 128
ROPE = 64
LAT = 512
VHEAD = 128
WIDTH = LAT + 2 * ROPE

NEG = -1e30
EPS = 1e-06
SCALE2 = (NOPE + ROPE) ** (-0.5) * math.log2(math.e)
TOK = 16
PARTS = 2
CHUNK = 512
VMEM_LIMIT = 60 << 20

NT = (((1,), (1,)), ((), ()))
ANY = pl.BlockSpec(memory_space=pl.ANY)


def normed(values):
    values = values.astype(jnp.float32)
    mean = jnp.sum(values * values, axis=-1, keepdims=True) * (1.0 / values.shape[-1])
    return (values * lax.rsqrt(mean + EPS)).astype(jnp.bfloat16)


def prepare_kernel(info_ref, lat_ref, rope_ref, q_ref, nl_ref, nr_ref, cache_ref, pack_ref, *, group):
    steps, docs, block, _ = q_ref.shape
    cache_ref[:, :LAT] = normed(lat_ref[...])
    rope = jnp.transpose(rope_ref[...].astype(jnp.float32))
    rope = rope.astype(jnp.bfloat16)
    cache_ref[:, LAT:] = jnp.concatenate([rope, jnp.zeros_like(rope)], axis=1)
    wide = group * NOPE
    for t in range(steps):
        row = pl.ds(t * docs, docs)
        q = jnp.swapaxes(q_ref[t].astype(jnp.float32), 0, 1)
        part = q[:group]
        for k in range(1, block // group):
            chosen = lax.rem(info_ref[0], block // group) == k
            part = jnp.where(chosen, q[k * group : (k + 1) * group], part)
        part = part.astype(jnp.bfloat16)
        pack_ref[row, wide : wide + LAT] = normed(nl_ref[t])
        base = wide + LAT
        for h in range(group):
            pack_ref[row, h * NOPE : (h + 1) * NOPE] = part[h, :, :NOPE]
            pack_ref[row, base + h * ROPE : base + (h + 1) * ROPE] = part[h, :, NOPE:]
        rope = nr_ref[t]
        pack_ref[row, base + group * ROPE :] = jnp.concatenate([rope, jnp.zeros_like(rope)], axis=1)


def prepare(info, latent, rope, q_decode, new_latent, new_rope, group):
    tokens = latent.shape[0]
    steps, docs, heads, size = q_decode.shape
    block = max(group, 8)
    ratio = block // group
    full = lambda x: pl.BlockSpec(x.shape, lambda i, info: (0,) * x.ndim)
    out_shape = (
        jax.ShapeDtypeStruct((tokens, WIDTH), jnp.bfloat16),
        jax.ShapeDtypeStruct((steps * docs, group * size + WIDTH), jnp.bfloat16),
    )
    return pl.pallas_call(
        functools.partial(prepare_kernel, group=group),
        grid_spec=pltpu.PrefetchScalarGridSpec(
            num_scalar_prefetch=1,
            grid=(1,),
            in_specs=[
                full(latent),
                full(rope),
                pl.BlockSpec((steps, docs, block, size), lambda i, info: (0, 0, info[0] // ratio, 0)),
                full(new_latent),
                full(new_rope),
            ],
            out_specs=tuple(full(s) for s in out_shape),
        ),
        out_shape=out_shape,
        name="prepare",
    )(info, latent, rope, q_decode, new_latent, new_rope)


def absorb_kernel(q_hbm, ak_hbm, o_hbm, q_buf, ak_buf, o_buf, q_sem, ak_sem, o_sem, *, group):
    heads, _, tokens = q_buf.shape
    number = heads // group

    def copies(i):
        part = pl.ds(i * group, group)
        return (
            pltpu.make_async_copy(q_hbm.at[part], q_buf.at[part], q_sem.at[i]),
            pltpu.make_async_copy(ak_hbm.at[part], ak_buf.at[part], ak_sem.at[i]),
        )

    def result(i):
        part = pl.ds(pl.multiple_of(i * group * TOK, group * TOK), group * TOK)
        return pltpu.make_async_copy(o_buf.at[:, part], o_hbm.at[:, part], o_sem.at[i])

    for i in range(number):
        for copy in copies(i):
            copy.start()

    @pl.loop(0, number)
    def _(i):
        for copy in copies(i):
            copy.wait()
        for j in range(group):
            h = i * group + j
            q = jnp.transpose(q_buf[h])
            lat = jnp.dot(q[:, :NOPE], ak_buf[h], preferred_element_type=jnp.float32)
            row = pl.ds(pl.multiple_of(h * TOK, TOK), TOK)
            o_buf[:, row, :LAT] = lat.astype(jnp.bfloat16).reshape(tokens // TOK, TOK, LAT)
            rope = jnp.concatenate([q[:, NOPE:], jnp.zeros_like(q[:, NOPE:])], axis=1)
            o_buf[:, row, LAT:] = rope.reshape(tokens // TOK, TOK, 2 * ROPE)
        result(i).start()

    for i in range(number):
        result(i).wait()


def absorb_prefill(q, absorb_key, group=8):
    heads, size, tokens = q.shape
    shape = (tokens // TOK, heads * TOK, WIDTH)
    return pl.pallas_call(
        functools.partial(absorb_kernel, group=group),
        in_specs=[ANY, ANY],
        out_specs=ANY,
        out_shape=jax.ShapeDtypeStruct(shape, jnp.bfloat16),
        scratch_shapes=[
            pltpu.VMEM(q.shape, jnp.bfloat16),
            pltpu.VMEM(absorb_key.shape, jnp.bfloat16),
            pltpu.VMEM(shape, jnp.bfloat16),
            pltpu.SemaphoreType.DMA((heads // group,)),
            pltpu.SemaphoreType.DMA((heads // group,)),
            pltpu.SemaphoreType.DMA((heads // group,)),
        ],
        cost_estimate=pl.CostEstimate(
            flops=2 * tokens * heads * NOPE * LAT,
            bytes_accessed=2 * heads * (tokens * (size + WIDTH) + NOPE * LAT),
            transcendentals=0,
        ),
        compiler_params=pltpu.CompilerParams(vmem_limit_bytes=VMEM_LIMIT),
        name="absorb_prefill",
    )(q, absorb_key)


def source_of(i, seq_idx, count):
    half = count // 2
    origin = seq_idx if i < half else seq_idx + 1 - 2 * lax.rem(seq_idx, 2)
    return lax.rem(origin - 2 * (i % half) + count, count)


def direct_source(i, seq_idx, count):
    return lax.rem(seq_idx - i + count, count)


def gather_copies(pieces, kbuf, sems, seq_idx):
    rows = pieces[0].shape[0]
    copies = []
    for i, piece in enumerate(pieces):
        start = pl.multiple_of(source_of(i, seq_idx, len(pieces)) * rows, TOK)
        copies.append(pltpu.make_async_copy(piece, kbuf.at[pl.ds(start, rows)], sems.at[i]))
    return copies


def prefill_kernel(
    info_ref, segs_ref, seg_ref, qa_hbm, *refs, count, part, fast, slow, heads, chunk, aliased
):
    pieces = refs[:count]
    refs = refs[count + (1 if aliased else 0) :]
    av_hbm, o_ref, kbuf, olat, av, qa_buf, ksem, qsem, vsem = refs
    blocks, rows, _ = qa_buf.shape
    tokens = olat.shape[1]
    length = kbuf.shape[0]
    seq_idx = info_ref[0]
    span_idx = info_ref[1]
    av_copy = pltpu.make_async_copy(av_hbm.at[pl.ds(part * heads, heads)], av, vsem)
    copies = gather_copies(pieces, kbuf, ksem, seq_idx)

    def qa_copy(i):
        return pltpu.make_async_copy(
            qa_hbm.at[i, pl.ds(part * rows, rows)], qa_buf.at[i], qsem.at[i]
        )

    ahead = min(2, blocks)
    near = fast // tokens + 1
    used = []
    for i in range(count):
        gap = seq_idx - source_of(i, seq_idx, count)
        used.append((gap >= 0) & (gap <= near) | (seq_idx < near))
    for copy, use in zip(copies, used):
        pl.when(use)(copy.start)
    for i in range(ahead):
        qa_copy(i).start()
    for copy, use in zip(copies, used):
        pl.when(use)(copy.wait)
    seg = seg_ref[pl.ds(span_idx, 1), :]
    row = lax.broadcasted_iota(jnp.int32, (TOK, 1), 0)

    @pl.loop(0, blocks)
    def _(tb):
        base = seq_idx * tokens + tb * TOK
        first = jnp.sum((seg < segs_ref[span_idx, base]).astype(jnp.int32))
        seg_q = jnp.zeros((TOK, 1), jnp.int32)
        for i in range(TOK):
            seg_q = jnp.where(row == i, segs_ref[span_idx, base + i], seg_q)
        start = jnp.sum((seg < seg_q).astype(jnp.int32), axis=1, keepdims=True)
        qa_copy(tb).wait()

        @pl.when(tb + ahead < blocks)
        def _():
            qa_copy(tb + ahead).start()

        @pl.when(tb == blocks // 2)
        def _():
            av_copy.start()

        def attend(window, begin, chunk):
            begin = pl.multiple_of(begin, TOK)
            pos_k = begin + lax.broadcasted_iota(jnp.int32, (TOK, window), 1)
            keep = (pos_k >= start) & (pos_k <= base + row)
            bias = jnp.where(keep, 0.0, NEG)[None]
            for c in range(0, heads * TOK, chunk):
                q = qa_buf[tb, pl.ds(c, chunk), :]
                keys = kbuf[pl.ds(begin, window), :]
                s = lax.dot_general(q, keys, NT, preferred_element_type=jnp.float32)
                s = (s.reshape(chunk // TOK, TOK, window) + bias).reshape(chunk, window)
                m = jnp.max(s, axis=1, keepdims=True)
                p = jnp.exp2((s - m) * SCALE2)
                den = jnp.sum(p, axis=1, keepdims=True)
                o = jnp.dot(
                    p.astype(jnp.bfloat16),
                    kbuf[pl.ds(begin, window), :LAT],
                    preferred_element_type=jnp.float32,
                )
                o = (o * (1.0 / den)).astype(jnp.bfloat16)
                place = pl.ds(pl.multiple_of(tb * TOK, TOK), TOK)
                olat[pl.ds(c // TOK, chunk // TOK), place, :] = o.reshape(chunk // TOK, TOK, LAT)

        fast_begin = jnp.clip(base + TOK - fast, 0, length - fast)
        slow_begin = jnp.clip(base + TOK - slow, 0, length - slow)

        @pl.when(first >= fast_begin)
        def _():
            attend(fast, fast_begin, chunk)

        @pl.when(first < fast_begin)
        def _():
            attend(slow, slow_begin, 128)

    av_copy.wait()
    for h in range(heads):
        r = jnp.dot(olat[h], av[h], preferred_element_type=jnp.float32)
        o_ref[:, h * VHEAD : (h + 1) * VHEAD] = r.astype(jnp.bfloat16)


def attend_prefill(info, segment_ids, qa, pieces, absorb_value, part, parts, most, out=None):
    blocks, rows, _ = qa.shape
    tokens = blocks * TOK
    heads = rows // TOK // parts
    count = len(pieces)
    length = count * tokens
    fast = min(most, length)
    slow = min(most + 128, length)
    aliased = out is not None
    args = [info, segment_ids, segment_ids, qa, *pieces, *([out] if aliased else []), absorb_value]
    return pl.pallas_call(
        functools.partial(
            prefill_kernel,
            count=count,
            part=part,
            fast=fast,
            slow=slow,
            heads=heads,
            chunk=CHUNK,
            aliased=aliased,
        ),
        grid_spec=pltpu.PrefetchScalarGridSpec(
            num_scalar_prefetch=2,
            grid=(1,),
            in_specs=[
                pl.BlockSpec(segment_ids.shape, lambda i, *_: (0, 0)),
                *([ANY] * (count + aliased + 2)),
            ],
            out_specs=pl.BlockSpec((tokens, heads * VHEAD), lambda i, *_: (0, part)),
            scratch_shapes=[
                pltpu.VMEM((length, WIDTH), jnp.bfloat16),
                pltpu.VMEM((heads, tokens, LAT), jnp.bfloat16),
                pltpu.VMEM((heads, LAT, VHEAD), jnp.bfloat16),
                pltpu.VMEM((blocks, heads * TOK, WIDTH), jnp.bfloat16),
                pltpu.SemaphoreType.DMA((count,)),
                pltpu.SemaphoreType.DMA((blocks,)),
                pltpu.SemaphoreType.DMA,
            ],
        ),
        out_shape=jax.ShapeDtypeStruct((tokens, parts * heads * VHEAD), jnp.bfloat16),
        input_output_aliases={4 + count: 0} if aliased else {},
        cost_estimate=pl.CostEstimate(
            flops=2 * tokens * heads * (fast * (WIDTH + LAT) + LAT * VHEAD),
            bytes_accessed=2 * heads * (tokens * (WIDTH + VHEAD) + LAT * VHEAD),
            transcendentals=tokens * heads * fast,
        ),
        compiler_params=pltpu.CompilerParams(vmem_limit_bytes=VMEM_LIMIT),
        name=f"attend_prefill_{part}",
    )(*args)


def decode_kernel(info_ref, assign_ref, seg_ref, *refs, count, spans, docs, steps, group):
    pieces = refs[:count]
    packs = refs[count : count + spans]
    ak_ref, av_ref, _, o_ref, kbuf, qa, ksem = refs[count + spans :]
    seq_idx = info_ref[0]
    span_idx = info_ref[1]
    near = steps * docs
    rows = near * group
    copies = gather_copies(pieces, kbuf, ksem, seq_idx)
    for copy in copies:
        copy.start()
    pack = jnp.concatenate([ref[...] for ref in packs], axis=0)
    row = lax.broadcasted_iota(jnp.int32, (near, 1), 0)
    want = jnp.zeros((near, 1), jnp.int32)
    for d in range(docs):
        want = jnp.where(lax.rem(row, docs) == d, assign_ref[span_idx * docs + d], want)
    want = want * steps
    step = row // docs
    lane = lax.broadcasted_iota(jnp.int32, (1, spans * near), 1)
    place = lax.rem(lane, near)
    owner = lax.rem(span_idx - lane // near + spans, spans)
    number = (owner * docs + lax.rem(place, docs)) * steps + place // docs
    pick = jnp.where(number == want + step, 1.0, 0.0).astype(jnp.bfloat16)
    wide = group * NOPE
    nope = jnp.dot(pick, pack[:, :wide], preferred_element_type=jnp.float32).astype(jnp.bfloat16)
    rope = jnp.dot(
        pick, pack[:, wide + LAT : wide + LAT + group * ROPE], preferred_element_type=jnp.float32
    ).astype(jnp.bfloat16)
    fresh = jnp.concatenate(
        [pack[:, wide : wide + LAT], pack[:, wide + LAT + group * ROPE :]], axis=1
    )
    for h in range(group):
        lat = jnp.dot(
            nope[:, h * NOPE : (h + 1) * NOPE], ak_ref[h], preferred_element_type=jnp.float32
        )
        qa[pl.ds(h * near, near), :LAT] = lat.astype(jnp.bfloat16)
        part = rope[:, h * ROPE : (h + 1) * ROPE]
        qa[pl.ds(h * near, near), LAT:] = jnp.concatenate([part, jnp.zeros_like(part)], axis=1)
    for copy in copies:
        copy.wait()
    keys = kbuf[...]
    seg = seg_ref[pl.ds(span_idx, 1), :]
    old_bias = jnp.where(seg == lax.rem(row, docs), 0.0, NEG)[None]
    new_bias = jnp.where((number >= want) & (number <= want + step), 0.0, NEG)[None]
    query = qa[...]
    old = lax.dot_general(query, keys, NT, preferred_element_type=jnp.float32)
    old = (old.reshape(group, near, -1) + old_bias).reshape(rows, -1)
    new = lax.dot_general(query, fresh, NT, preferred_element_type=jnp.float32)
    new = (new.reshape(group, near, -1) + new_bias).reshape(rows, -1)
    m = jnp.maximum(jnp.max(old, axis=1, keepdims=True), jnp.max(new, axis=1, keepdims=True))
    old = jnp.exp2((old - m) * SCALE2)
    new = jnp.exp2((new - m) * SCALE2)
    den = jnp.sum(old, axis=1, keepdims=True) + jnp.sum(new, axis=1, keepdims=True)
    o = jnp.dot(old.astype(jnp.bfloat16), keys[:, :LAT], preferred_element_type=jnp.float32)
    o = o + jnp.dot(new.astype(jnp.bfloat16), fresh[:, :LAT], preferred_element_type=jnp.float32)
    o = o * (1.0 / den)
    high = o.astype(jnp.bfloat16)
    low = (o - high.astype(jnp.float32)).astype(jnp.bfloat16)
    for h in range(group):
        both = jnp.concatenate(
            [high[h * near : (h + 1) * near], low[h * near : (h + 1) * near]], axis=0
        )
        r = jnp.dot(both, av_ref[h], preferred_element_type=jnp.float32)
        o_ref[:, h * VHEAD : (h + 1) * VHEAD] = (r[:near] + r[near:]).astype(jnp.bfloat16)


def attend_decode(info, assignment, segment_ids, pieces, packs, absorb_key, absorb_value, after, steps):
    near, size = packs[0].shape
    docs = near // steps
    count, spans = len(pieces), len(packs)
    tokens = pieces[0].shape[0]
    heads = absorb_key.shape[0]
    group = heads // count
    rows = near * group
    length = count * tokens
    return pl.pallas_call(
        functools.partial(
            decode_kernel, count=count, spans=spans, docs=docs, steps=steps, group=group
        ),
        grid_spec=pltpu.PrefetchScalarGridSpec(
            num_scalar_prefetch=2,
            grid=(1,),
            in_specs=[
                pl.BlockSpec(segment_ids.shape, lambda i, *_: (0, 0)),
                *([ANY] * count),
                *([pl.BlockSpec((near, size), lambda i, *_: (0, 0))] * spans),
                pl.BlockSpec((group, NOPE, LAT), lambda i, info, _: (info[0], 0, 0)),
                pl.BlockSpec((group, LAT, VHEAD), lambda i, info, _: (info[0], 0, 0)),
                ANY,
            ],
            out_specs=pl.BlockSpec((near, group * VHEAD), lambda i, *_: (0, 0)),
            scratch_shapes=[
                pltpu.VMEM((length, WIDTH), jnp.bfloat16),
                pltpu.VMEM((rows, WIDTH), jnp.bfloat16),
                pltpu.SemaphoreType.DMA((count,)),
            ],
        ),
        out_shape=jax.ShapeDtypeStruct((near, group * VHEAD), jnp.bfloat16),
        cost_estimate=pl.CostEstimate(
            flops=2 * rows * length * (WIDTH + LAT),
            bytes_accessed=2 * (length * WIDTH + group * LAT * VHEAD * 2),
            transcendentals=rows * length,
        ),
        compiler_params=pltpu.CompilerParams(vmem_limit_bytes=VMEM_LIMIT),
        name="attend_decode",
    )(info, assignment, segment_ids, *pieces, *packs, absorb_key, absorb_value, after)


def select_kernel(info_ref, assign_ref, *refs, spans, docs, steps):
    parts, o_ref = refs[:spans], refs[-1]
    span_idx = info_ref[1]
    near = steps * docs
    value = jnp.concatenate([ref[...] for ref in parts], axis=0)
    lane = lax.broadcasted_iota(jnp.int32, (1, spans * near), 1)
    number = jnp.zeros((1, spans * near), jnp.int32)
    for j in range(spans):
        source = lax.rem(span_idx - j + spans, spans)
        for d in range(docs):
            here = (lane // near == j) & (lax.rem(lane, docs) == d)
            number = jnp.where(here, assign_ref[source * docs + d], number)
    number = number * steps + lax.rem(lane, near) // docs
    row = lax.broadcasted_iota(jnp.int32, (near, 1), 0)
    want = (span_idx * docs + lax.rem(row, docs)) * steps + row // docs
    pick = jnp.where(number == want, 1.0, 0.0).astype(jnp.bfloat16)
    o_ref[...] = jnp.dot(pick, value, preferred_element_type=jnp.float32).astype(jnp.bfloat16)


def select_rows(info, assignment, parts, after, steps):
    near, size = parts[0].shape
    spans = len(parts)
    return pl.pallas_call(
        functools.partial(select_kernel, spans=spans, docs=near // steps, steps=steps),
        grid_spec=pltpu.PrefetchScalarGridSpec(
            num_scalar_prefetch=2,
            grid=(1,),
            in_specs=[*([pl.BlockSpec((near, size), lambda i, *_: (0, 0))] * spans), ANY],
            out_specs=pl.BlockSpec((near, size), lambda i, *_: (0, 0)),
        ),
        out_shape=jax.ShapeDtypeStruct((near, size), jnp.bfloat16),
        name="select_rows",
    )(info, assignment, *parts, after)


def assemble_kernel(info_ref, *refs):
    parts, o_ref, sems = refs[:-2], refs[-2], refs[-1]
    near, size = parts[0].shape
    copies = []
    for i, part in enumerate(parts):
        start = pl.multiple_of(direct_source(i, info_ref[0], len(parts)) * size, 128)
        copies.append(pltpu.make_async_copy(part, o_ref.at[:, pl.ds(start, size)], sems.at[i]))
    for copy in copies:
        copy.start()
    for copy in copies:
        copy.wait()


def assemble(info, parts):
    near, size = parts[0].shape
    shape = (near, len(parts) * size)
    return pl.pallas_call(
        assemble_kernel,
        grid_spec=pltpu.PrefetchScalarGridSpec(
            num_scalar_prefetch=1,
            grid=(1,),
            in_specs=[ANY] * len(parts),
            out_specs=pl.BlockSpec(shape, lambda i, info: (0, 0)),
            scratch_shapes=[pltpu.SemaphoreType.DMA((len(parts),))],
        ),
        out_shape=jax.ShapeDtypeStruct(shape, jnp.bfloat16),
        name="assemble",
    )(info, *parts)


def spread_far(value, count):
    return [value] + [
        lax.ppermute(value, "seq", [(i, (i + 2 * k) % count) for i in range(count)])
        for k in range(1, count // 2)
    ]


def spread_near(pieces, count):
    swap = [(i, i ^ 1) for i in range(count)]
    return pieces + [lax.ppermute(piece, "seq", swap) for piece in pieces]


def spread(value, axis, count):
    return [value] + [
        lax.ppermute(value, axis, [(i, (i + k) % count) for i in range(count)])
        for k in range(1, count)
    ]


def body(
    q_prefill,
    kv_latent,
    key_rope,
    segment_ids,
    assignment,
    absorb_key,
    absorb_value,
    q_decode,
    new_latent,
    new_rope,
):
    steps, docs, heads, _ = q_decode.shape
    count = lax.axis_size("seq")
    spans = lax.axis_size("span")
    group = heads // count
    most = segment_ids.shape[1] // 2
    info = jnp.stack([lax.axis_index("seq"), lax.axis_index("span")]).astype(jnp.int32)

    cache, pack = prepare(
        info, kv_latent[0], key_rope[0].T, q_decode, new_latent, new_rope, group
    )
    pieces = spread_far(cache, count)
    packs = spread(pack, "span", spans)
    qa = absorb_prefill(q_prefill[0].transpose(1, 2, 0), absorb_key)
    pieces, qa = lax.optimization_barrier((pieces, qa))
    pieces = spread_near(pieces, count)
    decoded = attend_decode(
        info, assignment, segment_ids, pieces, packs, absorb_key, absorb_value, qa, steps
    )
    returned = spread(decoded, "span", spans)
    out = attend_prefill(info, segment_ids, qa, pieces, absorb_value, 0, PARTS, most)
    chosen = select_rows(info, assignment, returned, out, steps)
    finals = spread(chosen, "seq", count)
    for part in range(1, PARTS):
        out = attend_prefill(info, segment_ids, qa, pieces, absorb_value, part, PARTS, most, out)
    decode_out = assemble(info, finals)
    return (out[None], decode_out.reshape(steps, docs, heads * VHEAD))


def solution(mesh):
    in_specs = (
        P("span", "seq", None, None),
        P("span", "seq", None),
        P("span", "seq", None),
        P(),
        P(),
        P(),
        P(),
        P(None, "span", None, None),
        P(None, "span", None),
        P(None, "span", None),
    )
    out_specs = (P("span", "seq", None), P(None, "span", None))
    return jax.shard_map(body, mesh=mesh, in_specs=in_specs, out_specs=out_specs, check_vma=False)
```

```python
import functools
import math

import jax
import jax.numpy as jnp
from jax import lax
from jax.experimental import pallas as pl
from jax.experimental.pallas import tpu as pltpu
from jax.sharding import PartitionSpec as P


NOPE = 128
ROPE = 64
LAT = 512
VHEAD = 128
WIDTH = LAT + 2 * ROPE

NEG = -1e30
EPS = 1e-06
SCALE2 = (NOPE + ROPE) ** (-0.5) * math.log2(math.e)
TOK = 16
PARTS = 2
CHUNK = 512
VMEM_LIMIT = 60 << 20

NT = (((1,), (1,)), ((), ()))
ANY = pl.BlockSpec(memory_space=pltpu.HBM)


def normed(values):
    values = values.astype(jnp.float32)
    mean = jnp.sum(values * values, axis=-1, keepdims=True) * (1.0 / values.shape[-1])
    return (values * lax.rsqrt(mean + EPS)).astype(jnp.bfloat16)


def prepare_kernel(info_ref, lat_ref, rope_ref, q_ref, nl_ref, nr_ref, cache_ref, pack_ref, *, group):
    steps, docs, block, _ = q_ref.shape
    cache_ref[:, :LAT] = normed(lat_ref[...])
    rope = jnp.transpose(rope_ref[...].astype(jnp.float32))
    rope = rope.astype(jnp.bfloat16)
    cache_ref[:, LAT:] = jnp.concatenate([rope, jnp.zeros_like(rope)], axis=1)
    wide = group * NOPE
    for t in range(steps):
        row = pl.ds(t * docs, docs)
        q = jnp.swapaxes(q_ref[t].astype(jnp.float32), 0, 1)
        part = q[:group]
        for k in range(1, block // group):
            chosen = lax.rem(info_ref[0], block // group) == k
            part = jnp.where(chosen, q[k * group : (k + 1) * group], part)
        part = part.astype(jnp.bfloat16)
        pack_ref[row, wide : wide + LAT] = normed(nl_ref[t])
        base = wide + LAT
        for h in range(group):
            pack_ref[row, h * NOPE : (h + 1) * NOPE] = part[h, :, :NOPE]
            pack_ref[row, base + h * ROPE : base + (h + 1) * ROPE] = part[h, :, NOPE:]
        rope = nr_ref[t]
        pack_ref[row, base + group * ROPE :] = jnp.concatenate([rope, jnp.zeros_like(rope)], axis=1)


def prepare(info, latent, rope, q_decode, new_latent, new_rope, group):
    tokens = latent.shape[0]
    steps, docs, _, size = q_decode.shape
    block = max(group, 8)
    ratio = block // group
    full = lambda x: pl.BlockSpec(x.shape, lambda i, info: (0,) * x.ndim)
    out_shape = (
        jax.ShapeDtypeStruct((tokens, WIDTH), jnp.bfloat16),
        jax.ShapeDtypeStruct((steps * docs, group * size + WIDTH), jnp.bfloat16),
    )
    return pl.pallas_call(
        functools.partial(prepare_kernel, group=group),
        grid_spec=pltpu.PrefetchScalarGridSpec(
            num_scalar_prefetch=1,
            grid=(1,),
            in_specs=[
                full(latent),
                full(rope),
                pl.BlockSpec((steps, docs, block, size), lambda i, info: (0, 0, info[0] // ratio, 0)),
                full(new_latent),
                full(new_rope),
            ],
            out_specs=tuple(full(s) for s in out_shape),
        ),
        out_shape=out_shape,
        name="prepare",
    )(info, latent, rope, q_decode, new_latent, new_rope)


def absorb_kernel(q_hbm, ak_hbm, o_hbm, q_buf, ak_buf, o_buf, q_sem, ak_sem, o_sem, *, group):
    heads, _, tokens = q_buf.shape
    number = heads // group

    def copies(i):
        part = pl.ds(i * group, group)
        return (
            pltpu.make_async_copy(q_hbm.at[part], q_buf.at[part], q_sem.at[i]),
            pltpu.make_async_copy(ak_hbm.at[part], ak_buf.at[part], ak_sem.at[i]),
        )

    def result(i):
        part = pl.ds(pl.multiple_of(i * group * TOK, group * TOK), group * TOK)
        return pltpu.make_async_copy(o_buf.at[:, part], o_hbm.at[:, part], o_sem.at[i])

    for i in range(number):
        for copy in copies(i):
            copy.start()

    @pl.loop(0, number)
    def _(i):
        for copy in copies(i):
            copy.wait()
        for j in range(group):
            h = i * group + j
            q = jnp.transpose(q_buf[h])
            lat = jnp.dot(q[:, :NOPE], ak_buf[h], preferred_element_type=jnp.float32)
            row = pl.ds(pl.multiple_of(h * TOK, TOK), TOK)
            o_buf[:, row, :LAT] = lat.astype(jnp.bfloat16).reshape(tokens // TOK, TOK, LAT)
            rope = jnp.concatenate([q[:, NOPE:], jnp.zeros_like(q[:, NOPE:])], axis=1)
            o_buf[:, row, LAT:] = rope.reshape(tokens // TOK, TOK, 2 * ROPE)
        result(i).start()

    for i in range(number):
        result(i).wait()


def absorb_prefill(q, absorb_key, group=8):
    heads, size, tokens = q.shape
    shape = (tokens // TOK, heads * TOK, WIDTH)
    return pl.pallas_call(
        functools.partial(absorb_kernel, group=group),
        in_specs=[ANY, ANY],
        out_specs=ANY,
        out_shape=jax.ShapeDtypeStruct(shape, jnp.bfloat16),
        scratch_shapes=[
            pltpu.VMEM(q.shape, jnp.bfloat16),
            pltpu.VMEM(absorb_key.shape, jnp.bfloat16),
            pltpu.VMEM(shape, jnp.bfloat16),
            pltpu.SemaphoreType.DMA((heads // group,)),
            pltpu.SemaphoreType.DMA((heads // group,)),
            pltpu.SemaphoreType.DMA((heads // group,)),
        ],
        cost_estimate=pl.CostEstimate(
            flops=2 * tokens * heads * NOPE * LAT,
            bytes_accessed=2 * heads * (tokens * (size + WIDTH) + NOPE * LAT),
            transcendentals=0,
        ),
        compiler_params=pltpu.CompilerParams(vmem_limit_bytes=VMEM_LIMIT),
        name="absorb_prefill",
    )(q, absorb_key)


def source_of(i, seq_idx, count):
    half = count // 2
    origin = seq_idx if i < half else seq_idx + 1 - 2 * lax.rem(seq_idx, 2)
    return lax.rem(origin - 2 * (i % half) + count, count)


def direct_source(i, seq_idx, count):
    return lax.rem(seq_idx - i + count, count)


def gather_copies(pieces, kbuf, sems, seq_idx):
    rows = pieces[0].shape[0]
    copies = []
    for i, piece in enumerate(pieces):
        start = pl.multiple_of(source_of(i, seq_idx, len(pieces)) * rows, TOK)
        copies.append(pltpu.make_async_copy(piece, kbuf.at[pl.ds(start, rows)], sems.at[i]))
    return copies


def prefill_kernel(
    info_ref, segs_ref, seg_ref, qa_hbm, *refs, count, part, fast, slow, heads, chunk, aliased
):
    pieces = refs[:count]
    refs = refs[count + (1 if aliased else 0) :]
    av_hbm, o_ref, kbuf, olat, av, qa_buf, ksem, qsem, vsem = refs
    blocks, rows, _ = qa_buf.shape
    tokens = olat.shape[1]
    length = kbuf.shape[0]
    seq_idx = info_ref[0]
    span_idx = info_ref[1]
    av_copy = pltpu.make_async_copy(av_hbm.at[pl.ds(part * heads, heads)], av, vsem)
    copies = gather_copies(pieces, kbuf, ksem, seq_idx)

    def qa_copy(i):
        return pltpu.make_async_copy(
            qa_hbm.at[i, pl.ds(part * rows, rows)], qa_buf.at[i], qsem.at[i]
        )

    ahead = min(2, blocks)
    near = fast // tokens + 1
    used = []
    for i in range(count):
        gap = seq_idx - source_of(i, seq_idx, count)
        used.append((gap >= 0) & (gap <= near) | (seq_idx < near))
    for copy, use in zip(copies, used):
        pl.when(use)(copy.start)
    for i in range(ahead):
        qa_copy(i).start()
    for copy, use in zip(copies, used):
        pl.when(use)(copy.wait)
    seg = seg_ref[pl.ds(span_idx, 1), :]
    row = lax.broadcasted_iota(jnp.int32, (TOK, 1), 0)

    @pl.loop(0, blocks)
    def _(tb):
        base = seq_idx * tokens + tb * TOK
        qa_copy(tb).wait()

        @pl.when(tb + ahead < blocks)
        def _():
            qa_copy(tb + ahead).start()

        @pl.when(tb == blocks // 2)
        def _():
            av_copy.start()

        def attend(window, begin, chunk):
            begin = pl.multiple_of(begin, TOK)
            seg_q = jnp.zeros((TOK, 1), jnp.int32)
            for i in range(TOK):
                seg_q = jnp.where(row == i, segs_ref[span_idx, base + i], seg_q)
            start = jnp.sum((seg < seg_q).astype(jnp.int32), axis=1, keepdims=True)
            pos_k = begin + lax.broadcasted_iota(jnp.int32, (TOK, window), 1)
            keep = (pos_k >= start) & (pos_k <= base + row)
            bias = jnp.where(keep, 0.0, NEG)[None]
            for c in range(0, heads * TOK, chunk):
                q = qa_buf[tb, pl.ds(c, chunk), :]
                keys = kbuf[pl.ds(begin, window), :]
                s = lax.dot_general(q, keys, NT, preferred_element_type=jnp.float32)
                s = (s.reshape(chunk // TOK, TOK, window) + bias).reshape(chunk, window)
                m = jnp.max(s, axis=1, keepdims=True)
                p = jnp.exp2((s - m) * SCALE2)
                den = jnp.sum(p, axis=1, keepdims=True)
                o = jnp.dot(
                    p.astype(jnp.bfloat16),
                    kbuf[pl.ds(begin, window), :LAT],
                    preferred_element_type=jnp.float32,
                )
                o = (o * (1.0 / den)).astype(jnp.bfloat16)
                place = pl.ds(pl.multiple_of(tb * TOK, TOK), TOK)
                olat[pl.ds(c // TOK, chunk // TOK), place, :] = o.reshape(chunk // TOK, TOK, LAT)

        fast_begin = jnp.clip(base + TOK - fast, 0, length - fast)
        slow_begin = jnp.clip(base + TOK - slow, 0, length - slow)

        ahead_seg = segs_ref[span_idx, jnp.maximum(fast_begin - 1, 0)]
        reaches = (fast_begin > 0) & (ahead_seg == segs_ref[span_idx, base])

        @pl.when(jnp.logical_not(reaches))
        def _():
            attend(fast, fast_begin, chunk)

        @pl.when(reaches)
        def _():
            attend(slow, slow_begin, 128)

    av_copy.wait()
    for h in range(heads):
        r = jnp.dot(olat[h], av[h], preferred_element_type=jnp.float32)
        o_ref[:, h * VHEAD : (h + 1) * VHEAD] = r.astype(jnp.bfloat16)


def attend_prefill(info, segment_ids, qa, pieces, absorb_value, part, parts, most, out=None):
    blocks, rows, _ = qa.shape
    tokens = blocks * TOK
    heads = rows // TOK // parts
    count = len(pieces)
    length = count * tokens
    fast = min(most, length)
    slow = min(most + 128, length)
    aliased = out is not None
    args = [info, segment_ids, segment_ids, qa, *pieces, *([out] if aliased else []), absorb_value]
    return pl.pallas_call(
        functools.partial(
            prefill_kernel,
            count=count,
            part=part,
            fast=fast,
            slow=slow,
            heads=heads,
            chunk=CHUNK,
            aliased=aliased,
        ),
        grid_spec=pltpu.PrefetchScalarGridSpec(
            num_scalar_prefetch=2,
            grid=(1,),
            in_specs=[
                pl.BlockSpec(segment_ids.shape, lambda i, *_: (0, 0)),
                *([ANY] * (count + aliased + 2)),
            ],
            out_specs=pl.BlockSpec((tokens, heads * VHEAD), lambda i, *_: (0, part)),
            scratch_shapes=[
                pltpu.VMEM((length, WIDTH), jnp.bfloat16),
                pltpu.VMEM((heads, tokens, LAT), jnp.bfloat16),
                pltpu.VMEM((heads, LAT, VHEAD), jnp.bfloat16),
                pltpu.VMEM((blocks, heads * TOK, WIDTH), jnp.bfloat16),
                pltpu.SemaphoreType.DMA((count,)),
                pltpu.SemaphoreType.DMA((blocks,)),
                pltpu.SemaphoreType.DMA,
            ],
        ),
        out_shape=jax.ShapeDtypeStruct((tokens, parts * heads * VHEAD), jnp.bfloat16),
        input_output_aliases={4 + count: 0} if aliased else {},
        cost_estimate=pl.CostEstimate(
            flops=2 * tokens * heads * (fast * (WIDTH + LAT) + LAT * VHEAD),
            bytes_accessed=2 * heads * (tokens * (WIDTH + VHEAD) + LAT * VHEAD),
            transcendentals=tokens * heads * fast,
        ),
        compiler_params=pltpu.CompilerParams(vmem_limit_bytes=VMEM_LIMIT),
    )(*args)


def decode_kernel(info_ref, assign_ref, seg_ref, *refs, count, spans, docs, steps, group):
    pieces = refs[:count]
    packs = refs[count : count + spans]
    ak_hbm, av_hbm, _, o_ref, kbuf, qa, pack_ref, ak_ref, av_ref, ksem, sems = refs[count + spans :]
    seq_idx = info_ref[0]
    span_idx = info_ref[1]
    near = steps * docs
    rows = near * group
    copies = gather_copies(pieces, kbuf, ksem, seq_idx)
    own = pl.ds(seq_idx * group, group)
    early = [
        pltpu.make_async_copy(pack, pack_ref.at[pl.ds(i * near, near)], sems.at[i])
        for i, pack in enumerate(packs)
    ]
    early.append(pltpu.make_async_copy(ak_hbm.at[own], ak_ref, sems.at[spans]))
    late = pltpu.make_async_copy(av_hbm.at[own], av_ref, sems.at[spans + 1])
    for copy in (*early, *copies, late):
        copy.start()
    row = lax.broadcasted_iota(jnp.int32, (near, 1), 0)
    want = jnp.zeros((near, 1), jnp.int32)
    for d in range(docs):
        want = jnp.where(lax.rem(row, docs) == d, assign_ref[span_idx * docs + d], want)
    want = want * steps
    step = row // docs
    lane = lax.broadcasted_iota(jnp.int32, (1, spans * near), 1)
    place = lax.rem(lane, near)
    owner = lax.rem(span_idx - lane // near + spans, spans)
    number = (owner * docs + lax.rem(place, docs)) * steps + place // docs
    pick = jnp.where(number == want + step, 1.0, 0.0).astype(jnp.bfloat16)
    wide = group * NOPE
    for copy in early:
        copy.wait()
    pack = pack_ref[...]
    nope = jnp.dot(pick, pack[:, :wide], preferred_element_type=jnp.float32).astype(jnp.bfloat16)
    rope = jnp.dot(
        pick, pack[:, wide + LAT : wide + LAT + group * ROPE], preferred_element_type=jnp.float32
    ).astype(jnp.bfloat16)
    fresh = jnp.concatenate(
        [pack[:, wide : wide + LAT], pack[:, wide + LAT + group * ROPE :]], axis=1
    )
    for h in range(group):
        lat = jnp.dot(
            nope[:, h * NOPE : (h + 1) * NOPE], ak_ref[h], preferred_element_type=jnp.float32
        )
        qa[pl.ds(h * near, near), :LAT] = lat.astype(jnp.bfloat16)
        part = rope[:, h * ROPE : (h + 1) * ROPE]
        qa[pl.ds(h * near, near), LAT:] = jnp.concatenate([part, jnp.zeros_like(part)], axis=1)
    for copy in copies:
        copy.wait()
    keys = kbuf[...]
    seg = seg_ref[pl.ds(span_idx, 1), :]
    old_bias = jnp.where(seg == lax.rem(row, docs), 0.0, NEG)[None]
    new_bias = jnp.where((number >= want) & (number <= want + step), 0.0, NEG)[None]
    query = qa[...]
    old = lax.dot_general(query, keys, NT, preferred_element_type=jnp.float32)
    old = (old.reshape(group, near, -1) + old_bias).reshape(rows, -1)
    new = lax.dot_general(query, fresh, NT, preferred_element_type=jnp.float32)
    new = (new.reshape(group, near, -1) + new_bias).reshape(rows, -1)
    m = jnp.maximum(jnp.max(old, axis=1, keepdims=True), jnp.max(new, axis=1, keepdims=True))
    old = jnp.exp2((old - m) * SCALE2)
    new = jnp.exp2((new - m) * SCALE2)
    den = jnp.sum(old, axis=1, keepdims=True) + jnp.sum(new, axis=1, keepdims=True)
    o = jnp.dot(old.astype(jnp.bfloat16), keys[:, :LAT], preferred_element_type=jnp.float32)
    o = o + jnp.dot(new.astype(jnp.bfloat16), fresh[:, :LAT], preferred_element_type=jnp.float32)
    o = o * (1.0 / den)
    high = o.astype(jnp.bfloat16)
    low = (o - high.astype(jnp.float32)).astype(jnp.bfloat16)
    late.wait()
    for h in range(group):
        both = jnp.concatenate(
            [high[h * near : (h + 1) * near], low[h * near : (h + 1) * near]], axis=0
        )
        r = jnp.dot(both, av_ref[h], preferred_element_type=jnp.float32)
        o_ref[:, h * VHEAD : (h + 1) * VHEAD] = (r[:near] + r[near:]).astype(jnp.bfloat16)


def attend_decode(info, assignment, segment_ids, pieces, packs, absorb_key, absorb_value, after, steps):
    near, size = packs[0].shape
    docs = near // steps
    count, spans = len(pieces), len(packs)
    tokens = pieces[0].shape[0]
    heads = absorb_key.shape[0]
    group = heads // count
    rows = near * group
    length = count * tokens
    return pl.pallas_call(
        functools.partial(
            decode_kernel, count=count, spans=spans, docs=docs, steps=steps, group=group
        ),
        grid_spec=pltpu.PrefetchScalarGridSpec(
            num_scalar_prefetch=2,
            grid=(1,),
            in_specs=[
                pl.BlockSpec(segment_ids.shape, lambda i, *_: (0, 0)),
                *([ANY] * (count + spans + 3)),
            ],
            out_specs=pl.BlockSpec((near, group * VHEAD), lambda i, *_: (0, 0)),
            scratch_shapes=[
                pltpu.VMEM((length, WIDTH), jnp.bfloat16),
                pltpu.VMEM((rows, WIDTH), jnp.bfloat16),
                pltpu.VMEM((spans * near, size), jnp.bfloat16),
                pltpu.VMEM((group, NOPE, LAT), jnp.bfloat16),
                pltpu.VMEM((group, LAT, VHEAD), jnp.bfloat16),
                pltpu.SemaphoreType.DMA((count,)),
                pltpu.SemaphoreType.DMA((spans + 2,)),
            ],
        ),
        out_shape=jax.ShapeDtypeStruct((near, group * VHEAD), jnp.bfloat16),
        cost_estimate=pl.CostEstimate(
            flops=2 * rows * length * (WIDTH + LAT),
            bytes_accessed=2 * (length * WIDTH + group * LAT * VHEAD * 2),
            transcendentals=rows * length,
        ),
        compiler_params=pltpu.CompilerParams(vmem_limit_bytes=VMEM_LIMIT),
        name="attend_decode",
    )(info, assignment, segment_ids, *pieces, *packs, absorb_key, absorb_value, after)


def select_kernel(info_ref, assign_ref, *refs, spans, docs, steps):
    parts = refs[:spans]
    o_ref, value, sems = refs[spans + 1 :]
    span_idx = info_ref[1]
    near = steps * docs
    copies = [
        pltpu.make_async_copy(part, value.at[pl.ds(i * near, near)], sems.at[i])
        for i, part in enumerate(parts)
    ]
    for copy in copies:
        copy.start()
    lane = lax.broadcasted_iota(jnp.int32, (1, spans * near), 1)
    number = jnp.zeros((1, spans * near), jnp.int32)
    for j in range(spans):
        source = lax.rem(span_idx - j + spans, spans)
        for d in range(docs):
            here = (lane // near == j) & (lax.rem(lane, docs) == d)
            number = jnp.where(here, assign_ref[source * docs + d], number)
    number = number * steps + lax.rem(lane, near) // docs
    row = lax.broadcasted_iota(jnp.int32, (near, 1), 0)
    want = (span_idx * docs + lax.rem(row, docs)) * steps + row // docs
    pick = jnp.where(number == want, 1.0, 0.0).astype(jnp.bfloat16)
    for copy in copies:
        copy.wait()
    o_ref[...] = jnp.dot(pick, value[...], preferred_element_type=jnp.float32).astype(jnp.bfloat16)


def select_rows(info, assignment, parts, after, steps):
    near, size = parts[0].shape
    spans = len(parts)
    return pl.pallas_call(
        functools.partial(select_kernel, spans=spans, docs=near // steps, steps=steps),
        grid_spec=pltpu.PrefetchScalarGridSpec(
            num_scalar_prefetch=2,
            grid=(1,),
            in_specs=[ANY] * (spans + 1),
            out_specs=pl.BlockSpec((near, size), lambda i, *_: (0, 0)),
            scratch_shapes=[
                pltpu.VMEM((spans * near, size), jnp.bfloat16),
                pltpu.SemaphoreType.DMA((spans,)),
            ],
        ),
        out_shape=jax.ShapeDtypeStruct((near, size), jnp.bfloat16),
        name="select_rows",
    )(info, assignment, *parts, after)


def assemble_kernel(info_ref, *refs):
    parts, o_ref, sems = refs[:-2], refs[-2], refs[-1]
    _, size = parts[0].shape
    copies = []
    for i, part in enumerate(parts):
        start = pl.multiple_of(direct_source(i, info_ref[0], len(parts)) * size, 128)
        copies.append(pltpu.make_async_copy(part, o_ref.at[:, pl.ds(start, size)], sems.at[i]))
    for copy in copies:
        copy.start()
    for copy in copies:
        copy.wait()


def assemble(info, parts):
    near, size = parts[0].shape
    shape = (near, len(parts) * size)
    return pl.pallas_call(
        assemble_kernel,
        grid_spec=pltpu.PrefetchScalarGridSpec(
            num_scalar_prefetch=1,
            grid=(1,),
            in_specs=[ANY] * len(parts),
            out_specs=pl.BlockSpec(shape, lambda i, info: (0, 0)),
            scratch_shapes=[pltpu.SemaphoreType.DMA((len(parts),))],
        ),
        out_shape=jax.ShapeDtypeStruct(shape, jnp.bfloat16),
        name="assemble",
    )(info, *parts)


def spread_far(value, count):
    return [value] + [
        lax.ppermute(value, "seq", [(i, (i + 2 * k) % count) for i in range(count)])
        for k in range(1, count // 2)
    ]


def spread_near(pieces, count):
    swap = [(i, i ^ 1) for i in range(count)]
    return pieces + [lax.ppermute(p, "seq", swap) for p in pieces]


def spread(value, axis, count):
    return [value] + [
        lax.ppermute(value, axis, [(i, (i + k) % count) for i in range(count)])
        for k in range(1, count)
    ]


def body(
    q_prefill,
    kv_latent,
    key_rope,
    segment_ids,
    assignment,
    absorb_key,
    absorb_value,
    q_decode,
    new_latent,
    new_rope,
):
    steps, docs, heads, _ = q_decode.shape
    count = lax.axis_size("seq")
    spans = lax.axis_size("span")
    group = heads // count
    most = segment_ids.shape[1] // 2
    info = jnp.stack([lax.axis_index("seq"), lax.axis_index("span")]).astype(jnp.int32)

    cache, pack = prepare(
        info, kv_latent[0], key_rope[0].T, q_decode, new_latent, new_rope, group
    )
    pieces = spread_far(cache, count)
    packs = spread(pack, "span", spans)
    qa = absorb_prefill(q_prefill[0].transpose(1, 2, 0), absorb_key)
    far, qa = lax.optimization_barrier((pieces[1:], qa))
    pieces = spread_near([cache, *far], count)
    decoded = attend_decode(
        info, assignment, segment_ids, pieces, packs, absorb_key, absorb_value, qa, steps
    )
    returned = spread(decoded, "span", spans)
    out = attend_prefill(info, segment_ids, qa, pieces, absorb_value, 0, PARTS, most)
    chosen = select_rows(info, assignment, returned, out, steps)
    finals = spread(chosen, "seq", count)
    for part in range(1, PARTS):
        out = attend_prefill(info, segment_ids, qa, pieces, absorb_value, part, PARTS, most, out)
    decode_out = assemble(info, finals)
    return (out[None], decode_out.reshape(steps, docs, heads * VHEAD))


def solution(mesh):
    in_specs = (
        P("span", "seq", None, None),
        P("span", "seq", None),
        P("span", "seq", None),
        P(),
        P(),
        P(),
        P(),
        P(None, "span", None, None),
        P(None, "span", None),
        P(None, "span", None),
    )
    out_specs = (P("span", "seq", None), P(None, "span", None))
    return jax.shard_map(body, mesh=mesh, in_specs=in_specs, out_specs=out_specs, check_vma=False)
```

```python
import functools
import math

import jax
import jax.numpy as jnp
from jax import lax
from jax.experimental import pallas as pl
from jax.experimental.pallas import tpu as pltpu
from jax.sharding import PartitionSpec as P


NOPE = 128
ROPE = 64
LAT = 512
VHEAD = 128
WIDTH = LAT + 2 * ROPE

NEG = -1e30
EPS = 1e-06
SCALE2 = (NOPE + ROPE) ** (-0.5) * math.log2(math.e)
TOK = 16
PARTS = 2
CHUNK = 512
MIB = 1 << 20

NT = (((1,), (1,)), ((), ()))
FAR = pl.BlockSpec(memory_space=pltpu.HBM)
ANY = pl.BlockSpec(memory_space=pl.ANY)


def normed(values):
    values = values.astype(jnp.float32)
    mean = jnp.sum(values * values, axis=-1, keepdims=True) * (1.0 / values.shape[-1])
    return (values * lax.rsqrt(mean + EPS)).astype(jnp.bfloat16)


def prepare_kernel(info_ref, lat_ref, rope_ref, q_ref, nl_ref, nr_ref, cache_ref, pack_ref, *, group):
    steps, docs, block, _ = q_ref.shape
    cache_ref[:, :LAT] = normed(lat_ref[...])
    rope = jnp.transpose(rope_ref[...].astype(jnp.float32))
    rope = rope.astype(jnp.bfloat16)
    cache_ref[:, LAT:] = jnp.concatenate([rope, jnp.zeros_like(rope)], axis=1)
    wide = group * NOPE
    for t in range(steps):
        row = pl.ds(t * docs, docs)
        q = jnp.swapaxes(q_ref[t].astype(jnp.float32), 0, 1)
        part = q[:group]
        for k in range(1, block // group):
            chosen = lax.rem(info_ref[0], block // group) == k
            part = jnp.where(chosen, q[k * group : (k + 1) * group], part)
        part = part.astype(jnp.bfloat16)
        pack_ref[row, wide : wide + LAT] = normed(nl_ref[t])
        base = wide + LAT
        for h in range(group):
            pack_ref[row, h * NOPE : (h + 1) * NOPE] = part[h, :, :NOPE]
            pack_ref[row, base + h * ROPE : base + (h + 1) * ROPE] = part[h, :, NOPE:]
        rope = nr_ref[t]
        pack_ref[row, base + group * ROPE :] = jnp.concatenate([rope, jnp.zeros_like(rope)], axis=1)


def prepare(info, latent, rope, q_decode, new_latent, new_rope, group):
    tokens = latent.shape[0]
    steps, docs, _, size = q_decode.shape
    block = max(group, 8)
    ratio = block // group
    full = lambda x: pl.BlockSpec(x.shape, lambda i, info: (0,) * x.ndim)
    out_shape = (
        jax.ShapeDtypeStruct((tokens, WIDTH), jnp.bfloat16),
        jax.ShapeDtypeStruct((steps * docs, group * size + WIDTH), jnp.bfloat16),
    )
    return pl.pallas_call(
        functools.partial(prepare_kernel, group=group),
        grid_spec=pltpu.PrefetchScalarGridSpec(
            num_scalar_prefetch=1,
            grid=(1,),
            in_specs=[
                full(latent),
                full(rope),
                pl.BlockSpec((steps, docs, block, size), lambda i, info: (0, 0, info[0] // ratio, 0)),
                full(new_latent),
                full(new_rope),
            ],
            out_specs=tuple(full(s) for s in out_shape),
        ),
        out_shape=out_shape,
        compiler_params=pltpu.CompilerParams(vmem_limit_bytes=60 * MIB),
        name="prepare",
    )(info, latent, rope, q_decode, new_latent, new_rope)


def absorb_kernel(q_hbm, ak_hbm, o_hbm, token_ref, q_buf, ak_buf, o_buf, q_sem, ak_sem, o_sem, *, group):
    heads, _, tokens = q_buf.shape
    number = heads // group
    token_ref[...] = jnp.zeros_like(token_ref)

    def copies(i):
        part = pl.ds(i * group, group)
        return (
            pltpu.make_async_copy(q_hbm.at[part], q_buf.at[part], q_sem.at[i]),
            pltpu.make_async_copy(ak_hbm.at[part], ak_buf.at[part], ak_sem.at[i]),
        )

    def result(i):
        part = pl.ds(pl.multiple_of(i * group * TOK, group * TOK), group * TOK)
        return pltpu.make_async_copy(o_buf.at[:, part], o_hbm.at[:, part], o_sem.at[i])

    for i in range(number):
        for copy in copies(i):
            copy.start()

    @pl.loop(0, number)
    def _(i):
        for copy in copies(i):
            copy.wait()
        for j in range(group):
            h = i * group + j
            q = jnp.transpose(q_buf[h])
            lat = jnp.dot(q[:, :NOPE], ak_buf[h], preferred_element_type=jnp.float32)
            row = pl.ds(pl.multiple_of(h * TOK, TOK), TOK)
            o_buf[:, row, :LAT] = lat.astype(jnp.bfloat16).reshape(tokens // TOK, TOK, LAT)
            rope = jnp.concatenate([q[:, NOPE:], jnp.zeros_like(q[:, NOPE:])], axis=1)
            o_buf[:, row, LAT:] = rope.reshape(tokens // TOK, TOK, 2 * ROPE)
        result(i).start()

    for i in range(number):
        result(i).wait()


def absorb_prefill(q, absorb_key, group=8):
    heads, size, tokens = q.shape
    shape = (tokens // TOK, heads * TOK, WIDTH)
    return pl.pallas_call(
        functools.partial(absorb_kernel, group=group),
        in_specs=[FAR, FAR],
        out_specs=(FAR, pl.BlockSpec(memory_space=pltpu.VMEM)),
        out_shape=(
            jax.ShapeDtypeStruct(shape, jnp.bfloat16),
            jax.ShapeDtypeStruct((8, 128), jnp.int32),
        ),
        scratch_shapes=[
            pltpu.VMEM(q.shape, jnp.bfloat16),
            pltpu.VMEM(absorb_key.shape, jnp.bfloat16),
            pltpu.VMEM(shape, jnp.bfloat16),
            pltpu.SemaphoreType.DMA((heads // group,)),
            pltpu.SemaphoreType.DMA((heads // group,)),
            pltpu.SemaphoreType.DMA((heads // group,)),
        ],
        cost_estimate=pl.CostEstimate(
            flops=2 * tokens * heads * NOPE * LAT,
            bytes_accessed=2 * heads * (tokens * (size + WIDTH) + NOPE * LAT),
            transcendentals=0,
        ),
        compiler_params=pltpu.CompilerParams(vmem_limit_bytes=61 * MIB),
        name="absorb_prefill",
    )(q, absorb_key)


def source_of(i, seq_idx, count):
    half = count // 2
    origin = seq_idx if i < half else seq_idx + 1 - 2 * lax.rem(seq_idx, 2)
    return lax.rem(origin - 2 * (i % half) + count, count)


def direct_source(i, seq_idx, count):
    return lax.rem(seq_idx - i + count, count)


def gather_copies(pieces, kbuf, sems, seq_idx):
    rows = pieces[0].shape[0]
    copies = []
    for i, piece in enumerate(pieces):
        start = pl.multiple_of(source_of(i, seq_idx, len(pieces)) * rows, TOK)
        copies.append(pltpu.make_async_copy(piece, kbuf.at[pl.ds(start, rows)], sems.at[i]))
    return copies


def prefill_kernel(
    info_ref, segs_ref, seg_ref, qa_hbm, keys_hbm, *refs, part, fast, slow, heads, chunk, aliased
):
    refs = refs[1 if aliased else 0 :]
    av_hbm, o_ref, token_ref, kbuf, olat, av, qa_buf, ksem, qsem, vsem = refs
    token_ref[...] = jnp.zeros_like(token_ref)
    blocks, rows, _ = qa_buf.shape
    tokens = olat.shape[1]
    held = kbuf.shape[0]
    length = keys_hbm.shape[0]
    seq_idx = info_ref[0]
    span_idx = info_ref[1]
    low = jnp.clip((seq_idx + 1) * tokens - held, 0, length - held)
    low = pl.multiple_of(low, TOK)
    keys_copy = pltpu.make_async_copy(keys_hbm.at[pl.ds(low, held)], kbuf, ksem)
    av_copy = pltpu.make_async_copy(av_hbm.at[pl.ds(part * heads, heads)], av, vsem)

    def qa_copy(i):
        return pltpu.make_async_copy(
            qa_hbm.at[i, pl.ds(part * rows, rows)], qa_buf.at[i], qsem.at[i]
        )

    ahead = min(2, blocks)
    keys_copy.start()
    for i in range(ahead):
        qa_copy(i).start()
    keys_copy.wait()
    seg = seg_ref[pl.ds(span_idx, 1), :]
    row = lax.broadcasted_iota(jnp.int32, (TOK, 1), 0)

    @pl.loop(0, blocks)
    def _(tb):
        base = seq_idx * tokens + tb * TOK
        qa_copy(tb).wait()

        @pl.when(tb + ahead < blocks)
        def _():
            qa_copy(tb + ahead).start()

        @pl.when(tb == blocks // 2)
        def _():
            av_copy.start()

        def attend(window, begin, chunk):
            begin = pl.multiple_of(begin, TOK)
            seg_q = jnp.zeros((TOK, 1), jnp.int32)
            for i in range(TOK):
                seg_q = jnp.where(row == i, segs_ref[span_idx, base + i], seg_q)
            start = jnp.sum((seg < seg_q).astype(jnp.int32), axis=1, keepdims=True)
            pos_k = begin + lax.broadcasted_iota(jnp.int32, (TOK, window), 1)
            keep = (pos_k >= start) & (pos_k <= base + row)
            bias = jnp.where(keep, 0.0, NEG)[None]
            spot = pl.multiple_of(begin - low, TOK)
            for c in range(0, heads * TOK, chunk):
                q = qa_buf[tb, pl.ds(c, chunk), :]
                keys = kbuf[pl.ds(spot, window), :]
                s = lax.dot_general(q, keys, NT, preferred_element_type=jnp.float32)
                s = (s.reshape(chunk // TOK, TOK, window) + bias).reshape(chunk, window)
                m = jnp.max(s, axis=1, keepdims=True)
                p = jnp.exp2((s - m) * SCALE2)
                den = jnp.sum(p, axis=1, keepdims=True)
                o = jnp.dot(
                    p.astype(jnp.bfloat16),
                    kbuf[pl.ds(spot, window), :LAT],
                    preferred_element_type=jnp.float32,
                )
                o = (o * (1.0 / den)).astype(jnp.bfloat16)
                place = pl.ds(pl.multiple_of(tb * TOK, TOK), TOK)
                olat[pl.ds(c // TOK, chunk // TOK), place, :] = o.reshape(chunk // TOK, TOK, LAT)

        fast_begin = jnp.clip(base + TOK - fast, 0, length - fast)
        slow_begin = jnp.clip(base + TOK - slow, 0, length - slow)

        ahead_seg = segs_ref[span_idx, jnp.maximum(fast_begin - 1, 0)]
        reaches = (fast_begin > 0) & (ahead_seg == segs_ref[span_idx, base])

        @pl.when(jnp.logical_not(reaches))
        def _():
            attend(fast, fast_begin, chunk)

        @pl.when(reaches)
        def _():
            attend(slow, slow_begin, 128)

    av_copy.wait()
    for h in range(heads):
        r = jnp.dot(olat[h], av[h], preferred_element_type=jnp.float32)
        o_ref[:, h * VHEAD : (h + 1) * VHEAD] = r.astype(jnp.bfloat16)


def attend_prefill(info, segment_ids, qa, keys, absorb_value, part, parts, most, out=None):
    blocks, rows, _ = qa.shape
    tokens = blocks * TOK
    heads = rows // TOK // parts
    length = keys.shape[0]
    fast = min(most, length)
    slow = min(most + 128, length)
    aliased = out is not None
    args = [info, segment_ids, segment_ids, qa, keys, *([out] if aliased else []), absorb_value]
    return pl.pallas_call(
        functools.partial(
            prefill_kernel,
            part=part,
            fast=fast,
            slow=slow,
            heads=heads,
            chunk=CHUNK,
            aliased=aliased,
        ),
        grid_spec=pltpu.PrefetchScalarGridSpec(
            num_scalar_prefetch=2,
            grid=(1,),
            in_specs=[
                pl.BlockSpec(segment_ids.shape, lambda i, *_: (0, 0)),
                *([FAR] * (aliased + 3)),
            ],
            out_specs=(
                pl.BlockSpec((tokens, heads * VHEAD), lambda i, *_: (0, part)),
                pl.BlockSpec((8, 128), lambda i, *_: (0, 0)),
            ),
            scratch_shapes=[
                pltpu.VMEM((min(slow + tokens, length), WIDTH), jnp.bfloat16),
                pltpu.VMEM((heads, tokens, LAT), jnp.bfloat16),
                pltpu.VMEM((heads, LAT, VHEAD), jnp.bfloat16),
                pltpu.VMEM((blocks, heads * TOK, WIDTH), jnp.bfloat16),
                pltpu.SemaphoreType.DMA,
                pltpu.SemaphoreType.DMA((blocks,)),
                pltpu.SemaphoreType.DMA,
            ],
        ),
        out_shape=(
            jax.ShapeDtypeStruct((tokens, parts * heads * VHEAD), jnp.bfloat16),
            jax.ShapeDtypeStruct((8, 128), jnp.int32),
        ),
        input_output_aliases={5: 0} if aliased else {},
        cost_estimate=pl.CostEstimate(
            flops=2 * tokens * heads * (fast * (WIDTH + LAT) + LAT * VHEAD),
            bytes_accessed=2 * heads * (tokens * (WIDTH + VHEAD) + LAT * VHEAD),
            transcendentals=tokens * heads * fast,
        ),
        compiler_params=pltpu.CompilerParams(vmem_limit_bytes=61 * MIB),
    )(*args)


def decode_kernel(info_ref, assign_ref, seg_ref, *refs, count, spans, docs, steps, group):
    pieces = refs[:count]
    packs = refs[count : count + spans]
    ak_hbm, av_hbm, o_ref, keys_hbm, kbuf, qa, pack_ref, ak_ref, av_ref, ksem, sems = refs[
        count + spans :
    ]
    seq_idx = info_ref[0]
    span_idx = info_ref[1]
    near = steps * docs
    rows = near * group
    copies = gather_copies(pieces, kbuf, ksem, seq_idx)
    own = pl.ds(seq_idx * group, group)
    early = [
        pltpu.make_async_copy(pack, pack_ref.at[pl.ds(i * near, near)], sems.at[i])
        for i, pack in enumerate(packs)
    ]
    early.append(pltpu.make_async_copy(ak_hbm.at[own], ak_ref, sems.at[spans]))
    late = pltpu.make_async_copy(av_hbm.at[own], av_ref, sems.at[spans + 1])
    for copy in (*early, *copies, late):
        copy.start()
    row = lax.broadcasted_iota(jnp.int32, (near, 1), 0)
    want = jnp.zeros((near, 1), jnp.int32)
    for d in range(docs):
        want = jnp.where(lax.rem(row, docs) == d, assign_ref[span_idx * docs + d], want)
    want = want * steps
    step = row // docs
    lane = lax.broadcasted_iota(jnp.int32, (1, spans * near), 1)
    place = lax.rem(lane, near)
    owner = lax.rem(span_idx - lane // near + spans, spans)
    number = (owner * docs + lax.rem(place, docs)) * steps + place // docs
    pick = jnp.where(number == want + step, 1.0, 0.0).astype(jnp.bfloat16)
    wide = group * NOPE
    for copy in early:
        copy.wait()
    pack = pack_ref[...]
    nope = jnp.dot(pick, pack[:, :wide], preferred_element_type=jnp.float32).astype(jnp.bfloat16)
    rope = jnp.dot(
        pick, pack[:, wide + LAT : wide + LAT + group * ROPE], preferred_element_type=jnp.float32
    ).astype(jnp.bfloat16)
    fresh = jnp.concatenate(
        [pack[:, wide : wide + LAT], pack[:, wide + LAT + group * ROPE :]], axis=1
    )
    for h in range(group):
        lat = jnp.dot(
            nope[:, h * NOPE : (h + 1) * NOPE], ak_ref[h], preferred_element_type=jnp.float32
        )
        qa[pl.ds(h * near, near), :LAT] = lat.astype(jnp.bfloat16)
        part = rope[:, h * ROPE : (h + 1) * ROPE]
        qa[pl.ds(h * near, near), LAT:] = jnp.concatenate([part, jnp.zeros_like(part)], axis=1)
    for copy in copies:
        copy.wait()
    handed = pltpu.make_async_copy(kbuf, keys_hbm, sems.at[spans + 2])
    handed.start()
    keys = kbuf[...]
    seg = seg_ref[pl.ds(span_idx, 1), :]
    old_bias = jnp.where(seg == lax.rem(row, docs), 0.0, NEG)[None]
    new_bias = jnp.where((number >= want) & (number <= want + step), 0.0, NEG)[None]
    query = qa[...]
    old = lax.dot_general(query, keys, NT, preferred_element_type=jnp.float32)
    old = (old.reshape(group, near, -1) + old_bias).reshape(rows, -1)
    new = lax.dot_general(query, fresh, NT, preferred_element_type=jnp.float32)
    new = (new.reshape(group, near, -1) + new_bias).reshape(rows, -1)
    m = jnp.maximum(jnp.max(old, axis=1, keepdims=True), jnp.max(new, axis=1, keepdims=True))
    old = jnp.exp2((old - m) * SCALE2)
    new = jnp.exp2((new - m) * SCALE2)
    den = jnp.sum(old, axis=1, keepdims=True) + jnp.sum(new, axis=1, keepdims=True)
    o = jnp.dot(old.astype(jnp.bfloat16), keys[:, :LAT], preferred_element_type=jnp.float32)
    o = o + jnp.dot(new.astype(jnp.bfloat16), fresh[:, :LAT], preferred_element_type=jnp.float32)
    o = o * (1.0 / den)
    high = o.astype(jnp.bfloat16)
    low = (o - high.astype(jnp.float32)).astype(jnp.bfloat16)
    late.wait()
    for h in range(group):
        both = jnp.concatenate(
            [high[h * near : (h + 1) * near], low[h * near : (h + 1) * near]], axis=0
        )
        r = jnp.dot(both, av_ref[h], preferred_element_type=jnp.float32)
        o_ref[:, h * VHEAD : (h + 1) * VHEAD] = (r[:near] + r[near:]).astype(jnp.bfloat16)
    handed.wait()


def attend_decode(info, assignment, segment_ids, pieces, packs, absorb_key, absorb_value, steps):
    near, size = packs[0].shape
    docs = near // steps
    count, spans = len(pieces), len(packs)
    tokens = pieces[0].shape[0]
    heads = absorb_key.shape[0]
    group = heads // count
    rows = near * group
    length = count * tokens
    return pl.pallas_call(
        functools.partial(
            decode_kernel, count=count, spans=spans, docs=docs, steps=steps, group=group
        ),
        grid_spec=pltpu.PrefetchScalarGridSpec(
            num_scalar_prefetch=2,
            grid=(1,),
            in_specs=[
                pl.BlockSpec(segment_ids.shape, lambda i, *_: (0, 0)),
                *([ANY] * (count + spans)),
                *([FAR] * 2),
            ],
            out_specs=(pl.BlockSpec((near, group * VHEAD), lambda i, *_: (0, 0)), FAR),
            scratch_shapes=[
                pltpu.VMEM((length, WIDTH), jnp.bfloat16),
                pltpu.VMEM((rows, WIDTH), jnp.bfloat16),
                pltpu.VMEM((spans * near, size), jnp.bfloat16),
                pltpu.VMEM((group, NOPE, LAT), jnp.bfloat16),
                pltpu.VMEM((group, LAT, VHEAD), jnp.bfloat16),
                pltpu.SemaphoreType.DMA((count,)),
                pltpu.SemaphoreType.DMA((spans + 3,)),
            ],
        ),
        out_shape=(
            jax.ShapeDtypeStruct((near, group * VHEAD), jnp.bfloat16),
            jax.ShapeDtypeStruct((length, WIDTH), jnp.bfloat16),
        ),
        cost_estimate=pl.CostEstimate(
            flops=2 * rows * length * (WIDTH + LAT),
            bytes_accessed=2 * (length * WIDTH + group * LAT * VHEAD * 2),
            transcendentals=rows * length,
        ),
        compiler_params=pltpu.CompilerParams(vmem_limit_bytes=55 * MIB),
        name="attend_decode",
    )(info, assignment, segment_ids, *pieces, *packs, absorb_key, absorb_value)


def select_kernel(info_ref, assign_ref, *refs, spans, docs, steps):
    parts = refs[:spans]
    o_ref, value, sems = refs[spans:]
    span_idx = info_ref[1]
    near = steps * docs
    copies = [
        pltpu.make_async_copy(part, value.at[pl.ds(i * near, near)], sems.at[i])
        for i, part in enumerate(parts)
    ]
    for copy in copies:
        copy.start()
    lane = lax.broadcasted_iota(jnp.int32, (1, spans * near), 1)
    number = jnp.zeros((1, spans * near), jnp.int32)
    for j in range(spans):
        source = lax.rem(span_idx - j + spans, spans)
        for d in range(docs):
            here = (lane // near == j) & (lax.rem(lane, docs) == d)
            number = jnp.where(here, assign_ref[source * docs + d], number)
    number = number * steps + lax.rem(lane, near) // docs
    row = lax.broadcasted_iota(jnp.int32, (near, 1), 0)
    want = (span_idx * docs + lax.rem(row, docs)) * steps + row // docs
    pick = jnp.where(number == want, 1.0, 0.0).astype(jnp.bfloat16)
    for copy in copies:
        copy.wait()
    o_ref[...] = jnp.dot(pick, value[...], preferred_element_type=jnp.float32).astype(jnp.bfloat16)


def select_rows(info, assignment, parts, steps):
    near, size = parts[0].shape
    spans = len(parts)
    return pl.pallas_call(
        functools.partial(select_kernel, spans=spans, docs=near // steps, steps=steps),
        grid_spec=pltpu.PrefetchScalarGridSpec(
            num_scalar_prefetch=2,
            grid=(1,),
            in_specs=[ANY] * spans,
            out_specs=pl.BlockSpec((near, size), lambda i, *_: (0, 0)),
            scratch_shapes=[
                pltpu.VMEM((spans * near, size), jnp.bfloat16),
                pltpu.SemaphoreType.DMA((spans,)),
            ],
        ),
        out_shape=jax.ShapeDtypeStruct((near, size), jnp.bfloat16),
        compiler_params=pltpu.CompilerParams(vmem_limit_bytes=8 * MIB),
        name="select_rows",
    )(info, assignment, *parts)


def assemble_kernel(info_ref, *refs):
    parts, o_ref, sems = refs[:-2], refs[-2], refs[-1]
    _, size = parts[0].shape
    copies = []
    for i, part in enumerate(parts):
        start = pl.multiple_of(direct_source(i, info_ref[0], len(parts)) * size, 128)
        copies.append(pltpu.make_async_copy(part, o_ref.at[:, pl.ds(start, size)], sems.at[i]))
    for copy in copies:
        copy.start()
    for copy in copies:
        copy.wait()


def assemble(info, parts):
    near, size = parts[0].shape
    shape = (near, len(parts) * size)
    return pl.pallas_call(
        assemble_kernel,
        grid_spec=pltpu.PrefetchScalarGridSpec(
            num_scalar_prefetch=1,
            grid=(1,),
            in_specs=[ANY] * len(parts),
            out_specs=pl.BlockSpec(shape, lambda i, info: (0, 0)),
            scratch_shapes=[pltpu.SemaphoreType.DMA((len(parts),))],
        ),
        out_shape=jax.ShapeDtypeStruct(shape, jnp.bfloat16),
        compiler_params=pltpu.CompilerParams(vmem_limit_bytes=8 * MIB),
        name="assemble",
    )(info, *parts)


def spread_far(value, count):
    return [value] + [
        lax.ppermute(value, "seq", [(i, (i + 2 * k) % count) for i in range(count)])
        for k in range(1, count // 2)
    ]


def spread_near(pieces, count):
    swap = [(i, i ^ 1) for i in range(count)]
    return pieces + [lax.ppermute(p, "seq", swap) for p in pieces]


def spread(value, axis, count):
    return [value] + [
        lax.ppermute(value, axis, [(i, (i + k) % count) for i in range(count)])
        for k in range(1, count)
    ]


def body(
    q_prefill,
    kv_latent,
    key_rope,
    segment_ids,
    assignment,
    absorb_key,
    absorb_value,
    q_decode,
    new_latent,
    new_rope,
):
    steps, docs, heads, _ = q_decode.shape
    count = lax.axis_size("seq")
    spans = lax.axis_size("span")
    group = heads // count
    most = segment_ids.shape[1] // 2
    info = jnp.stack([lax.axis_index("seq"), lax.axis_index("span")]).astype(jnp.int32)

    cache, pack = prepare(
        info, kv_latent[0], key_rope[0].T, q_decode, new_latent, new_rope, group
    )
    pieces = spread_far(cache, count)
    packs = spread(pack, "span", spans)
    qa, token = absorb_prefill(q_prefill[0].transpose(1, 2, 0), absorb_key)
    far, token = lax.optimization_barrier((pieces[1:], token))
    pieces = spread_near([cache, *far], count)
    decoded, keys = attend_decode(
        info, assignment, segment_ids, pieces, packs, absorb_key, absorb_value, steps
    )
    returned = spread(decoded, "span", spans)
    out, token = attend_prefill(info, segment_ids, qa, keys, absorb_value, 0, PARTS, most)
    late, _ = lax.optimization_barrier((info, token))
    chosen = select_rows(late, assignment, returned, steps)
    finals = spread(chosen, "seq", count)
    for part in range(1, PARTS):
        out, _ = attend_prefill(
            info, segment_ids, qa, keys, absorb_value, part, PARTS, most, out
        )
    decode_out = assemble(info, finals)
    return (out[None], decode_out.reshape(steps, docs, heads * VHEAD))


def solution(mesh):
    in_specs = (
        P("span", "seq", None, None),
        P("span", "seq", None),
        P("span", "seq", None),
        P(),
        P(),
        P(),
        P(),
        P(None, "span", None, None),
        P(None, "span", None),
        P(None, "span", None),
    )
    out_specs = (P("span", "seq", None), P(None, "span", None))
    return jax.shard_map(body, mesh=mesh, in_specs=in_specs, out_specs=out_specs, check_vma=False)
```

```python
import functools
import math

import jax
import jax.numpy as jnp
from jax import lax
from jax.experimental import pallas as pl
from jax.experimental.pallas import tpu as pltpu
from jax.sharding import PartitionSpec as P


NOPE = 128
ROPE = 64
LAT = 512
VHEAD = 128
WIDTH = LAT + 2 * ROPE

NEG = -1e30
EPS = 1e-06
SCALE2 = (NOPE + ROPE) ** (-0.5) * math.log2(math.e)
TOK = 16
PARTS = 2
GROUP = 2
OUTS = 4
MIB = 1 << 20

NT = (((1,), (1,)), ((), ()))
FAR = pl.BlockSpec(memory_space=pltpu.HBM)
ANY = pl.BlockSpec(memory_space=pl.ANY)


def normed(values):
    values = values.astype(jnp.float32)
    mean = jnp.sum(values * values, axis=-1, keepdims=True) * (1.0 / values.shape[-1])
    return (values * lax.rsqrt(mean + EPS)).astype(jnp.bfloat16)


def prepare_kernel(info_ref, lat_ref, rope_ref, q_ref, nl_ref, nr_ref, cache_ref, pack_ref, *, group):
    steps, docs, block, _ = q_ref.shape
    cache_ref[:, :LAT] = normed(lat_ref[...])
    rope = jnp.transpose(rope_ref[...].astype(jnp.float32))
    rope = rope.astype(jnp.bfloat16)
    cache_ref[:, LAT:] = jnp.concatenate([rope, jnp.zeros_like(rope)], axis=1)
    wide = group * NOPE
    for t in range(steps):
        row = pl.ds(t * docs, docs)
        q = jnp.swapaxes(q_ref[t].astype(jnp.float32), 0, 1)
        part = q[:group]
        for k in range(1, block // group):
            chosen = lax.rem(info_ref[0], block // group) == k
            part = jnp.where(chosen, q[k * group : (k + 1) * group], part)
        part = part.astype(jnp.bfloat16)
        pack_ref[row, wide : wide + LAT] = normed(nl_ref[t])
        base = wide + LAT
        for h in range(group):
            pack_ref[row, h * NOPE : (h + 1) * NOPE] = part[h, :, :NOPE]
            pack_ref[row, base + h * ROPE : base + (h + 1) * ROPE] = part[h, :, NOPE:]
        rope = nr_ref[t]
        pack_ref[row, base + group * ROPE :] = jnp.concatenate([rope, jnp.zeros_like(rope)], axis=1)


def prepare(info, latent, rope, q_decode, new_latent, new_rope, group):
    tokens = latent.shape[0]
    steps, docs, _, size = q_decode.shape
    block = max(group, 8)
    ratio = block // group
    full = lambda x: pl.BlockSpec(x.shape, lambda i, info: (0,) * x.ndim)
    out_shape = (
        jax.ShapeDtypeStruct((tokens, WIDTH), jnp.bfloat16),
        jax.ShapeDtypeStruct((steps * docs, group * size + WIDTH), jnp.bfloat16),
    )
    return pl.pallas_call(
        functools.partial(prepare_kernel, group=group),
        grid_spec=pltpu.PrefetchScalarGridSpec(
            num_scalar_prefetch=1,
            grid=(1,),
            in_specs=[
                full(latent),
                full(rope),
                pl.BlockSpec((steps, docs, block, size), lambda i, info: (0, 0, info[0] // ratio, 0)),
                full(new_latent),
                full(new_rope),
            ],
            out_specs=tuple(full(s) for s in out_shape),
        ),
        out_shape=out_shape,
        compiler_params=pltpu.CompilerParams(vmem_limit_bytes=60 * MIB),
        name="prepare",
    )(info, latent, rope, q_decode, new_latent, new_rope)


def absorb_kernel(q_hbm, ak_hbm, o_hbm, q_buf, ak_buf, o_buf, q_sem, ak_sem, o_sem, *, group):
    heads, _, tokens = q_buf.shape
    number = heads // group

    def copies(i):
        part = pl.ds(i * group, group)
        return (
            pltpu.make_async_copy(q_hbm.at[part], q_buf.at[part], q_sem.at[i]),
            pltpu.make_async_copy(ak_hbm.at[part], ak_buf.at[part], ak_sem.at[i]),
        )

    def result(i):
        part = pl.ds(pl.multiple_of(i * group * TOK, group * TOK), group * TOK)
        return pltpu.make_async_copy(o_buf.at[:, part], o_hbm.at[:, part], o_sem.at[i])

    for i in range(number):
        for copy in copies(i):
            copy.start()

    @pl.loop(0, number)
    def _(i):
        for copy in copies(i):
            copy.wait()
        for j in range(group):
            h = i * group + j
            q = jnp.transpose(q_buf[h])
            lat = jnp.dot(q[:, :NOPE], ak_buf[h], preferred_element_type=jnp.float32)
            row = pl.ds(pl.multiple_of(h * TOK, TOK), TOK)
            o_buf[:, row, :LAT] = lat.astype(jnp.bfloat16).reshape(tokens // TOK, TOK, LAT)
            rope = jnp.concatenate([q[:, NOPE:], jnp.zeros_like(q[:, NOPE:])], axis=1)
            o_buf[:, row, LAT:] = rope.reshape(tokens // TOK, TOK, 2 * ROPE)
        result(i).start()

    for i in range(number):
        result(i).wait()


def absorb_prefill(q, absorb_key, group=8):
    heads, size, tokens = q.shape
    shape = (tokens // TOK, heads * TOK, WIDTH)
    return pl.pallas_call(
        functools.partial(absorb_kernel, group=group),
        in_specs=[FAR, FAR],
        out_specs=FAR,
        out_shape=jax.ShapeDtypeStruct(shape, jnp.bfloat16),
        scratch_shapes=[
            pltpu.VMEM(q.shape, jnp.bfloat16),
            pltpu.VMEM(absorb_key.shape, jnp.bfloat16),
            pltpu.VMEM(shape, jnp.bfloat16),
            pltpu.SemaphoreType.DMA((heads // group,)),
            pltpu.SemaphoreType.DMA((heads // group,)),
            pltpu.SemaphoreType.DMA((heads // group,)),
        ],
        cost_estimate=pl.CostEstimate(
            flops=2 * tokens * heads * NOPE * LAT,
            bytes_accessed=2 * heads * (tokens * (size + WIDTH) + NOPE * LAT),
            transcendentals=0,
        ),
        compiler_params=pltpu.CompilerParams(vmem_limit_bytes=61 * MIB),
        name="absorb_prefill",
    )(q, absorb_key)


def source_of(i, seq_idx, count):
    half = count // 2
    origin = seq_idx if i < half else seq_idx + 1 - 2 * lax.rem(seq_idx, 2)
    return lax.rem(origin - 2 * (i % half) + count, count)


def gather_copies(pieces, kbuf, sems, seq_idx):
    rows = pieces[0].shape[0]
    copies = []
    for i, piece in enumerate(pieces):
        start = pl.multiple_of(source_of(i, seq_idx, len(pieces)) * rows, TOK)
        copies.append(pltpu.make_async_copy(piece, kbuf.at[pl.ds(start, rows)], sems.at[i]))
    return copies


def prefill_kernel(
    info_ref, segs_ref, seg_hbm, qa_hbm, keys_hbm, *refs, part, fast, slow, heads, aliased
):
    refs = refs[1 if aliased else 0 :]
    av_hbm, o_hbm, kbuf, olat, av, qa_buf, seg_buf, o_buf, ksem, qsem, vsem, ssem, osem = refs
    blocks, rows, _ = qa_buf.shape
    tokens = olat.shape[1]
    held = kbuf.shape[0]
    length = keys_hbm.shape[0]
    seq_idx = info_ref[0]
    span_idx = info_ref[1]
    low = jnp.clip((seq_idx + 1) * tokens - held, 0, length - held)
    low = pl.multiple_of(low, TOK)
    keys_copy = pltpu.make_async_copy(keys_hbm.at[pl.ds(low, held)], kbuf, ksem)
    av_copy = pltpu.make_async_copy(av_hbm.at[pl.ds(part * heads, heads)], av, vsem)

    def qa_copy(i):
        return pltpu.make_async_copy(
            qa_hbm.at[i, pl.ds(part * rows, rows)], qa_buf.at[i], qsem.at[i]
        )

    ahead = min(2 * GROUP, blocks)
    seg_copy = pltpu.make_async_copy(seg_hbm, seg_buf, ssem)
    seg_copy.start()
    keys_copy.start()
    for i in range(ahead):
        qa_copy(i).start()
    seg_copy.wait()
    keys_copy.wait()
    seg = seg_buf[pl.ds(span_idx, 1), :]
    row = lax.broadcasted_iota(jnp.int32, (TOK, 1), 0)

    def base_of(tb):
        return seq_idx * tokens + tb * TOK

    def attend(window, tbs):
        staged = []
        for tb in tbs:
            base = base_of(tb)
            begin = jnp.clip(base + TOK - window, 0, length - window)
            seg_q = jnp.zeros((TOK, 1), jnp.int32)
            for i in range(TOK):
                seg_q = jnp.where(row == i, segs_ref[span_idx, base + i], seg_q)
            start = jnp.sum((seg < seg_q).astype(jnp.int32), axis=1, keepdims=True)
            pos_k = begin + lax.broadcasted_iota(jnp.int32, (TOK, window), 1)
            keep = (pos_k >= start) & (pos_k <= base + row)
            bias = jnp.where(keep, 0.0, NEG)[None]
            spot = pl.ds(pl.multiple_of(begin - low, TOK), window)
            s = lax.dot_general(qa_buf[tb], kbuf[spot, :], NT, preferred_element_type=jnp.float32)
            staged.append((tb, spot, bias, s))
        for tb, spot, bias, s in staged:
            s = (s.reshape(heads, TOK, window) + bias).reshape(rows, window)
            m = jnp.max(s, axis=1, keepdims=True)
            p = jnp.exp2((s - m) * SCALE2)
            den = jnp.sum(p, axis=1, keepdims=True)
            o = jnp.dot(
                p.astype(jnp.bfloat16), kbuf[spot, :LAT], preferred_element_type=jnp.float32
            )
            o = (o * (1.0 / den)).astype(jnp.bfloat16)
            place = pl.ds(pl.multiple_of(tb * TOK, TOK), TOK)
            olat[:, place, :] = o.reshape(heads, TOK, LAT)

    def reaches(tb):
        begin = jnp.clip(base_of(tb) + TOK - fast, 0, length - fast)
        ahead_seg = segs_ref[span_idx, jnp.maximum(begin - 1, 0)]
        return (begin > 0) & (ahead_seg == segs_ref[span_idx, base_of(tb)])

    @pl.loop(0, blocks // GROUP)
    def _(step):
        tbs = [step * GROUP + k for k in range(GROUP)]
        for tb in tbs:
            qa_copy(tb).wait()

            @pl.when(tb + ahead < blocks)
            def _():
                qa_copy(tb + ahead).start()

        @pl.when(step == blocks // GROUP // 2)
        def _():
            av_copy.start()

        far = [reaches(tb) for tb in tbs]
        any_far = functools.reduce(jnp.logical_or, far)

        @pl.when(jnp.logical_not(any_far))
        def _():
            attend(fast, tbs)

        @pl.when(any_far)
        def _():
            @pl.loop(0, GROUP)
            def _(k):
                attend(slow, [step * GROUP + k])

    av_copy.wait()
    batch = heads // OUTS
    results = []
    for i in range(OUTS):
        for h in range(i * batch, (i + 1) * batch):
            r = jnp.dot(olat[h], av[h], preferred_element_type=jnp.float32)
            o_buf[:, h * VHEAD : (h + 1) * VHEAD] = r.astype(jnp.bfloat16)
        source = pl.ds(i * batch * VHEAD, batch * VHEAD)
        target = pl.ds((part * heads + i * batch) * VHEAD, batch * VHEAD)
        results.append(
            pltpu.make_async_copy(o_buf.at[:, source], o_hbm.at[:, target], osem.at[i])
        )
        results[-1].start()
    for result in results:
        result.wait()


def attend_prefill(info, segment_ids, qa, keys, absorb_value, part, parts, most, out=None):
    blocks, rows, _ = qa.shape
    tokens = blocks * TOK
    heads = rows // TOK // parts
    length = keys.shape[0]
    fast = min(most, length)
    slow = min(most + 128, length)
    aliased = out is not None
    args = [info, segment_ids, segment_ids, qa, keys, *([out] if aliased else []), absorb_value]
    return pl.pallas_call(
        functools.partial(
            prefill_kernel,
            part=part,
            fast=fast,
            slow=slow,
            heads=heads,
            aliased=aliased,
        ),
        grid_spec=pltpu.PrefetchScalarGridSpec(
            num_scalar_prefetch=2,
            grid=(1,),
            in_specs=[
                *([FAR] * (aliased + 4)),
            ],
            out_specs=FAR,
            scratch_shapes=[
                pltpu.VMEM((min(slow + tokens, length), WIDTH), jnp.bfloat16),
                pltpu.VMEM((heads, tokens, LAT), jnp.bfloat16),
                pltpu.VMEM((heads, LAT, VHEAD), jnp.bfloat16),
                pltpu.VMEM((blocks, heads * TOK, WIDTH), jnp.bfloat16),
                pltpu.VMEM(segment_ids.shape, jnp.int32),
                pltpu.VMEM((tokens, heads * VHEAD), jnp.bfloat16),
                pltpu.SemaphoreType.DMA,
                pltpu.SemaphoreType.DMA((blocks,)),
                pltpu.SemaphoreType.DMA,
                pltpu.SemaphoreType.DMA,
                pltpu.SemaphoreType.DMA((OUTS,)),
            ],
        ),
        out_shape=jax.ShapeDtypeStruct((tokens, parts * heads * VHEAD), jnp.bfloat16),
        input_output_aliases={5: 0} if aliased else {},
        cost_estimate=pl.CostEstimate(
            flops=2 * tokens * heads * (fast * (WIDTH + LAT) + LAT * VHEAD),
            bytes_accessed=2 * heads * (tokens * (WIDTH + VHEAD) + LAT * VHEAD),
            transcendentals=tokens * heads * fast,
        ),
        compiler_params=pltpu.CompilerParams(vmem_limit_bytes=61 * MIB),
    )(*args)


def decode_kernel(info_ref, assign_ref, seg_hbm, *refs, count, spans, docs, steps, group):
    pieces = refs[:count]
    packs = refs[count : count + spans]
    ak_hbm, av_hbm, o_ref, keys_hbm, kbuf, qa, pack_ref, ak_ref, av_ref, seg_ref, ksem, sems = refs[
        count + spans :
    ]
    seq_idx = info_ref[0]
    span_idx = info_ref[1]
    near = steps * docs
    rows = near * group
    copies = gather_copies(pieces, kbuf, ksem, seq_idx)
    own = pl.ds(seq_idx * group, group)
    early = [
        pltpu.make_async_copy(pack, pack_ref.at[pl.ds(i * near, near)], sems.at[i])
        for i, pack in enumerate(packs)
    ]
    early.append(pltpu.make_async_copy(ak_hbm.at[own], ak_ref, sems.at[spans]))
    early.append(pltpu.make_async_copy(seg_hbm, seg_ref, sems.at[spans + 3]))
    late = pltpu.make_async_copy(av_hbm.at[own], av_ref, sems.at[spans + 1])
    for copy in (*early, *copies, late):
        copy.start()
    row = lax.broadcasted_iota(jnp.int32, (near, 1), 0)
    want = jnp.zeros((near, 1), jnp.int32)
    for d in range(docs):
        want = jnp.where(lax.rem(row, docs) == d, assign_ref[span_idx * docs + d], want)
    want = want * steps
    step = row // docs
    lane = lax.broadcasted_iota(jnp.int32, (1, spans * near), 1)
    place = lax.rem(lane, near)
    owner = lax.rem(span_idx - lane // near + spans, spans)
    number = (owner * docs + lax.rem(place, docs)) * steps + place // docs
    pick = jnp.where(number == want + step, 1.0, 0.0).astype(jnp.bfloat16)
    wide = group * NOPE
    for copy in early:
        copy.wait()
    pack = pack_ref[...]
    nope = jnp.dot(pick, pack[:, :wide], preferred_element_type=jnp.float32).astype(jnp.bfloat16)
    rope = jnp.dot(
        pick, pack[:, wide + LAT : wide + LAT + group * ROPE], preferred_element_type=jnp.float32
    ).astype(jnp.bfloat16)
    fresh = jnp.concatenate(
        [pack[:, wide : wide + LAT], pack[:, wide + LAT + group * ROPE :]], axis=1
    )
    for h in range(group):
        lat = jnp.dot(
            nope[:, h * NOPE : (h + 1) * NOPE], ak_ref[h], preferred_element_type=jnp.float32
        )
        qa[pl.ds(h * near, near), :LAT] = lat.astype(jnp.bfloat16)
        part = rope[:, h * ROPE : (h + 1) * ROPE]
        qa[pl.ds(h * near, near), LAT:] = jnp.concatenate([part, jnp.zeros_like(part)], axis=1)
    for copy in copies:
        copy.wait()
    handed = pltpu.make_async_copy(kbuf, keys_hbm, sems.at[spans + 2])
    handed.start()
    keys = kbuf[...]
    seg = seg_ref[pl.ds(span_idx, 1), :]
    old_bias = jnp.where(seg == lax.rem(row, docs), 0.0, NEG)[None]
    new_bias = jnp.where((number >= want) & (number <= want + step), 0.0, NEG)[None]
    query = qa[...]
    old = lax.dot_general(query, keys, NT, preferred_element_type=jnp.float32)
    old = (old.reshape(group, near, -1) + old_bias).reshape(rows, -1)
    new = lax.dot_general(query, fresh, NT, preferred_element_type=jnp.float32)
    new = (new.reshape(group, near, -1) + new_bias).reshape(rows, -1)
    m = jnp.maximum(jnp.max(old, axis=1, keepdims=True), jnp.max(new, axis=1, keepdims=True))
    old = jnp.exp2((old - m) * SCALE2)
    new = jnp.exp2((new - m) * SCALE2)
    den = jnp.sum(old, axis=1, keepdims=True) + jnp.sum(new, axis=1, keepdims=True)
    o = jnp.dot(old.astype(jnp.bfloat16), keys[:, :LAT], preferred_element_type=jnp.float32)
    o = o + jnp.dot(new.astype(jnp.bfloat16), fresh[:, :LAT], preferred_element_type=jnp.float32)
    o = o * (1.0 / den)
    high = o.astype(jnp.bfloat16)
    low = (o - high.astype(jnp.float32)).astype(jnp.bfloat16)
    late.wait()
    for h in range(group):
        both = jnp.concatenate(
            [high[h * near : (h + 1) * near], low[h * near : (h + 1) * near]], axis=0
        )
        r = jnp.dot(both, av_ref[h], preferred_element_type=jnp.float32)
        o_ref[:, h * VHEAD : (h + 1) * VHEAD] = (r[:near] + r[near:]).astype(jnp.bfloat16)
    handed.wait()


def attend_decode(info, assignment, segment_ids, pieces, packs, absorb_key, absorb_value, steps):
    near, size = packs[0].shape
    docs = near // steps
    count, spans = len(pieces), len(packs)
    tokens = pieces[0].shape[0]
    heads = absorb_key.shape[0]
    group = heads // count
    rows = near * group
    length = count * tokens
    return pl.pallas_call(
        functools.partial(
            decode_kernel, count=count, spans=spans, docs=docs, steps=steps, group=group
        ),
        grid_spec=pltpu.PrefetchScalarGridSpec(
            num_scalar_prefetch=2,
            grid=(1,),
            in_specs=[
                FAR,
                *([ANY] * (count + spans)),
                *([FAR] * 2),
            ],
            out_specs=(pl.BlockSpec((near, group * VHEAD), lambda i, *_: (0, 0)), FAR),
            scratch_shapes=[
                pltpu.VMEM((length, WIDTH), jnp.bfloat16),
                pltpu.VMEM((rows, WIDTH), jnp.bfloat16),
                pltpu.VMEM((spans * near, size), jnp.bfloat16),
                pltpu.VMEM((group, NOPE, LAT), jnp.bfloat16),
                pltpu.VMEM((group, LAT, VHEAD), jnp.bfloat16),
                pltpu.VMEM(segment_ids.shape, jnp.int32),
                pltpu.SemaphoreType.DMA((count,)),
                pltpu.SemaphoreType.DMA((spans + 4,)),
            ],
        ),
        out_shape=(
            jax.ShapeDtypeStruct((near, group * VHEAD), jnp.bfloat16),
            jax.ShapeDtypeStruct((length, WIDTH), jnp.bfloat16),
        ),
        cost_estimate=pl.CostEstimate(
            flops=2 * rows * length * (WIDTH + LAT),
            bytes_accessed=2 * (length * WIDTH + group * LAT * VHEAD * 2),
            transcendentals=rows * length,
        ),
        compiler_params=pltpu.CompilerParams(vmem_limit_bytes=55 * MIB),
        name="attend_decode",
    )(info, assignment, segment_ids, *pieces, *packs, absorb_key, absorb_value)


def select_kernel(info_ref, assign_ref, *refs, spans, docs, steps):
    parts = refs[:spans]
    o_ref, value, sems = refs[spans:]
    span_idx = info_ref[1]
    near = steps * docs
    copies = [
        pltpu.make_async_copy(part, value.at[pl.ds(i * near, near)], sems.at[i])
        for i, part in enumerate(parts)
    ]
    for copy in copies:
        copy.start()
    lane = lax.broadcasted_iota(jnp.int32, (1, spans * near), 1)
    number = jnp.zeros((1, spans * near), jnp.int32)
    for j in range(spans):
        source = lax.rem(span_idx - j + spans, spans)
        for d in range(docs):
            here = (lane // near == j) & (lax.rem(lane, docs) == d)
            number = jnp.where(here, assign_ref[source * docs + d], number)
    number = number * steps + lax.rem(lane, near) // docs
    row = lax.broadcasted_iota(jnp.int32, (near, 1), 0)
    want = (span_idx * docs + lax.rem(row, docs)) * steps + row // docs
    pick = jnp.where(number == want, 1.0, 0.0).astype(jnp.bfloat16)
    for copy in copies:
        copy.wait()
    o_ref[...] = jnp.dot(pick, value[...], preferred_element_type=jnp.float32).astype(jnp.bfloat16)


def select_rows(info, assignment, parts, steps):
    near, size = parts[0].shape
    spans = len(parts)
    return pl.pallas_call(
        functools.partial(select_kernel, spans=spans, docs=near // steps, steps=steps),
        grid_spec=pltpu.PrefetchScalarGridSpec(
            num_scalar_prefetch=2,
            grid=(1,),
            in_specs=[ANY] * spans,
            out_specs=pl.BlockSpec((near, size), lambda i, *_: (0, 0)),
            scratch_shapes=[
                pltpu.VMEM((spans * near, size), jnp.bfloat16),
                pltpu.SemaphoreType.DMA((spans,)),
            ],
        ),
        out_shape=jax.ShapeDtypeStruct((near, size), jnp.bfloat16),
        compiler_params=pltpu.CompilerParams(vmem_limit_bytes=8 * MIB),
        name="select_rows",
    )(info, assignment, *parts)


def assemble_kernel(info_ref, *refs):
    parts, o_ref, sems = refs[:-2], refs[-2], refs[-1]
    near = parts[0].shape[0] // 2
    size = parts[0].shape[1]
    seq_idx = info_ref[0]
    core = lax.rem(seq_idx, 2)
    copies = []
    for i, part in enumerate(parts):
        source = lax.rem(seq_idx - 2 * i + 2 * len(parts), 2 * len(parts))
        for k in range(2):
            owner = source if k == 0 else source + 1 - 2 * core
            start = pl.multiple_of(owner * size, 128)
            copies.append(
                pltpu.make_async_copy(
                    part.at[pl.ds(k * near, near)],
                    o_ref.at[:, pl.ds(start, size)],
                    sems.at[2 * i + k],
                )
            )
    for copy in copies:
        copy.start()
    for copy in copies:
        copy.wait()


def assemble(info, parts):
    near, size = parts[0].shape
    number = 2 * len(parts)
    shape = (near // 2, number * size)
    return pl.pallas_call(
        assemble_kernel,
        grid_spec=pltpu.PrefetchScalarGridSpec(
            num_scalar_prefetch=1,
            grid=(1,),
            in_specs=[ANY] * len(parts),
            out_specs=pl.BlockSpec(shape, lambda i, info: (0, 0)),
            scratch_shapes=[pltpu.SemaphoreType.DMA((number,))],
        ),
        out_shape=jax.ShapeDtypeStruct(shape, jnp.bfloat16),
        compiler_params=pltpu.CompilerParams(vmem_limit_bytes=8 * MIB),
        name="assemble",
    )(info, *parts)


def spread_far(value, count):
    return [value] + [
        lax.ppermute(value, "seq", [(i, (i + 2 * k) % count) for i in range(count)])
        for k in range(1, count // 2)
    ]


def spread_near(pieces, count):
    swap = [(i, i ^ 1) for i in range(count)]
    return pieces + [lax.ppermute(p, "seq", swap) for p in pieces]


def spread(value, axis, count):
    return [value] + [
        lax.ppermute(value, axis, [(i, (i + k) % count) for i in range(count)])
        for k in range(1, count)
    ]


def body(
    q_prefill,
    kv_latent,
    key_rope,
    segment_ids,
    assignment,
    absorb_key,
    absorb_value,
    q_decode,
    new_latent,
    new_rope,
):
    steps, docs, heads, _ = q_decode.shape
    count = lax.axis_size("seq")
    spans = lax.axis_size("span")
    group = heads // count
    most = segment_ids.shape[1] // 2
    info = jnp.stack([lax.axis_index("seq"), lax.axis_index("span")]).astype(jnp.int32)

    cache, pack = prepare(
        info, kv_latent[0], key_rope[0].T, q_decode, new_latent, new_rope, group
    )
    pieces = spread_far(cache, count)
    packs = spread(pack, "span", spans)
    qa = absorb_prefill(q_prefill[0].transpose(1, 2, 0), absorb_key)
    pieces = spread_near(pieces, count)
    decoded, keys = attend_decode(
        info, assignment, segment_ids, pieces, packs, absorb_key, absorb_value, steps
    )
    returned = spread(decoded, "span", spans)
    out = attend_prefill(info, segment_ids, qa, keys, absorb_value, 0, PARTS, most)
    chosen = select_rows(info, assignment, returned, steps)
    swapped = lax.ppermute(chosen, "seq", [(i, i ^ 1) for i in range(count)])
    both = jnp.concatenate([chosen, swapped], axis=0)
    finals = spread_far(both, count)
    for part in range(1, PARTS):
        out = attend_prefill(info, segment_ids, qa, keys, absorb_value, part, PARTS, most, out)
    decode_out = assemble(info, finals)
    return (out[None], decode_out.reshape(steps, docs, heads * VHEAD))


def solution(mesh):
    in_specs = (
        P("span", "seq", None, None),
        P("span", "seq", None),
        P("span", "seq", None),
        P(),
        P(),
        P(),
        P(),
        P(None, "span", None, None),
        P(None, "span", None),
        P(None, "span", None),
    )
    out_specs = (P("span", "seq", None), P(None, "span", None))
    return jax.shard_map(body, mesh=mesh, in_specs=in_specs, out_specs=out_specs, check_vma=False)
```

```python
import functools
import math

import jax
import jax.numpy as jnp
from jax import lax
from jax.experimental import pallas as pl
from jax.experimental.pallas import tpu as pltpu
from jax.sharding import PartitionSpec as P


NOPE = 128
ROPE = 64
LAT = 512
VHEAD = 128
WIDTH = LAT + 2 * ROPE

NEG = -1e30
EPS = 1e-06
SCALE2 = (NOPE + ROPE) ** (-0.5) * math.log2(math.e)
TOK = 16
PARTS = 2
GROUP = 2
OUTS = 4
MIB = 1 << 20

NT = (((1,), (1,)), ((), ()))
FAR = pl.BlockSpec(memory_space=pltpu.HBM)
ANY = pl.BlockSpec(memory_space=pl.ANY)


def normed(values):
    values = values.astype(jnp.float32)
    mean = jnp.sum(values * values, axis=-1, keepdims=True) * (1.0 / values.shape[-1])
    return (values * lax.rsqrt(mean + EPS)).astype(jnp.bfloat16)


def prepare_kernel(lat_ref, rope_ref, q_hbm, nl_ref, nr_ref, cache_ref, pack_ref, q_ref, sem, *, group):
    steps, docs, block, _ = q_ref.shape
    seq_idx = lax.axis_index("seq")
    ratio = block // group
    begin = pl.multiple_of(seq_idx // ratio * block, block)
    copy = pltpu.make_async_copy(q_hbm.at[:, :, pl.ds(begin, block)], q_ref, sem)
    copy.start()
    cache_ref[:, :LAT] = normed(lat_ref[...])
    rope = jnp.transpose(rope_ref[...].astype(jnp.float32))
    rope = rope.astype(jnp.bfloat16)
    cache_ref[:, LAT:] = jnp.concatenate([rope, jnp.zeros_like(rope)], axis=1)
    wide = group * NOPE
    base = wide + LAT
    for t in range(steps):
        row = pl.ds(t * docs, docs)
        pack_ref[row, wide : wide + LAT] = normed(nl_ref[t])
        rope = nr_ref[t]
        pack_ref[row, base + group * ROPE :] = jnp.concatenate([rope, jnp.zeros_like(rope)], axis=1)
    copy.wait()
    for t in range(steps):
        row = pl.ds(t * docs, docs)
        q = jnp.swapaxes(q_ref[t].astype(jnp.float32), 0, 1)
        part = q[:group]
        for k in range(1, ratio):
            chosen = lax.rem(seq_idx, ratio) == k
            part = jnp.where(chosen, q[k * group : (k + 1) * group], part)
        part = part.astype(jnp.bfloat16)
        for h in range(group):
            pack_ref[row, h * NOPE : (h + 1) * NOPE] = part[h, :, :NOPE]
            pack_ref[row, base + h * ROPE : base + (h + 1) * ROPE] = part[h, :, NOPE:]


def prepare(latent, rope, q_decode, new_latent, new_rope, group):
    tokens = latent.shape[0]
    steps, docs, _, size = q_decode.shape
    block = max(group, 8)
    full = lambda x: pl.BlockSpec(x.shape, lambda i: (0,) * len(x.shape))
    out_shape = (
        jax.ShapeDtypeStruct((tokens, WIDTH), jnp.bfloat16),
        jax.ShapeDtypeStruct((steps * docs, group * size + WIDTH), jnp.bfloat16),
    )
    return pl.pallas_call(
        functools.partial(prepare_kernel, group=group),
        grid=(1,),
        in_specs=[full(latent), full(rope), FAR, full(new_latent), full(new_rope)],
        out_specs=tuple(full(s) for s in out_shape),
        out_shape=out_shape,
        scratch_shapes=[
            pltpu.VMEM((steps, docs, block, size), jnp.bfloat16),
            pltpu.SemaphoreType.DMA,
        ],
        compiler_params=pltpu.CompilerParams(vmem_limit_bytes=60 * MIB),
        name="prepare",
    )(latent, rope, q_decode, new_latent, new_rope)


def absorb_kernel(q_hbm, ak_hbm, o_hbm, q_buf, ak_buf, o_buf, q_sem, ak_sem, o_sem, *, group):
    heads, _, tokens = q_buf.shape
    number = heads // group

    def copies(i):
        part = pl.ds(i * group, group)
        return (
            pltpu.make_async_copy(q_hbm.at[part], q_buf.at[part], q_sem.at[i]),
            pltpu.make_async_copy(ak_hbm.at[part], ak_buf.at[part], ak_sem.at[i]),
        )

    def result(i):
        part = pl.ds(pl.multiple_of(i * group * TOK, group * TOK), group * TOK)
        return pltpu.make_async_copy(o_buf.at[:, part], o_hbm.at[:, part], o_sem.at[i])

    for i in range(number):
        for copy in copies(i):
            copy.start()

    @pl.loop(0, number)
    def _(i):
        for copy in copies(i):
            copy.wait()
        for j in range(group):
            h = i * group + j
            q = jnp.transpose(q_buf[h])
            lat = jnp.dot(q[:, :NOPE], ak_buf[h], preferred_element_type=jnp.float32)
            row = pl.ds(pl.multiple_of(h * TOK, TOK), TOK)
            o_buf[:, row, :LAT] = lat.astype(jnp.bfloat16).reshape(tokens // TOK, TOK, LAT)
            rope = jnp.concatenate([q[:, NOPE:], jnp.zeros_like(q[:, NOPE:])], axis=1)
            o_buf[:, row, LAT:] = rope.reshape(tokens // TOK, TOK, 2 * ROPE)
        result(i).start()

    for i in range(number):
        result(i).wait()


def absorb_prefill(q, absorb_key, group=8):
    heads, size, tokens = q.shape
    shape = (tokens // TOK, heads * TOK, WIDTH)
    return pl.pallas_call(
        functools.partial(absorb_kernel, group=group),
        in_specs=[FAR, FAR],
        out_specs=FAR,
        out_shape=jax.ShapeDtypeStruct(shape, jnp.bfloat16),
        scratch_shapes=[
            pltpu.VMEM(q.shape, jnp.bfloat16),
            pltpu.VMEM(absorb_key.shape, jnp.bfloat16),
            pltpu.VMEM(shape, jnp.bfloat16),
            pltpu.SemaphoreType.DMA((heads // group,)),
            pltpu.SemaphoreType.DMA((heads // group,)),
            pltpu.SemaphoreType.DMA((heads // group,)),
        ],
        cost_estimate=pl.CostEstimate(
            flops=2 * tokens * heads * NOPE * LAT,
            bytes_accessed=2 * heads * (tokens * (size + WIDTH) + NOPE * LAT),
            transcendentals=0,
        ),
        compiler_params=pltpu.CompilerParams(vmem_limit_bytes=61 * MIB),
        name="absorb_prefill",
    )(q, absorb_key)


def source_of(i, seq_idx, count):
    half = count // 2
    origin = seq_idx if i < half else seq_idx + 1 - 2 * lax.rem(seq_idx, 2)
    return lax.rem(origin - 2 * (i % half) + count, count)


def gather_copies(pieces, kbuf, sems, seq_idx):
    rows = pieces[0].shape[0]
    copies = []
    for i, piece in enumerate(pieces):
        start = pl.multiple_of(source_of(i, seq_idx, len(pieces)) * rows, TOK)
        copies.append(pltpu.make_async_copy(piece, kbuf.at[pl.ds(start, rows)], sems.at[i]))
    return copies


def prefill_kernel(
    segs_ref, seg_hbm, qa_hbm, keys_hbm, *refs, part, fast, slow, heads, aliased
):
    refs = refs[1 if aliased else 0 :]
    av_hbm, o_hbm, kbuf, olat, av, qa_buf, seg_buf, o_buf, ksem, qsem, vsem, ssem, osem = refs
    blocks, rows, _ = qa_buf.shape
    tokens = olat.shape[1]
    held = kbuf.shape[0]
    length = keys_hbm.shape[0]
    seq_idx = lax.axis_index("seq")
    span_idx = lax.axis_index("span")
    low = jnp.clip((seq_idx + 1) * tokens - held, 0, length - held)
    low = pl.multiple_of(low, TOK)
    keys_copy = pltpu.make_async_copy(keys_hbm.at[pl.ds(low, held)], kbuf, ksem)
    av_copy = pltpu.make_async_copy(av_hbm.at[pl.ds(part * heads, heads)], av, vsem)

    def qa_copy(i):
        return pltpu.make_async_copy(
            qa_hbm.at[i, pl.ds(part * rows, rows)], qa_buf.at[i], qsem.at[i]
        )

    ahead = min(2 * GROUP, blocks)
    seg_copy = pltpu.make_async_copy(seg_hbm, seg_buf, ssem)
    seg_copy.start()
    keys_copy.start()
    for i in range(ahead):
        qa_copy(i).start()
    seg_copy.wait()
    keys_copy.wait()
    seg = seg_buf[pl.ds(span_idx, 1), :]
    row = lax.broadcasted_iota(jnp.int32, (TOK, 1), 0)

    def base_of(tb):
        return seq_idx * tokens + tb * TOK

    def attend(window, tbs):
        staged = []
        for tb in tbs:
            base = base_of(tb)
            begin = jnp.clip(base + TOK - window, 0, length - window)
            seg_q = jnp.zeros((TOK, 1), jnp.int32)
            for i in range(TOK):
                seg_q = jnp.where(row == i, segs_ref[span_idx, base + i], seg_q)
            start = jnp.sum((seg < seg_q).astype(jnp.int32), axis=1, keepdims=True)
            pos_k = begin + lax.broadcasted_iota(jnp.int32, (TOK, window), 1)
            keep = (pos_k >= start) & (pos_k <= base + row)
            bias = jnp.where(keep, 0.0, NEG)[None]
            spot = pl.ds(pl.multiple_of(begin - low, TOK), window)
            s = lax.dot_general(qa_buf[tb], kbuf[spot, :], NT, preferred_element_type=jnp.float32)
            staged.append((tb, spot, bias, s))
        for tb, spot, bias, s in staged:
            s = (s.reshape(heads, TOK, window) + bias).reshape(rows, window)
            m = jnp.max(s, axis=1, keepdims=True)
            p = jnp.exp2((s - m) * SCALE2)
            den = jnp.sum(p, axis=1, keepdims=True)
            o = jnp.dot(
                p.astype(jnp.bfloat16), kbuf[spot, :LAT], preferred_element_type=jnp.float32
            )
            o = (o * (1.0 / den)).astype(jnp.bfloat16)
            place = pl.ds(pl.multiple_of(tb * TOK, TOK), TOK)
            olat[:, place, :] = o.reshape(heads, TOK, LAT)

    def reaches(tb):
        begin = jnp.clip(base_of(tb) + TOK - fast, 0, length - fast)
        ahead_seg = segs_ref[span_idx, jnp.maximum(begin - 1, 0)]
        return (begin > 0) & (ahead_seg == segs_ref[span_idx, base_of(tb)])

    @pl.loop(0, blocks // GROUP)
    def _(step):
        tbs = [step * GROUP + k for k in range(GROUP)]
        for tb in tbs:
            qa_copy(tb).wait()

            @pl.when(tb + ahead < blocks)
            def _():
                qa_copy(tb + ahead).start()

        @pl.when(step == blocks // GROUP // 2)
        def _():
            av_copy.start()

        far = [reaches(tb) for tb in tbs]
        any_far = functools.reduce(jnp.logical_or, far)

        @pl.when(jnp.logical_not(any_far))
        def _():
            attend(fast, tbs)

        @pl.when(any_far)
        def _():
            @pl.loop(0, GROUP)
            def _(k):
                attend(slow, [step * GROUP + k])

    av_copy.wait()
    batch = heads // OUTS
    results = []
    for i in range(OUTS):
        for h in range(i * batch, (i + 1) * batch):
            r = jnp.dot(olat[h], av[h], preferred_element_type=jnp.float32)
            o_buf[:, h * VHEAD : (h + 1) * VHEAD] = r.astype(jnp.bfloat16)
        source = pl.ds(i * batch * VHEAD, batch * VHEAD)
        target = pl.ds((part * heads + i * batch) * VHEAD, batch * VHEAD)
        results.append(
            pltpu.make_async_copy(o_buf.at[:, source], o_hbm.at[:, target], osem.at[i])
        )
        results[-1].start()
    for result in results:
        result.wait()


def attend_prefill(segment_ids, qa, keys, absorb_value, part, parts, most, out=None):
    blocks, rows, _ = qa.shape
    tokens = blocks * TOK
    heads = rows // TOK // parts
    length = keys.shape[0]
    fast = min(most, length)
    slow = min(most + 128, length)
    aliased = out is not None
    args = [segment_ids, segment_ids, qa, keys, *([out] if aliased else []), absorb_value]
    return pl.pallas_call(
        functools.partial(
            prefill_kernel,
            part=part,
            fast=fast,
            slow=slow,
            heads=heads,
            aliased=aliased,
        ),
        grid_spec=pltpu.PrefetchScalarGridSpec(
            num_scalar_prefetch=1,
            grid=(1,),
            in_specs=[
                *([FAR] * (aliased + 4)),
            ],
            out_specs=FAR,
            scratch_shapes=[
                pltpu.VMEM((min(slow + tokens, length), WIDTH), jnp.bfloat16),
                pltpu.VMEM((heads, tokens, LAT), jnp.bfloat16),
                pltpu.VMEM((heads, LAT, VHEAD), jnp.bfloat16),
                pltpu.VMEM((blocks, heads * TOK, WIDTH), jnp.bfloat16),
                pltpu.VMEM(segment_ids.shape, jnp.int32),
                pltpu.VMEM((tokens, heads * VHEAD), jnp.bfloat16),
                pltpu.SemaphoreType.DMA,
                pltpu.SemaphoreType.DMA((blocks,)),
                pltpu.SemaphoreType.DMA,
                pltpu.SemaphoreType.DMA,
                pltpu.SemaphoreType.DMA((OUTS,)),
            ],
        ),
        out_shape=jax.ShapeDtypeStruct((tokens, parts * heads * VHEAD), jnp.bfloat16),
        input_output_aliases={4: 0} if aliased else {},
        cost_estimate=pl.CostEstimate(
            flops=2 * tokens * heads * (fast * (WIDTH + LAT) + LAT * VHEAD),
            bytes_accessed=2 * heads * (tokens * (WIDTH + VHEAD) + LAT * VHEAD),
            transcendentals=tokens * heads * fast,
        ),
        compiler_params=pltpu.CompilerParams(vmem_limit_bytes=61 * MIB),
    )(*args)


def decode_kernel(assign_ref, seg_hbm, *refs, count, spans, docs, steps, group):
    pieces = refs[:count]
    packs = refs[count : count + spans]
    ak_hbm, av_hbm, o_ref, keys_hbm, kbuf, qa, pack_ref, ak_ref, av_ref, seg_ref, ksem, sems = refs[
        count + spans :
    ]
    seq_idx = lax.axis_index("seq")
    span_idx = lax.axis_index("span")
    near = steps * docs
    rows = near * group
    copies = gather_copies(pieces, kbuf, ksem, seq_idx)
    own = pl.ds(seq_idx * group, group)
    early = [
        pltpu.make_async_copy(pack, pack_ref.at[pl.ds(i * near, near)], sems.at[i])
        for i, pack in enumerate(packs)
    ]
    early.append(pltpu.make_async_copy(ak_hbm.at[own], ak_ref, sems.at[spans]))
    early.append(pltpu.make_async_copy(seg_hbm, seg_ref, sems.at[spans + 3]))
    late = pltpu.make_async_copy(av_hbm.at[own], av_ref, sems.at[spans + 1])
    for copy in (*early, *copies, late):
        copy.start()
    row = lax.broadcasted_iota(jnp.int32, (near, 1), 0)
    want = jnp.zeros((near, 1), jnp.int32)
    for d in range(docs):
        want = jnp.where(lax.rem(row, docs) == d, assign_ref[span_idx * docs + d], want)
    want = want * steps
    step = row // docs
    lane = lax.broadcasted_iota(jnp.int32, (1, spans * near), 1)
    place = lax.rem(lane, near)
    owner = lax.rem(span_idx - lane // near + spans, spans)
    number = (owner * docs + lax.rem(place, docs)) * steps + place // docs
    pick = jnp.where(number == want + step, 1.0, 0.0).astype(jnp.bfloat16)
    wide = group * NOPE
    for copy in early:
        copy.wait()
    pack = pack_ref[...]
    nope = jnp.dot(pick, pack[:, :wide], preferred_element_type=jnp.float32).astype(jnp.bfloat16)
    rope = jnp.dot(
        pick, pack[:, wide + LAT : wide + LAT + group * ROPE], preferred_element_type=jnp.float32
    ).astype(jnp.bfloat16)
    fresh = jnp.concatenate(
        [pack[:, wide : wide + LAT], pack[:, wide + LAT + group * ROPE :]], axis=1
    )
    for h in range(group):
        lat = jnp.dot(
            nope[:, h * NOPE : (h + 1) * NOPE], ak_ref[h], preferred_element_type=jnp.float32
        )
        qa[pl.ds(h * near, near), :LAT] = lat.astype(jnp.bfloat16)
        part = rope[:, h * ROPE : (h + 1) * ROPE]
        qa[pl.ds(h * near, near), LAT:] = jnp.concatenate([part, jnp.zeros_like(part)], axis=1)
    for copy in copies:
        copy.wait()
    handed = pltpu.make_async_copy(kbuf, keys_hbm, sems.at[spans + 2])
    handed.start()
    keys = kbuf[...]
    seg = seg_ref[pl.ds(span_idx, 1), :]
    old_bias = jnp.where(seg == lax.rem(row, docs), 0.0, NEG)[None]
    new_bias = jnp.where((number >= want) & (number <= want + step), 0.0, NEG)[None]
    query = qa[...]
    old = lax.dot_general(query, keys, NT, preferred_element_type=jnp.float32)
    old = (old.reshape(group, near, -1) + old_bias).reshape(rows, -1)
    new = lax.dot_general(query, fresh, NT, preferred_element_type=jnp.float32)
    new = (new.reshape(group, near, -1) + new_bias).reshape(rows, -1)
    m = jnp.maximum(jnp.max(old, axis=1, keepdims=True), jnp.max(new, axis=1, keepdims=True))
    old = jnp.exp2((old - m) * SCALE2)
    new = jnp.exp2((new - m) * SCALE2)
    den = jnp.sum(old, axis=1, keepdims=True) + jnp.sum(new, axis=1, keepdims=True)
    o = jnp.dot(old.astype(jnp.bfloat16), keys[:, :LAT], preferred_element_type=jnp.float32)
    o = o + jnp.dot(new.astype(jnp.bfloat16), fresh[:, :LAT], preferred_element_type=jnp.float32)
    o = o * (1.0 / den)
    high = o.astype(jnp.bfloat16)
    low = (o - high.astype(jnp.float32)).astype(jnp.bfloat16)
    late.wait()
    for h in range(group):
        both = jnp.concatenate(
            [high[h * near : (h + 1) * near], low[h * near : (h + 1) * near]], axis=0
        )
        r = jnp.dot(both, av_ref[h], preferred_element_type=jnp.float32)
        o_ref[:, h * VHEAD : (h + 1) * VHEAD] = (r[:near] + r[near:]).astype(jnp.bfloat16)
    handed.wait()


def attend_decode(assignment, segment_ids, pieces, packs, absorb_key, absorb_value, steps):
    near, size = packs[0].shape
    docs = near // steps
    count, spans = len(pieces), len(packs)
    tokens = pieces[0].shape[0]
    heads = absorb_key.shape[0]
    group = heads // count
    rows = near * group
    length = count * tokens
    return pl.pallas_call(
        functools.partial(
            decode_kernel, count=count, spans=spans, docs=docs, steps=steps, group=group
        ),
        grid_spec=pltpu.PrefetchScalarGridSpec(
            num_scalar_prefetch=1,
            grid=(1,),
            in_specs=[
                FAR,
                *([ANY] * (count + spans)),
                *([FAR] * 2),
            ],
            out_specs=(pl.BlockSpec((near, group * VHEAD), lambda i, *_: (0, 0)), FAR),
            scratch_shapes=[
                pltpu.VMEM((length, WIDTH), jnp.bfloat16),
                pltpu.VMEM((rows, WIDTH), jnp.bfloat16),
                pltpu.VMEM((spans * near, size), jnp.bfloat16),
                pltpu.VMEM((group, NOPE, LAT), jnp.bfloat16),
                pltpu.VMEM((group, LAT, VHEAD), jnp.bfloat16),
                pltpu.VMEM(segment_ids.shape, jnp.int32),
                pltpu.SemaphoreType.DMA((count,)),
                pltpu.SemaphoreType.DMA((spans + 4,)),
            ],
        ),
        out_shape=(
            jax.ShapeDtypeStruct((near, group * VHEAD), jnp.bfloat16),
            jax.ShapeDtypeStruct((length, WIDTH), jnp.bfloat16),
        ),
        cost_estimate=pl.CostEstimate(
            flops=2 * rows * length * (WIDTH + LAT),
            bytes_accessed=2 * (length * WIDTH + group * LAT * VHEAD * 2),
            transcendentals=rows * length,
        ),
        compiler_params=pltpu.CompilerParams(vmem_limit_bytes=52 * MIB),
        name="attend_decode",
    )(assignment, segment_ids, *pieces, *packs, absorb_key, absorb_value)


def select_kernel(assign_ref, *refs, spans, docs, steps):
    parts = refs[:spans]
    o_ref, value, sems = refs[spans:]
    span_idx = lax.axis_index("span")
    near = steps * docs
    copies = [
        pltpu.make_async_copy(part, value.at[pl.ds(i * near, near)], sems.at[i])
        for i, part in enumerate(parts)
    ]
    for copy in copies:
        copy.start()
    lane = lax.broadcasted_iota(jnp.int32, (1, spans * near), 1)
    number = jnp.zeros((1, spans * near), jnp.int32)
    for j in range(spans):
        source = lax.rem(span_idx - j + spans, spans)
        for d in range(docs):
            here = (lane // near == j) & (lax.rem(lane, docs) == d)
            number = jnp.where(here, assign_ref[source * docs + d], number)
    number = number * steps + lax.rem(lane, near) // docs
    row = lax.broadcasted_iota(jnp.int32, (near, 1), 0)
    want = (span_idx * docs + lax.rem(row, docs)) * steps + row // docs
    pick = jnp.where(number == want, 1.0, 0.0).astype(jnp.bfloat16)
    for copy in copies:
        copy.wait()
    o_ref[...] = jnp.dot(pick, value[...], preferred_element_type=jnp.float32).astype(jnp.bfloat16)


def select_rows(assignment, parts, steps):
    near, size = parts[0].shape
    spans = len(parts)
    return pl.pallas_call(
        functools.partial(select_kernel, spans=spans, docs=near // steps, steps=steps),
        grid_spec=pltpu.PrefetchScalarGridSpec(
            num_scalar_prefetch=1,
            grid=(1,),
            in_specs=[ANY] * spans,
            out_specs=pl.BlockSpec((near, size), lambda i, *_: (0, 0)),
            scratch_shapes=[
                pltpu.VMEM((spans * near, size), jnp.bfloat16),
                pltpu.SemaphoreType.DMA((spans,)),
            ],
        ),
        out_shape=jax.ShapeDtypeStruct((near, size), jnp.bfloat16),
        compiler_params=pltpu.CompilerParams(vmem_limit_bytes=8 * MIB),
        name="select_rows",
    )(assignment, *parts)


def assemble_kernel(*refs):
    parts, o_ref, sems = refs[:-2], refs[-2], refs[-1]
    near = parts[0].shape[0] // 2
    size = parts[0].shape[1]
    seq_idx = lax.axis_index("seq")
    core = lax.rem(seq_idx, 2)
    copies = []
    for i, part in enumerate(parts):
        source = lax.rem(seq_idx - 2 * i + 2 * len(parts), 2 * len(parts))
        for k in range(2):
            owner = source if k == 0 else source + 1 - 2 * core
            start = pl.multiple_of(owner * size, 128)
            copies.append(
                pltpu.make_async_copy(
                    part.at[pl.ds(k * near, near)],
                    o_ref.at[:, pl.ds(start, size)],
                    sems.at[2 * i + k],
                )
            )
    for copy in copies:
        copy.start()
    for copy in copies:
        copy.wait()


def assemble(parts):
    near, size = parts[0].shape
    number = 2 * len(parts)
    shape = (near // 2, number * size)
    return pl.pallas_call(
        assemble_kernel,
        grid_spec=pltpu.PrefetchScalarGridSpec(
            num_scalar_prefetch=0,
            grid=(1,),
            in_specs=[ANY] * len(parts),
            out_specs=pl.BlockSpec(shape, lambda i: (0, 0)),
            scratch_shapes=[pltpu.SemaphoreType.DMA((number,))],
        ),
        out_shape=jax.ShapeDtypeStruct(shape, jnp.bfloat16),
        compiler_params=pltpu.CompilerParams(vmem_limit_bytes=8 * MIB),
        name="assemble",
    )(*parts)


def spread_far(value, count):
    return [value] + [
        lax.ppermute(value, "seq", [(i, (i + 2 * k) % count) for i in range(count)])
        for k in range(1, count // 2)
    ]


def spread_near(pieces, count):
    swap = [(i, i ^ 1) for i in range(count)]
    return pieces + [lax.ppermute(p, "seq", swap) for p in pieces]


def spread(value, axis, count):
    return [value] + [
        lax.ppermute(value, axis, [(i, (i + k) % count) for i in range(count)])
        for k in range(1, count)
    ]


def body(
    q_prefill,
    kv_latent,
    key_rope,
    segment_ids,
    assignment,
    absorb_key,
    absorb_value,
    q_decode,
    new_latent,
    new_rope,
):
    steps, docs, heads, _ = q_decode.shape
    count = lax.axis_size("seq")
    spans = lax.axis_size("span")
    group = heads // count
    most = segment_ids.shape[1] // 2

    cache, pack = prepare(kv_latent[0], key_rope[0].T, q_decode, new_latent, new_rope, group)
    pieces = spread_far(cache, count)
    packs = spread(pack, "span", spans)
    qa = absorb_prefill(q_prefill[0].transpose(1, 2, 0), absorb_key)
    pieces = spread_near(pieces, count)
    decoded, keys = attend_decode(
        assignment, segment_ids, pieces, packs, absorb_key, absorb_value, steps
    )
    returned = spread(decoded, "span", spans)
    out = attend_prefill(segment_ids, qa, keys, absorb_value, 0, PARTS, most)
    chosen = select_rows(assignment, returned, steps)
    swapped = lax.ppermute(chosen, "seq", [(i, i ^ 1) for i in range(count)])
    both = jnp.concatenate([chosen, swapped], axis=0)
    finals = spread_far(both, count)
    for part in range(1, PARTS):
        out = attend_prefill(segment_ids, qa, keys, absorb_value, part, PARTS, most, out)
    decode_out = assemble(finals)
    return (out[None], decode_out.reshape(steps, docs, heads * VHEAD))


def solution(mesh):
    in_specs = (
        P("span", "seq", None, None),
        P("span", "seq", None),
        P("span", "seq", None),
        P(),
        P(),
        P(),
        P(),
        P(None, "span", None, None),
        P(None, "span", None),
        P(None, "span", None),
    )
    out_specs = (P("span", "seq", None), P(None, "span", None))
    return jax.shard_map(body, mesh=mesh, in_specs=in_specs, out_specs=out_specs, check_vma=False)
```

```python
import functools
import math

import jax
import jax.numpy as jnp
from jax import lax
from jax.experimental import pallas as pl
from jax.experimental.pallas import tpu as pltpu
from jax.sharding import PartitionSpec as P


NOPE = 128
ROPE = 64
LAT = 512
VHEAD = 128
WIDTH = LAT + 2 * ROPE

NEG = -1e30
EPS = 1e-06
SCALE2 = (NOPE + ROPE) ** (-0.5) * math.log2(math.e)
TOK = 16
PARTS = 2
GROUP = 2
OUTS = 4
MIB = 1 << 20

NT = (((1,), (1,)), ((), ()))
FAR = pl.BlockSpec(memory_space=pltpu.HBM)
ANY = pl.BlockSpec(memory_space=pl.ANY)


def normed(values):
    values = values.astype(jnp.float32)
    mean = jnp.sum(values * values, axis=-1, keepdims=True) * (1.0 / values.shape[-1])
    return (values * lax.rsqrt(mean + EPS)).astype(jnp.bfloat16)


def prepare_kernel(lat_ref, rope_ref, q_hbm, nl_ref, nr_ref, cache_ref, pack_ref, q_ref, sem, *, group):
    steps, docs, block, _ = q_ref.shape
    seq_idx = lax.axis_index("seq")
    ratio = block // group
    begin = pl.multiple_of(seq_idx // ratio * block, block)
    copy = pltpu.make_async_copy(q_hbm.at[:, :, pl.ds(begin, block)], q_ref, sem)
    copy.start()
    cache_ref[:, :LAT] = normed(lat_ref[...])
    rope = jnp.transpose(rope_ref[...].astype(jnp.float32))
    rope = rope.astype(jnp.bfloat16)
    cache_ref[:, LAT:] = jnp.concatenate([rope, jnp.zeros_like(rope)], axis=1)
    wide = group * NOPE
    base = wide + LAT
    for t in range(steps):
        row = pl.ds(t * docs, docs)
        pack_ref[row, wide : wide + LAT] = normed(nl_ref[t])
        rope = nr_ref[t]
        pack_ref[row, base + group * ROPE :] = jnp.concatenate([rope, jnp.zeros_like(rope)], axis=1)
    copy.wait()
    for t in range(steps):
        row = pl.ds(t * docs, docs)
        q = jnp.swapaxes(q_ref[t].astype(jnp.float32), 0, 1)
        part = q[:group]
        for k in range(1, ratio):
            chosen = lax.rem(seq_idx, ratio) == k
            part = jnp.where(chosen, q[k * group : (k + 1) * group], part)
        part = part.astype(jnp.bfloat16)
        for h in range(group):
            pack_ref[row, h * NOPE : (h + 1) * NOPE] = part[h, :, :NOPE]
            pack_ref[row, base + h * ROPE : base + (h + 1) * ROPE] = part[h, :, NOPE:]


def prepare(latent, rope, q_decode, new_latent, new_rope, group):
    tokens = latent.shape[0]
    steps, docs, _, size = q_decode.shape
    block = max(group, 8)
    full = lambda x: pl.BlockSpec(x.shape, lambda i: (0,) * len(x.shape))
    out_shape = (
        jax.ShapeDtypeStruct((tokens, WIDTH), jnp.bfloat16),
        jax.ShapeDtypeStruct((steps * docs, group * size + WIDTH), jnp.bfloat16),
    )
    return pl.pallas_call(
        functools.partial(prepare_kernel, group=group),
        grid=(1,),
        in_specs=[full(latent), full(rope), FAR, full(new_latent), full(new_rope)],
        out_specs=tuple(full(s) for s in out_shape),
        out_shape=out_shape,
        scratch_shapes=[
            pltpu.VMEM((steps, docs, block, size), jnp.bfloat16),
            pltpu.SemaphoreType.DMA,
        ],
        compiler_params=pltpu.CompilerParams(vmem_limit_bytes=60 * MIB),
        name="prepare",
    )(latent, rope, q_decode, new_latent, new_rope)


def absorb_kernel(q_hbm, ak_hbm, o_hbm, q_buf, ak_buf, o_buf, q_sem, ak_sem, o_sem, *, group):
    heads, _, tokens = q_buf.shape
    number = heads // group

    def copies(i):
        part = pl.ds(i * group, group)
        return (
            pltpu.make_async_copy(q_hbm.at[part], q_buf.at[part], q_sem.at[i]),
            pltpu.make_async_copy(ak_hbm.at[part], ak_buf.at[part], ak_sem.at[i]),
        )

    def result(i):
        part = pl.ds(pl.multiple_of(i * group * TOK, group * TOK), group * TOK)
        return pltpu.make_async_copy(o_buf.at[:, part], o_hbm.at[:, part], o_sem.at[i])

    for i in range(number):
        for copy in copies(i):
            copy.start()

    @pl.loop(0, number)
    def _(i):
        for copy in copies(i):
            copy.wait()
        for j in range(group):
            h = i * group + j
            q = jnp.transpose(q_buf[h])
            lat = jnp.dot(q[:, :NOPE], ak_buf[h], preferred_element_type=jnp.float32)
            row = pl.ds(pl.multiple_of(h * TOK, TOK), TOK)
            o_buf[:, row, :LAT] = lat.astype(jnp.bfloat16).reshape(tokens // TOK, TOK, LAT)
            rope = jnp.concatenate([q[:, NOPE:], jnp.zeros_like(q[:, NOPE:])], axis=1)
            o_buf[:, row, LAT:] = rope.reshape(tokens // TOK, TOK, 2 * ROPE)
        result(i).start()

    for i in range(number):
        result(i).wait()


def absorb_prefill(q, absorb_key, group=8):
    heads, size, tokens = q.shape
    shape = (tokens // TOK, heads * TOK, WIDTH)
    return pl.pallas_call(
        functools.partial(absorb_kernel, group=group),
        in_specs=[FAR, FAR],
        out_specs=FAR,
        out_shape=jax.ShapeDtypeStruct(shape, jnp.bfloat16),
        scratch_shapes=[
            pltpu.VMEM(q.shape, jnp.bfloat16),
            pltpu.VMEM(absorb_key.shape, jnp.bfloat16),
            pltpu.VMEM(shape, jnp.bfloat16),
            pltpu.SemaphoreType.DMA((heads // group,)),
            pltpu.SemaphoreType.DMA((heads // group,)),
            pltpu.SemaphoreType.DMA((heads // group,)),
        ],
        cost_estimate=pl.CostEstimate(
            flops=2 * tokens * heads * NOPE * LAT,
            bytes_accessed=2 * heads * (tokens * (size + WIDTH) + NOPE * LAT),
            transcendentals=0,
        ),
        compiler_params=pltpu.CompilerParams(vmem_limit_bytes=61 * MIB),
        name="absorb_prefill",
    )(q, absorb_key)


def source_of(i, seq_idx, count):
    half = count // 2
    origin = seq_idx if i < half else seq_idx + 1 - 2 * lax.rem(seq_idx, 2)
    return lax.rem(origin - 2 * (i % half) + count, count)


def gather_copies(pieces, kbuf, sems, seq_idx):
    rows = pieces[0].shape[0]
    copies = []
    for i, piece in enumerate(pieces):
        start = pl.multiple_of(source_of(i, seq_idx, len(pieces)) * rows, TOK)
        copies.append(pltpu.make_async_copy(piece, kbuf.at[pl.ds(start, rows)], sems.at[i]))
    return copies


def prefill_kernel(
    segs_ref, seg_hbm, qa_hbm, keys_hbm, *refs, part, fast, slow, heads, aliased
):
    refs = refs[1 if aliased else 0 :]
    av_hbm, o_hbm, kbuf, olat, av, qa_buf, seg_buf, o_buf, ksem, qsem, vsem, ssem, osem = refs
    blocks, rows, _ = qa_buf.shape
    tokens = olat.shape[1]
    held = kbuf.shape[0]
    length = keys_hbm.shape[0]
    seq_idx = lax.axis_index("seq")
    span_idx = lax.axis_index("span")
    low = jnp.clip((seq_idx + 1) * tokens - held, 0, length - held)
    low = pl.multiple_of(low, TOK)
    keys_copy = pltpu.make_async_copy(keys_hbm.at[pl.ds(low, held)], kbuf, ksem)
    av_copy = pltpu.make_async_copy(av_hbm.at[pl.ds(part * heads, heads)], av, vsem)

    def qa_copy(i):
        return pltpu.make_async_copy(
            qa_hbm.at[i, pl.ds(part * rows, rows)], qa_buf.at[i], qsem.at[i]
        )

    ahead = min(2 * GROUP, blocks)
    seg_copy = pltpu.make_async_copy(seg_hbm, seg_buf, ssem)
    seg_copy.start()
    keys_copy.start()
    for i in range(ahead):
        qa_copy(i).start()
    seg_copy.wait()
    keys_copy.wait()
    seg = seg_buf[pl.ds(span_idx, 1), :]
    row = lax.broadcasted_iota(jnp.int32, (TOK, 1), 0)

    def base_of(tb):
        return seq_idx * tokens + tb * TOK

    def attend(window, tbs):
        staged = []
        for tb in tbs:
            base = base_of(tb)
            begin = jnp.clip(base + TOK - window, 0, length - window)
            seg_q = jnp.zeros((TOK, 1), jnp.int32)
            for i in range(TOK):
                seg_q = jnp.where(row == i, segs_ref[span_idx, base + i], seg_q)
            start = jnp.sum((seg < seg_q).astype(jnp.int32), axis=1, keepdims=True)
            pos_k = begin + lax.broadcasted_iota(jnp.int32, (TOK, window), 1)
            keep = (pos_k >= start) & (pos_k <= base + row)
            bias = jnp.where(keep, 0.0, NEG)[None]
            spot = pl.ds(pl.multiple_of(begin - low, TOK), window)
            s = lax.dot_general(qa_buf[tb], kbuf[spot, :], NT, preferred_element_type=jnp.float32)
            staged.append((tb, spot, bias, s))
        for tb, spot, bias, s in staged:
            s = (s.reshape(heads, TOK, window) + bias).reshape(rows, window)
            m = jnp.max(s, axis=1, keepdims=True)
            p = jnp.exp2((s - m) * SCALE2)
            den = jnp.sum(p, axis=1, keepdims=True)
            o = jnp.dot(
                p.astype(jnp.bfloat16), kbuf[spot, :LAT], preferred_element_type=jnp.float32
            )
            o = (o * (1.0 / den)).astype(jnp.bfloat16)
            place = pl.ds(pl.multiple_of(tb * TOK, TOK), TOK)
            olat[:, place, :] = o.reshape(heads, TOK, LAT)

    def reaches(tb):
        begin = jnp.clip(base_of(tb) + TOK - fast, 0, length - fast)
        ahead_seg = segs_ref[span_idx, jnp.maximum(begin - 1, 0)]
        return (begin > 0) & (ahead_seg == segs_ref[span_idx, base_of(tb)])

    @pl.loop(0, blocks // GROUP)
    def _(step):
        tbs = [step * GROUP + k for k in range(GROUP)]
        for tb in tbs:
            qa_copy(tb).wait()

            @pl.when(tb + ahead < blocks)
            def _():
                qa_copy(tb + ahead).start()

        @pl.when(step == blocks // GROUP // 2)
        def _():
            av_copy.start()

        far = [reaches(tb) for tb in tbs]
        any_far = functools.reduce(jnp.logical_or, far)

        @pl.when(jnp.logical_not(any_far))
        def _():
            attend(fast, tbs)

        @pl.when(any_far)
        def _():
            @pl.loop(0, GROUP)
            def _(k):
                attend(slow, [step * GROUP + k])

    av_copy.wait()
    batch = heads // OUTS
    results = []
    for i in range(OUTS):
        for h in range(i * batch, (i + 1) * batch):
            r = jnp.dot(olat[h], av[h], preferred_element_type=jnp.float32)
            o_buf[:, h * VHEAD : (h + 1) * VHEAD] = r.astype(jnp.bfloat16)
        source = pl.ds(i * batch * VHEAD, batch * VHEAD)
        target = pl.ds((part * heads + i * batch) * VHEAD, batch * VHEAD)
        results.append(
            pltpu.make_async_copy(o_buf.at[:, source], o_hbm.at[:, target], osem.at[i])
        )
        results[-1].start()
    for result in results:
        result.wait()


def attend_prefill(segment_ids, qa, keys, absorb_value, part, parts, most, out=None):
    blocks, rows, _ = qa.shape
    tokens = blocks * TOK
    heads = rows // TOK // parts
    length = keys.shape[0]
    fast = min(most, length)
    slow = min(most + 128, length)
    aliased = out is not None
    args = [segment_ids, segment_ids, qa, keys, *([out] if aliased else []), absorb_value]
    return pl.pallas_call(
        functools.partial(
            prefill_kernel,
            part=part,
            fast=fast,
            slow=slow,
            heads=heads,
            aliased=aliased,
        ),
        grid_spec=pltpu.PrefetchScalarGridSpec(
            num_scalar_prefetch=1,
            grid=(1,),
            in_specs=[
                *([FAR] * (aliased + 4)),
            ],
            out_specs=FAR,
            scratch_shapes=[
                pltpu.VMEM((min(slow + tokens, length), WIDTH), jnp.bfloat16),
                pltpu.VMEM((heads, tokens, LAT), jnp.bfloat16),
                pltpu.VMEM((heads, LAT, VHEAD), jnp.bfloat16),
                pltpu.VMEM((blocks, heads * TOK, WIDTH), jnp.bfloat16),
                pltpu.VMEM(segment_ids.shape, jnp.int32),
                pltpu.VMEM((tokens, heads * VHEAD), jnp.bfloat16),
                pltpu.SemaphoreType.DMA,
                pltpu.SemaphoreType.DMA((blocks,)),
                pltpu.SemaphoreType.DMA,
                pltpu.SemaphoreType.DMA,
                pltpu.SemaphoreType.DMA((OUTS,)),
            ],
        ),
        out_shape=jax.ShapeDtypeStruct((tokens, parts * heads * VHEAD), jnp.bfloat16),
        input_output_aliases={4: 0} if aliased else {},
        cost_estimate=pl.CostEstimate(
            flops=2 * tokens * heads * (fast * (WIDTH + LAT) + LAT * VHEAD),
            bytes_accessed=2 * heads * (tokens * (WIDTH + VHEAD) + LAT * VHEAD),
            transcendentals=tokens * heads * fast,
        ),
        compiler_params=pltpu.CompilerParams(vmem_limit_bytes=61 * MIB),
    )(*args)


def decode_kernel(assign_ref, seg_hbm, *refs, count, spans, docs, steps, group):
    pieces = refs[:count]
    packs = refs[count : count + spans]
    ak_hbm, av_hbm, o_ref, keys_hbm, kbuf, qa, pack_ref, ak_ref, av_ref, seg_ref, ksem, sems = refs[
        count + spans :
    ]
    seq_idx = lax.axis_index("seq")
    span_idx = lax.axis_index("span")
    near = steps * docs
    rows = near * group
    copies = gather_copies(pieces, kbuf, ksem, seq_idx)
    own = pl.ds(seq_idx * group, group)
    early = [
        pltpu.make_async_copy(pack, pack_ref.at[pl.ds(i * near, near)], sems.at[i])
        for i, pack in enumerate(packs)
    ]
    middle = pltpu.make_async_copy(ak_hbm.at[own], ak_ref, sems.at[spans])
    early.append(pltpu.make_async_copy(seg_hbm, seg_ref, sems.at[spans + 3]))
    late = pltpu.make_async_copy(av_hbm.at[own], av_ref, sems.at[spans + 1])
    for copy in (*early, middle, *copies):
        copy.start()
    row = lax.broadcasted_iota(jnp.int32, (near, 1), 0)
    want = jnp.zeros((near, 1), jnp.int32)
    for d in range(docs):
        want = jnp.where(lax.rem(row, docs) == d, assign_ref[span_idx * docs + d], want)
    want = want * steps
    step = row // docs
    lane = lax.broadcasted_iota(jnp.int32, (1, spans * near), 1)
    place = lax.rem(lane, near)
    owner = lax.rem(span_idx - lane // near + spans, spans)
    number = (owner * docs + lax.rem(place, docs)) * steps + place // docs
    pick = jnp.where(number == want + step, 1.0, 0.0).astype(jnp.bfloat16)
    wide = group * NOPE
    for copy in early:
        copy.wait()
    late.start()
    pack = pack_ref[...]
    nope = jnp.dot(pick, pack[:, :wide], preferred_element_type=jnp.float32).astype(jnp.bfloat16)
    rope = jnp.dot(
        pick, pack[:, wide + LAT : wide + LAT + group * ROPE], preferred_element_type=jnp.float32
    ).astype(jnp.bfloat16)
    fresh = jnp.concatenate(
        [pack[:, wide : wide + LAT], pack[:, wide + LAT + group * ROPE :]], axis=1
    )
    middle.wait()
    for h in range(group):
        lat = jnp.dot(
            nope[:, h * NOPE : (h + 1) * NOPE], ak_ref[h], preferred_element_type=jnp.float32
        )
        qa[pl.ds(h * near, near), :LAT] = lat.astype(jnp.bfloat16)
        part = rope[:, h * ROPE : (h + 1) * ROPE]
        qa[pl.ds(h * near, near), LAT:] = jnp.concatenate([part, jnp.zeros_like(part)], axis=1)
    for copy in copies:
        copy.wait()
    handed = pltpu.make_async_copy(kbuf, keys_hbm, sems.at[spans + 2])
    handed.start()
    keys = kbuf[...]
    seg = seg_ref[pl.ds(span_idx, 1), :]
    old_bias = jnp.where(seg == lax.rem(row, docs), 0.0, NEG)[None]
    new_bias = jnp.where((number >= want) & (number <= want + step), 0.0, NEG)[None]
    query = qa[...]
    old = lax.dot_general(query, keys, NT, preferred_element_type=jnp.float32)
    old = (old.reshape(group, near, -1) + old_bias).reshape(rows, -1)
    new = lax.dot_general(query, fresh, NT, preferred_element_type=jnp.float32)
    new = (new.reshape(group, near, -1) + new_bias).reshape(rows, -1)
    m = jnp.maximum(jnp.max(old, axis=1, keepdims=True), jnp.max(new, axis=1, keepdims=True))
    old = jnp.exp2((old - m) * SCALE2)
    new = jnp.exp2((new - m) * SCALE2)
    den = jnp.sum(old, axis=1, keepdims=True) + jnp.sum(new, axis=1, keepdims=True)
    o = jnp.dot(old.astype(jnp.bfloat16), keys[:, :LAT], preferred_element_type=jnp.float32)
    o = o + jnp.dot(new.astype(jnp.bfloat16), fresh[:, :LAT], preferred_element_type=jnp.float32)
    o = o * (1.0 / den)
    high = o.astype(jnp.bfloat16)
    low = (o - high.astype(jnp.float32)).astype(jnp.bfloat16)
    late.wait()
    for h in range(group):
        both = jnp.concatenate(
            [high[h * near : (h + 1) * near], low[h * near : (h + 1) * near]], axis=0
        )
        r = jnp.dot(both, av_ref[h], preferred_element_type=jnp.float32)
        o_ref[:, h * VHEAD : (h + 1) * VHEAD] = (r[:near] + r[near:]).astype(jnp.bfloat16)
    handed.wait()


def attend_decode(assignment, segment_ids, pieces, packs, absorb_key, absorb_value, steps):
    near, size = packs[0].shape
    docs = near // steps
    count, spans = len(pieces), len(packs)
    tokens = pieces[0].shape[0]
    heads = absorb_key.shape[0]
    group = heads // count
    rows = near * group
    length = count * tokens
    return pl.pallas_call(
        functools.partial(
            decode_kernel, count=count, spans=spans, docs=docs, steps=steps, group=group
        ),
        grid_spec=pltpu.PrefetchScalarGridSpec(
            num_scalar_prefetch=1,
            grid=(1,),
            in_specs=[
                FAR,
                *([ANY] * (count + spans)),
                *([FAR] * 2),
            ],
            out_specs=(pl.BlockSpec((near, group * VHEAD), lambda i, *_: (0, 0)), FAR),
            scratch_shapes=[
                pltpu.VMEM((length, WIDTH), jnp.bfloat16),
                pltpu.VMEM((rows, WIDTH), jnp.bfloat16),
                pltpu.VMEM((spans * near, size), jnp.bfloat16),
                pltpu.VMEM((group, NOPE, LAT), jnp.bfloat16),
                pltpu.VMEM((group, LAT, VHEAD), jnp.bfloat16),
                pltpu.VMEM(segment_ids.shape, jnp.int32),
                pltpu.SemaphoreType.DMA((count,)),
                pltpu.SemaphoreType.DMA((spans + 4,)),
            ],
        ),
        out_shape=(
            jax.ShapeDtypeStruct((near, group * VHEAD), jnp.bfloat16),
            jax.ShapeDtypeStruct((length, WIDTH), jnp.bfloat16),
        ),
        cost_estimate=pl.CostEstimate(
            flops=2 * rows * length * (WIDTH + LAT),
            bytes_accessed=2 * (length * WIDTH + group * LAT * VHEAD * 2),
            transcendentals=rows * length,
        ),
        compiler_params=pltpu.CompilerParams(vmem_limit_bytes=52 * MIB),
        name="attend_decode",
    )(assignment, segment_ids, *pieces, *packs, absorb_key, absorb_value)


def select_kernel(assign_ref, *refs, spans, docs, steps):
    parts = refs[:spans]
    o_ref, value, sems = refs[spans:]
    span_idx = lax.axis_index("span")
    near = steps * docs
    copies = [
        pltpu.make_async_copy(part, value.at[pl.ds(i * near, near)], sems.at[i])
        for i, part in enumerate(parts)
    ]
    for copy in copies:
        copy.start()
    lane = lax.broadcasted_iota(jnp.int32, (1, spans * near), 1)
    number = jnp.zeros((1, spans * near), jnp.int32)
    for j in range(spans):
        source = lax.rem(span_idx - j + spans, spans)
        for d in range(docs):
            here = (lane // near == j) & (lax.rem(lane, docs) == d)
            number = jnp.where(here, assign_ref[source * docs + d], number)
    number = number * steps + lax.rem(lane, near) // docs
    row = lax.broadcasted_iota(jnp.int32, (near, 1), 0)
    want = (span_idx * docs + lax.rem(row, docs)) * steps + row // docs
    pick = jnp.where(number == want, 1.0, 0.0).astype(jnp.bfloat16)
    for copy in copies:
        copy.wait()
    o_ref[...] = jnp.dot(pick, value[...], preferred_element_type=jnp.float32).astype(jnp.bfloat16)


def select_rows(assignment, parts, steps):
    near, size = parts[0].shape
    spans = len(parts)
    return pl.pallas_call(
        functools.partial(select_kernel, spans=spans, docs=near // steps, steps=steps),
        grid_spec=pltpu.PrefetchScalarGridSpec(
            num_scalar_prefetch=1,
            grid=(1,),
            in_specs=[ANY] * spans,
            out_specs=pl.BlockSpec((near, size), lambda i, *_: (0, 0)),
            scratch_shapes=[
                pltpu.VMEM((spans * near, size), jnp.bfloat16),
                pltpu.SemaphoreType.DMA((spans,)),
            ],
        ),
        out_shape=jax.ShapeDtypeStruct((near, size), jnp.bfloat16),
        compiler_params=pltpu.CompilerParams(vmem_limit_bytes=8 * MIB),
        name="select_rows",
    )(assignment, *parts)


def assemble_kernel(*refs):
    parts, o_ref, sems = refs[:-2], refs[-2], refs[-1]
    near = parts[0].shape[0] // 2
    size = parts[0].shape[1]
    seq_idx = lax.axis_index("seq")
    core = lax.rem(seq_idx, 2)
    copies = []
    for i, part in enumerate(parts):
        source = lax.rem(seq_idx - 2 * i + 2 * len(parts), 2 * len(parts))
        for k in range(2):
            owner = source if k == 0 else source + 1 - 2 * core
            start = pl.multiple_of(owner * size, 128)
            copies.append(
                pltpu.make_async_copy(
                    part.at[pl.ds(k * near, near)],
                    o_ref.at[:, pl.ds(start, size)],
                    sems.at[2 * i + k],
                )
            )
    for copy in copies:
        copy.start()
    for copy in copies:
        copy.wait()


def assemble(parts):
    near, size = parts[0].shape
    number = 2 * len(parts)
    shape = (near // 2, number * size)
    return pl.pallas_call(
        assemble_kernel,
        grid_spec=pltpu.PrefetchScalarGridSpec(
            num_scalar_prefetch=0,
            grid=(1,),
            in_specs=[ANY] * len(parts),
            out_specs=pl.BlockSpec(shape, lambda i: (0, 0)),
            scratch_shapes=[pltpu.SemaphoreType.DMA((number,))],
        ),
        out_shape=jax.ShapeDtypeStruct(shape, jnp.bfloat16),
        compiler_params=pltpu.CompilerParams(vmem_limit_bytes=8 * MIB),
        name="assemble",
    )(*parts)


def spread_far(value, count):
    return [value] + [
        lax.ppermute(value, "seq", [(i, (i + 2 * k) % count) for i in range(count)])
        for k in range(1, count // 2)
    ]


def spread_near(pieces, count):
    swap = [(i, i ^ 1) for i in range(count)]
    return pieces + [lax.ppermute(p, "seq", swap) for p in pieces]


def spread(value, axis, count):
    return [value] + [
        lax.ppermute(value, axis, [(i, (i + k) % count) for i in range(count)])
        for k in range(1, count)
    ]


def body(
    q_prefill,
    kv_latent,
    key_rope,
    segment_ids,
    assignment,
    absorb_key,
    absorb_value,
    q_decode,
    new_latent,
    new_rope,
):
    steps, docs, heads, _ = q_decode.shape
    count = lax.axis_size("seq")
    spans = lax.axis_size("span")
    group = heads // count
    most = segment_ids.shape[1] // 2

    cache, pack = prepare(kv_latent[0], key_rope[0].T, q_decode, new_latent, new_rope, group)
    pieces = spread_far(cache, count)
    packs = spread(pack, "span", spans)
    qa = absorb_prefill(q_prefill[0].transpose(1, 2, 0), absorb_key)
    pieces = spread_near(pieces, count)
    decoded, keys = attend_decode(
        assignment, segment_ids, pieces, packs, absorb_key, absorb_value, steps
    )
    returned = spread(decoded, "span", spans)
    out = attend_prefill(segment_ids, qa, keys, absorb_value, 0, PARTS, most)
    chosen = select_rows(assignment, returned, steps)
    swapped = lax.ppermute(chosen, "seq", [(i, i ^ 1) for i in range(count)])
    both = jnp.concatenate([chosen, swapped], axis=0)
    finals = spread_far(both, count)
    for part in range(1, PARTS):
        out = attend_prefill(segment_ids, qa, keys, absorb_value, part, PARTS, most, out)
    decode_out = assemble(finals)
    return (out[None], decode_out.reshape(steps, docs, heads * VHEAD))


def solution(mesh):
    in_specs = (
        P("span", "seq", None, None),
        P("span", "seq", None),
        P("span", "seq", None),
        P(),
        P(),
        P(),
        P(),
        P(None, "span", None, None),
        P(None, "span", None),
        P(None, "span", None),
    )
    out_specs = (P("span", "seq", None), P(None, "span", None))
    return jax.shard_map(body, mesh=mesh, in_specs=in_specs, out_specs=out_specs, check_vma=False)
```
